256 devices in a mesh: space: 32 (over x, y, core), tm: 8 (over z).
Axes of the slice: x: 4, y: 4, z: 8, core: 2. Of those that a mesh axis runs over, the one named last changes fastest.
Arguments:
- velocity: bfloat16 [256, 2, 512, 1024], P('tm', None, 'space'), may hold values from -8.4 to 8.4
Outputs:
- vorticity: bfloat16 [256, 512, 1024], P('tm', 'space')
- modes: float32 [32, 512, 1024], P('tm', 'space')
The draws below stay inside these ranges and needn't reach their ends.
All inputs are finite; a program needn't handle non-finite values.
Results may differ from the reference program's by a relative error of at most 0.003.
Values may be sent and summed in bfloat16 or wider, within the bound.
A program may use at most 64 MiB of HBM per device.

```python
import jax
import jax.numpy as jnp
from jax import lax

NZ = 1024
RANK = 32
NX = 512
SNAPS = 256
LEVELS = 3
N_TM = 8


def draw_velocity(key, part):
    key_noise, key_spread = jax.random.split(key, 2)
    place = jnp.arange(NX, dtype=jnp.float32) / (NX - 1.0)
    noise = jnp.clip(jax.random.normal(key_noise, (SNAPS, 2, NX, NZ), jnp.float32), -2.0, 2.0)
    profile = 0.6 * jnp.exp(place * jnp.log(5.0))
    spread = jax.random.uniform(key_spread, (SNAPS, 1, 1, 1), jnp.float32, 0.8, 1.4)
    return (spread * profile[None, None, :, None] * noise).astype(jnp.bfloat16)


def setup_inputs(seed: int = 0) -> dict:
    key_list = jax.random.split(jax.random.key(seed), 2)
    velocity = draw_velocity(jax.random.fold_in(key_list[1], 71), 0)
    return dict(velocity=velocity)


def central(field, axis):
    ahead = jnp.roll(field, -1, axis)
    behind = jnp.roll(field, 1, axis)
    ahead_two = jnp.roll(field, -2, axis)
    behind_two = jnp.roll(field, 2, axis)
    return (8.0 * (ahead - behind) - (ahead_two - behind_two)) / 12.0

def merge_pair(first, second):
    high = lax.Precision.HIGHEST
    stacked = jnp.concatenate([first, second], axis=0)
    gram = jnp.einsum('axz,bxz->ab', stacked, stacked, precision=high)
    coeffs = gram[:, :RANK] + gram[:, RANK:]
    diagonal = jnp.diagonal(gram)
    scales = jnp.sqrt(diagonal[:RANK] + diagonal[RANK:])
    mixed = jnp.einsum('ab,axz->bxz', coeffs, stacked, precision=high)
    inner = jnp.einsum('axz,bxz->ab', mixed, mixed, precision=high)
    lower = jnp.linalg.cholesky(inner)
    eye = jnp.eye(RANK, dtype=jnp.float32)
    lower_inv = lax.linalg.triangular_solve(lower, eye, left_side=True, lower=True)
    factor = jnp.transpose(lower_inv) * scales[None, :]
    return jnp.einsum('ab,axz->bxz', factor, mixed, precision=high)

def reference(velocity):
    blocks = []
    outs = []
    for block in range(N_TM):
        piece = velocity[block * RANK:(block + 1) * RANK].astype(jnp.float32)
        vort = (central(piece[:, 1], 1) - central(piece[:, 0], 2)).astype(jnp.bfloat16)
        outs.append(vort)
        blocks.append(vort.astype(jnp.float32))
    for level in range(LEVELS):
        blocks = [merge_pair(blocks[2 * j], blocks[2 * j + 1]) for j in range(len(blocks) // 2)]
    return (jnp.concatenate(outs, axis=0), blocks[0])
```

```python
import jax
import jax.numpy as jnp
from jax import lax
from jax.sharding import PartitionSpec as P

RANK = 32
HIGH = lax.Precision.HIGHEST


def halo_rows(block, width):
    count = lax.axis_size("space")
    forward = [(i, (i + 1) % count) for i in range(count)]
    backward = [(target, source) for source, target in forward]
    rows = block.shape[1]
    low = lax.ppermute(block[:, rows - width :], "space", forward)
    high = lax.ppermute(block[:, :width], "space", backward)
    return jnp.concatenate([low, block, high], axis=1)


def spanwise(field):
    ahead = jnp.roll(field, -1, 2)
    behind = jnp.roll(field, 1, 2)
    ahead_two = jnp.roll(field, -2, 2)
    behind_two = jnp.roll(field, 2, 2)
    return (8.0 * (ahead - behind) - (ahead_two - behind_two)) / 12.0


def merge_small(gram):
    coeffs = gram[:, :, :RANK] + gram[:, :, RANK:]
    diagonal = jnp.diagonal(gram, axis1=1, axis2=2)
    scales = jnp.sqrt(diagonal[:, :RANK] + diagonal[:, RANK:])
    half = jnp.einsum("nab,nbc->nac", gram, coeffs, precision=HIGH)
    inner = jnp.einsum("nab,nac->nbc", coeffs, half, precision=HIGH)
    lower = jnp.linalg.cholesky(inner)
    eye = jnp.broadcast_to(jnp.eye(RANK, dtype=jnp.float32), inner.shape)
    lower_inv = lax.linalg.triangular_solve(lower, eye, left_side=True, lower=True)
    factor = jnp.swapaxes(lower_inv, 1, 2) * scales[:, None, :]
    return jnp.einsum("nab,nbc->nac", coeffs, factor, precision=HIGH)


def tree_basis(gram, leaves):
    width = leaves * RANK
    basis = None
    span = 1
    while span < leaves:
        nodes = leaves // (2 * span)
        size = 2 * span * RANK
        sub = jnp.stack(
            [gram[k * size : (k + 1) * size, k * size : (k + 1) * size] for k in range(nodes)]
        )
        if basis is None:
            h = sub
        else:
            b = basis.reshape(nodes, 2, span * RANK, RANK)
            zero = jnp.zeros_like(b[:, 0])
            bd = jnp.concatenate(
                [
                    jnp.concatenate([b[:, 0], zero], axis=2),
                    jnp.concatenate([zero, b[:, 1]], axis=2),
                ],
                axis=1,
            )
            gb = jnp.einsum("nab,nbc->nac", sub, bd, precision=HIGH)
            h = jnp.einsum("nab,nac->nbc", bd, gb, precision=HIGH)
        c = merge_small(h)
        if basis is None:
            basis = c
        else:
            basis = jnp.einsum("nab,nbc->nac", bd, c, precision=HIGH)
        span *= 2
    return basis.reshape(width, RANK)


def local(velocity):
    rows = velocity.shape[2]
    span_v = halo_rows(velocity[:, 1], 2).astype(jnp.float32)
    stream_u = velocity[:, 0].astype(jnp.float32)
    dv_dx = (
        8.0 * (span_v[:, 3 : rows + 3] - span_v[:, 1 : rows + 1])
        - (span_v[:, 4:] - span_v[:, :rows])
    ) / 12.0
    vorticity = (dv_dx - spanwise(stream_u)).astype(jnp.bfloat16)
    blocks = lax.axis_size("tm")
    cells = lax.all_to_all(vorticity, "tm", 2, 0, tiled=True)
    flat = cells.reshape(cells.shape[0], -1)
    gram = jnp.einsum("ax,bx->ab", flat, flat, preferred_element_type=jnp.float32)
    gram = lax.psum(gram, ("space", "tm"))
    basis = tree_basis(gram, blocks)
    part = jnp.einsum(
        "ab,ax->bx", basis, flat.astype(jnp.float32), precision=HIGH
    ).reshape(RANK, rows, -1)
    modes = lax.all_to_all(part, "tm", 0, 2, tiled=True)
    return (vorticity, modes)


def solution(mesh):
    in_specs = (P("tm", None, "space", None),)
    out_specs = (P("tm", "space", None), P("tm", "space", None))
    return jax.shard_map(local, mesh=mesh, in_specs=in_specs, out_specs=out_specs, check_vma=False)
```

```python
import functools

import jax
import jax.numpy as jnp
from jax import lax
from jax.experimental import pallas as pl
from jax.experimental.pallas import tpu as pltpu
from jax.sharding import PartitionSpec as P

RANK = 32
HIGH = lax.Precision.HIGHEST


def halo_rows(block, width):
    count = lax.axis_size("space")
    forward = [(i, (i + 1) % count) for i in range(count)]
    backward = [(target, source) for source, target in forward]
    rows = block.shape[1]
    low = lax.ppermute(block[:, rows - width :], "space", forward)
    high = lax.ppermute(block[:, :width], "space", backward)
    return jnp.concatenate([low, block, high], axis=1)


def spanwise(field):
    ahead = jnp.roll(field, -1, 2)
    behind = jnp.roll(field, 1, 2)
    ahead_two = jnp.roll(field, -2, 2)
    behind_two = jnp.roll(field, 2, 2)
    return (8.0 * (ahead - behind) - (ahead_two - behind_two)) / 12.0


def merge_small(gram):
    coeffs = gram[:, :, :RANK] + gram[:, :, RANK:]
    diagonal = jnp.diagonal(gram, axis1=1, axis2=2)
    scales = jnp.sqrt(diagonal[:, :RANK] + diagonal[:, RANK:])
    half = jnp.einsum("nab,nbc->nac", gram, coeffs, precision=HIGH)
    inner = jnp.einsum("nab,nac->nbc", coeffs, half, precision=HIGH)
    lower = jnp.linalg.cholesky(inner)
    eye = jnp.broadcast_to(jnp.eye(RANK, dtype=jnp.float32), inner.shape)
    lower_inv = lax.linalg.triangular_solve(lower, eye, left_side=True, lower=True)
    factor = jnp.swapaxes(lower_inv, 1, 2) * scales[:, None, :]
    return jnp.einsum("nab,nbc->nac", coeffs, factor, precision=HIGH)


def tree_basis(gram, leaves):
    width = leaves * RANK
    basis = None
    span = 1
    while span < leaves:
        nodes = leaves // (2 * span)
        size = 2 * span * RANK
        sub = jnp.stack(
            [gram[k * size : (k + 1) * size, k * size : (k + 1) * size] for k in range(nodes)]
        )
        if basis is None:
            h = sub
        else:
            b = basis.reshape(nodes, 2, span * RANK, RANK)
            zero = jnp.zeros_like(b[:, 0])
            bd = jnp.concatenate(
                [
                    jnp.concatenate([b[:, 0], zero], axis=2),
                    jnp.concatenate([zero, b[:, 1]], axis=2),
                ],
                axis=1,
            )
            gb = jnp.einsum("nab,nbc->nac", sub, bd, precision=HIGH)
            h = jnp.einsum("nab,nac->nbc", bd, gb, precision=HIGH)
        c = merge_small(h)
        if basis is None:
            basis = c
        else:
            basis = jnp.einsum("nab,nbc->nac", bd, c, precision=HIGH)
        span *= 2
    return basis.reshape(width, RANK)


MESH = pl.DeviceIdType.MESH


def allreduce_kernel(n_space, n_tm, g_ref, out_ref, buf1, buf2, buf3, send1, recv1, send2, recv2, send3, recv3):
    s = lax.axis_index("space")
    t = lax.axis_index("tm")

    barrier = pltpu.get_barrier_semaphore()

    def greet_space(k, carry):
        b = lax.rem(s + k, n_space)
        pl.semaphore_signal(barrier, inc=1, device_id=(b, t), device_id_type=MESH)
        return carry

    def greet_tm(k, carry):
        a = lax.rem(t + k, n_tm)
        pl.semaphore_signal(barrier, inc=1, device_id=(s, a), device_id_type=MESH)
        return carry

    lax.fori_loop(1, n_space, greet_space, 0)
    lax.fori_loop(1, n_tm, greet_tm, 0)
    pl.semaphore_wait(barrier, (n_space - 1) + (n_tm - 1))

    def space_copy(src, dst_buf, send, recv, k):
        b = lax.rem(s + k, n_space)
        return pltpu.make_async_remote_copy(
            src_ref=src(b), dst_ref=dst_buf.at[s], send_sem=send.at[k], recv_sem=recv.at[s],
            device_id=(b, t), device_id_type=MESH,
        )

    def space_wait(dst_buf, send, recv, k):
        j = lax.rem(s + k, n_space)
        pltpu.make_async_remote_copy(
            src_ref=dst_buf.at[j], dst_ref=dst_buf.at[j], send_sem=send.at[k], recv_sem=recv.at[j],
            device_id=(j, t), device_id_type=MESH,
        ).wait_recv()

    def send_p1(k, carry):
        space_copy(lambda b: g_ref.at[b], buf1, send1, recv1, k).start()
        return carry

    lax.fori_loop(1, n_space, send_p1, 0)
    buf1[s] = g_ref[s]

    def wait_p1(k, carry):
        space_wait(buf1, send1, recv1, k)
        return carry

    lax.fori_loop(1, n_space, wait_p1, 0)
    acc = buf1[0]
    for j in range(1, n_space):
        acc = acc + buf1[j]
    buf2[t] = acc

    copies = []
    for k in range(1, n_tm):
        a = lax.rem(t + k, n_tm)
        c = pltpu.make_async_remote_copy(
            src_ref=buf2.at[t], dst_ref=buf2.at[t], send_sem=send2.at[k], recv_sem=recv2.at[t],
            device_id=(s, a), device_id_type=MESH,
        )
        c.start()
        copies.append(c)
    for k in range(1, n_tm):
        j = lax.rem(t + k, n_tm)
        pltpu.make_async_remote_copy(
            src_ref=buf2.at[j], dst_ref=buf2.at[j], send_sem=send2.at[k], recv_sem=recv2.at[j],
            device_id=(s, j), device_id_type=MESH,
        ).wait_recv()
    for c in copies:
        c.wait_send()
    acc = buf2[0]
    for j in range(1, n_tm):
        acc = acc + buf2[j]
    buf3[s] = acc

    def send_p3(k, carry):
        space_copy(lambda b: buf3.at[s], buf3, send3, recv3, k).start()
        return carry

    lax.fori_loop(1, n_space, send_p3, 0)

    def wait_p3(k, carry):
        space_wait(buf3, send3, recv3, k)
        return carry

    lax.fori_loop(1, n_space, wait_p3, 0)

    def drain(k, carry):
        space_copy(lambda b: g_ref.at[b], buf1, send1, recv1, k).wait_send()
        space_copy(lambda b: buf3.at[s], buf3, send3, recv3, k).wait_send()
        return carry

    lax.fori_loop(1, n_space, drain, 0)
    out_ref[...] = buf3[...]


def allreduce(gram):
    n_space = lax.axis_size("space")
    n_tm = lax.axis_size("tm")
    size = gram.shape[0]
    chunks = gram.reshape(n_space, size // n_space, size)
    shape = chunks.shape
    out = pl.pallas_call(
        functools.partial(allreduce_kernel, n_space, n_tm),
        out_shape=jax.ShapeDtypeStruct(shape, jnp.float32),
        in_specs=[pl.BlockSpec(memory_space=pltpu.VMEM)],
        out_specs=pl.BlockSpec(memory_space=pltpu.VMEM),
        scratch_shapes=[
            pltpu.VMEM(shape, jnp.float32),
            pltpu.VMEM((n_tm,) + shape[1:], jnp.float32),
            pltpu.VMEM(shape, jnp.float32),
            pltpu.SemaphoreType.DMA((n_space,)),
            pltpu.SemaphoreType.DMA((n_space,)),
            pltpu.SemaphoreType.DMA((n_tm,)),
            pltpu.SemaphoreType.DMA((n_tm,)),
            pltpu.SemaphoreType.DMA((n_space,)),
            pltpu.SemaphoreType.DMA((n_space,)),
        ],
        compiler_params=pltpu.CompilerParams(collective_id=0, has_side_effects=True),
    )(chunks)
    return out.reshape(size, size)


def local(velocity):
    rows = velocity.shape[2]
    span_v = halo_rows(velocity[:, 1], 2).astype(jnp.float32)
    stream_u = velocity[:, 0].astype(jnp.float32)
    dv_dx = (
        8.0 * (span_v[:, 3 : rows + 3] - span_v[:, 1 : rows + 1])
        - (span_v[:, 4:] - span_v[:, :rows])
    ) / 12.0
    vorticity = (dv_dx - spanwise(stream_u)).astype(jnp.bfloat16)
    blocks = lax.axis_size("tm")
    cells = lax.all_to_all(vorticity, "tm", 2, 0, tiled=True)
    flat = cells.reshape(cells.shape[0], -1)
    gram = jnp.einsum("ax,bx->ab", flat, flat, preferred_element_type=jnp.float32)
    gram = allreduce(gram)
    basis = tree_basis(gram, blocks)
    part = jnp.einsum(
        "ab,ax->bx", basis, flat.astype(jnp.float32), precision=HIGH
    ).reshape(RANK, rows, -1)
    modes = lax.all_to_all(part, "tm", 0, 2, tiled=True)
    return (vorticity, modes)


def solution(mesh):
    in_specs = (P("tm", None, "space", None),)
    out_specs = (P("tm", "space", None), P("tm", "space", None))
    return jax.shard_map(local, mesh=mesh, in_specs=in_specs, out_specs=out_specs, check_vma=False)
```

```python
import functools

import jax
import jax.numpy as jnp
from jax import lax
from jax.experimental import pallas as pl
from jax.experimental.pallas import tpu as pltpu
from jax.sharding import PartitionSpec as P

RANK = 32
HIGH = lax.Precision.HIGHEST


def halo_rows(block, width):
    count = lax.axis_size("space")
    forward = [(i, (i + 1) % count) for i in range(count)]
    backward = [(target, source) for source, target in forward]
    rows = block.shape[1]
    low = lax.ppermute(block[:, rows - width :], "space", forward)
    high = lax.ppermute(block[:, :width], "space", backward)
    return jnp.concatenate([low, block, high], axis=1)


def spanwise(field):
    ahead = jnp.roll(field, -1, 2)
    behind = jnp.roll(field, 1, 2)
    ahead_two = jnp.roll(field, -2, 2)
    behind_two = jnp.roll(field, 2, 2)
    return (8.0 * (ahead - behind) - (ahead_two - behind_two)) / 12.0


def merge_small(gram):
    coeffs = gram[:, :, :RANK] + gram[:, :, RANK:]
    diagonal = jnp.diagonal(gram, axis1=1, axis2=2)
    scales = jnp.sqrt(diagonal[:, :RANK] + diagonal[:, RANK:])
    half = jnp.einsum("nab,nbc->nac", gram, coeffs, precision=HIGH)
    inner = jnp.einsum("nab,nac->nbc", coeffs, half, precision=HIGH)
    lower = jnp.linalg.cholesky(inner)
    eye = jnp.broadcast_to(jnp.eye(RANK, dtype=jnp.float32), inner.shape)
    lower_inv = lax.linalg.triangular_solve(lower, eye, left_side=True, lower=True)
    factor = jnp.swapaxes(lower_inv, 1, 2) * scales[:, None, :]
    return jnp.einsum("nab,nbc->nac", coeffs, factor, precision=HIGH)


def tree_basis(gram, leaves):
    width = leaves * RANK
    basis = None
    span = 1
    while span < leaves:
        nodes = leaves // (2 * span)
        size = 2 * span * RANK
        sub = jnp.stack(
            [gram[k * size : (k + 1) * size, k * size : (k + 1) * size] for k in range(nodes)]
        )
        if basis is None:
            h = sub
        else:
            b = basis.reshape(nodes, 2, span * RANK, RANK)
            zero = jnp.zeros_like(b[:, 0])
            bd = jnp.concatenate(
                [
                    jnp.concatenate([b[:, 0], zero], axis=2),
                    jnp.concatenate([zero, b[:, 1]], axis=2),
                ],
                axis=1,
            )
            gb = jnp.einsum("nab,nbc->nac", sub, bd, precision=HIGH)
            h = jnp.einsum("nab,nac->nbc", bd, gb, precision=HIGH)
        c = merge_small(h)
        if basis is None:
            basis = c
        else:
            basis = jnp.einsum("nab,nbc->nac", bd, c, precision=HIGH)
        span *= 2
    return basis.reshape(width, RANK)


MESH = pl.DeviceIdType.MESH


def allreduce_kernel(n_space, n_tm, g_ref, out_ref, buf1, buf2, buf3, send1, recv1, send2, recv2, send3, recv3):
    s = lax.axis_index("space")
    t = lax.axis_index("tm")

    barrier = pltpu.get_barrier_semaphore()

    def greet_space(k, carry):
        b = lax.rem(s + k, n_space)
        pl.semaphore_signal(barrier, inc=1, device_id=(b, t), device_id_type=MESH)
        return carry

    def greet_tm(k, carry):
        a = lax.rem(t + k, n_tm)
        pl.semaphore_signal(barrier, inc=1, device_id=(s, a), device_id_type=MESH)
        return carry

    lax.fori_loop(1, n_space, greet_space, 0)
    lax.fori_loop(1, n_tm, greet_tm, 0)
    pl.semaphore_wait(barrier, (n_space - 1) + (n_tm - 1))

    def space_copy(src, dst_buf, send, recv, k):
        b = lax.rem(s + k, n_space)
        return pltpu.make_async_remote_copy(
            src_ref=src(b), dst_ref=dst_buf.at[s], send_sem=send.at[k], recv_sem=recv.at[s],
            device_id=(b, t), device_id_type=MESH,
        )

    def space_wait(dst_buf, send, recv, k):
        j = lax.rem(s + k, n_space)
        pltpu.make_async_remote_copy(
            src_ref=dst_buf.at[j], dst_ref=dst_buf.at[j], send_sem=send.at[k], recv_sem=recv.at[j],
            device_id=(j, t), device_id_type=MESH,
        ).wait_recv()

    def send_p1(k, carry):
        space_copy(lambda b: g_ref.at[b], buf1, send1, recv1, k).start()
        return carry

    lax.fori_loop(1, n_space, send_p1, 0)
    buf1[s] = g_ref[s]

    def wait_p1(k, carry):
        space_wait(buf1, send1, recv1, k)
        return carry

    lax.fori_loop(1, n_space, wait_p1, 0)
    acc = buf1[0]
    for j in range(1, n_space):
        acc = acc + buf1[j]
    buf2[t] = acc

    copies = []
    for k in range(1, n_tm):
        a = lax.rem(t + k, n_tm)
        c = pltpu.make_async_remote_copy(
            src_ref=buf2.at[t], dst_ref=buf2.at[t], send_sem=send2.at[k], recv_sem=recv2.at[t],
            device_id=(s, a), device_id_type=MESH,
        )
        c.start()
        copies.append(c)
    for k in range(1, n_tm):
        j = lax.rem(t + k, n_tm)
        pltpu.make_async_remote_copy(
            src_ref=buf2.at[j], dst_ref=buf2.at[j], send_sem=send2.at[k], recv_sem=recv2.at[j],
            device_id=(s, j), device_id_type=MESH,
        ).wait_recv()
    for c in copies:
        c.wait_send()
    acc = buf2[0]
    for j in range(1, n_tm):
        acc = acc + buf2[j]
    buf3[s] = acc

    def send_p3(k, carry):
        space_copy(lambda b: buf3.at[s], buf3, send3, recv3, k).start()
        return carry

    lax.fori_loop(1, n_space, send_p3, 0)

    def wait_p3(k, carry):
        space_wait(buf3, send3, recv3, k)
        return carry

    lax.fori_loop(1, n_space, wait_p3, 0)

    def drain(k, carry):
        space_copy(lambda b: g_ref.at[b], buf1, send1, recv1, k).wait_send()
        space_copy(lambda b: buf3.at[s], buf3, send3, recv3, k).wait_send()
        return carry

    lax.fori_loop(1, n_space, drain, 0)
    out_ref[...] = buf3[...]


def allreduce(gram):
    n_space = lax.axis_size("space")
    n_tm = lax.axis_size("tm")
    size = gram.shape[0]
    chunks = gram.reshape(n_space, size // n_space, size)
    shape = chunks.shape
    out = pl.pallas_call(
        functools.partial(allreduce_kernel, n_space, n_tm),
        out_shape=jax.ShapeDtypeStruct(shape, jnp.float32),
        in_specs=[pl.BlockSpec(memory_space=pltpu.VMEM)],
        out_specs=pl.BlockSpec(memory_space=pltpu.VMEM),
        scratch_shapes=[
            pltpu.VMEM(shape, jnp.float32),
            pltpu.VMEM((n_tm,) + shape[1:], jnp.float32),
            pltpu.VMEM(shape, jnp.float32),
            pltpu.SemaphoreType.DMA((n_space,)),
            pltpu.SemaphoreType.DMA((n_space,)),
            pltpu.SemaphoreType.DMA((n_tm,)),
            pltpu.SemaphoreType.DMA((n_tm,)),
            pltpu.SemaphoreType.DMA((n_space,)),
            pltpu.SemaphoreType.DMA((n_space,)),
        ],
        compiler_params=pltpu.CompilerParams(collective_id=0, has_side_effects=True),
    )(chunks)
    return out.reshape(size, size)


def a2a_kernel(n_tm, src_at, dst_at, x_ref, out_ref, buf, send, recv, own):
    s = lax.axis_index("space")
    t = lax.axis_index("tm")
    barrier = pltpu.get_barrier_semaphore()
    for k in range(1, n_tm):
        a = lax.rem(t + k, n_tm)
        pl.semaphore_signal(barrier, inc=1, device_id=(s, a), device_id_type=MESH)
    pl.semaphore_wait(barrier, n_tm - 1)
    copies = []
    for k in range(1, n_tm):
        a = lax.rem(t + k, n_tm)
        c = pltpu.make_async_remote_copy(
            src_ref=src_at(x_ref, a), dst_ref=dst_at(buf, t), send_sem=send.at[k], recv_sem=recv.at[t],
            device_id=(s, a), device_id_type=MESH,
        )
        c.start()
        copies.append(c)
    mine = pltpu.make_async_copy(src_at(x_ref, t), dst_at(buf, t), own.at[0])
    mine.start()
    mine.wait()
    for k in range(1, n_tm):
        j = lax.rem(t + k, n_tm)
        pltpu.make_async_remote_copy(
            src_ref=src_at(x_ref, j), dst_ref=dst_at(buf, j), send_sem=send.at[k], recv_sem=recv.at[j],
            device_id=(s, j), device_id_type=MESH,
        ).wait_recv()
    for c in copies:
        c.wait_send()
    out_ref[...] = buf[...]


def all_to_all(x, out_shape, src_at, dst_at, cid):
    n_tm = lax.axis_size("tm")
    return pl.pallas_call(
        functools.partial(a2a_kernel, n_tm, src_at, dst_at),
        out_shape=jax.ShapeDtypeStruct(out_shape, x.dtype),
        in_specs=[pl.BlockSpec(memory_space=pltpu.VMEM)],
        out_specs=pl.BlockSpec(memory_space=pltpu.VMEM),
        scratch_shapes=[
            pltpu.VMEM(out_shape, x.dtype),
            pltpu.SemaphoreType.DMA((n_tm,)),
            pltpu.SemaphoreType.DMA((n_tm,)),
            pltpu.SemaphoreType.DMA((1,)),
        ],
        compiler_params=pltpu.CompilerParams(collective_id=cid, has_side_effects=True),
    )(x)


def lanes(a, width):
    return pl.ds(pl.multiple_of(a * width, width), width)


def local(velocity):
    rows = velocity.shape[2]
    span_v = halo_rows(velocity[:, 1], 2).astype(jnp.float32)
    stream_u = velocity[:, 0].astype(jnp.float32)
    dv_dx = (
        8.0 * (span_v[:, 3 : rows + 3] - span_v[:, 1 : rows + 1])
        - (span_v[:, 4:] - span_v[:, :rows])
    ) / 12.0
    vorticity = (dv_dx - spanwise(stream_u)).astype(jnp.bfloat16)
    blocks = lax.axis_size("tm")
    cols = vorticity.shape[2]
    width = cols // blocks
    cells = all_to_all(
        vorticity,
        (blocks,) + vorticity.shape[:2] + (width,),
        lambda ref, a: ref.at[:, :, lanes(a, width)],
        lambda ref, j: ref.at[j],
        1,
    ).reshape(blocks * RANK, rows, width)
    gram = jnp.einsum("axz,bxz->ab", cells, cells, preferred_element_type=jnp.float32)
    gram = allreduce(gram)
    basis = tree_basis(gram, blocks)
    part = jnp.einsum("ab,axz->bxz", basis, cells.astype(jnp.float32), precision=HIGH)
    share = RANK // blocks
    modes = all_to_all(
        part,
        (share, rows, cols),
        lambda ref, a: ref.at[pl.ds(a * share, share)],
        lambda ref, j: ref.at[:, :, lanes(j, width)],
        2,
    )
    return (vorticity, modes)


def solution(mesh):
    in_specs = (P("tm", None, "space", None),)
    out_specs = (P("tm", "space", None), P("tm", "space", None))
    return jax.shard_map(local, mesh=mesh, in_specs=in_specs, out_specs=out_specs, check_vma=False)
```

```python
import functools

import jax
import jax.numpy as jnp
from jax import lax
from jax.experimental import pallas as pl
from jax.experimental.pallas import tpu as pltpu
from jax.sharding import PartitionSpec as P

RANK = 32
HIGH = lax.Precision.HIGHEST


def halo_rows(block, width):
    count = lax.axis_size("space")
    forward = [(i, (i + 1) % count) for i in range(count)]
    backward = [(target, source) for source, target in forward]
    rows = block.shape[1]
    low = lax.ppermute(block[:, rows - width :], "space", forward)
    high = lax.ppermute(block[:, :width], "space", backward)
    return jnp.concatenate([low, block, high], axis=1)


def spanwise(field):
    ahead = jnp.roll(field, -1, 2)
    behind = jnp.roll(field, 1, 2)
    ahead_two = jnp.roll(field, -2, 2)
    behind_two = jnp.roll(field, 2, 2)
    return (8.0 * (ahead - behind) - (ahead_two - behind_two)) / 12.0


def merge_small(gram):
    coeffs = gram[:, :, :RANK] + gram[:, :, RANK:]
    diagonal = jnp.diagonal(gram, axis1=1, axis2=2)
    scales = jnp.sqrt(diagonal[:, :RANK] + diagonal[:, RANK:])
    half = jnp.einsum("nab,nbc->nac", gram, coeffs, precision=HIGH)
    inner = jnp.einsum("nab,nac->nbc", coeffs, half, precision=HIGH)
    lower = jnp.linalg.cholesky(inner)
    eye = jnp.broadcast_to(jnp.eye(RANK, dtype=jnp.float32), inner.shape)
    lower_inv = lax.linalg.triangular_solve(lower, eye, left_side=True, lower=True)
    factor = jnp.swapaxes(lower_inv, 1, 2) * scales[:, None, :]
    return jnp.einsum("nab,nbc->nac", coeffs, factor, precision=HIGH)


def tree_basis(gram, leaves):
    width = leaves * RANK
    basis = None
    span = 1
    while span < leaves:
        nodes = leaves // (2 * span)
        size = 2 * span * RANK
        sub = jnp.stack(
            [gram[k * size : (k + 1) * size, k * size : (k + 1) * size] for k in range(nodes)]
        )
        if basis is None:
            h = sub
        else:
            b = basis.reshape(nodes, 2, span * RANK, RANK)
            zero = jnp.zeros_like(b[:, 0])
            bd = jnp.concatenate(
                [
                    jnp.concatenate([b[:, 0], zero], axis=2),
                    jnp.concatenate([zero, b[:, 1]], axis=2),
                ],
                axis=1,
            )
            gb = jnp.einsum("nab,nbc->nac", sub, bd, precision=HIGH)
            h = jnp.einsum("nab,nac->nbc", bd, gb, precision=HIGH)
        c = merge_small(h)
        if basis is None:
            basis = c
        else:
            basis = jnp.einsum("nab,nbc->nac", bd, c, precision=HIGH)
        span *= 2
    return basis.reshape(width, RANK)


MESH = pl.DeviceIdType.MESH


def allreduce_kernel(n_space, n_tm, g_ref, out_ref, buf1, buf2, buf3, send1, recv1, send2, recv2, send3, recv3):
    s = lax.axis_index("space")
    t = lax.axis_index("tm")

    barrier = pltpu.get_barrier_semaphore()

    def greet_space(k, carry):
        b = lax.rem(s + k, n_space)
        pl.semaphore_signal(barrier, inc=1, device_id=(b, t), device_id_type=MESH)
        return carry

    def greet_tm(k, carry):
        a = lax.rem(t + k, n_tm)
        pl.semaphore_signal(barrier, inc=1, device_id=(s, a), device_id_type=MESH)
        return carry

    lax.fori_loop(1, n_space, greet_space, 0)
    lax.fori_loop(1, n_tm, greet_tm, 0)
    pl.semaphore_wait(barrier, (n_space - 1) + (n_tm - 1))

    def space_copy(src, dst_buf, send, recv, k):
        b = lax.rem(s + k, n_space)
        return pltpu.make_async_remote_copy(
            src_ref=src(b), dst_ref=dst_buf.at[s], send_sem=send.at[k], recv_sem=recv.at[s],
            device_id=(b, t), device_id_type=MESH,
        )

    def space_wait(dst_buf, send, recv, k):
        j = lax.rem(s + k, n_space)
        pltpu.make_async_remote_copy(
            src_ref=dst_buf.at[j], dst_ref=dst_buf.at[j], send_sem=send.at[k], recv_sem=recv.at[j],
            device_id=(j, t), device_id_type=MESH,
        ).wait_recv()

    def send_p1(k, carry):
        space_copy(lambda b: g_ref.at[b], buf1, send1, recv1, k).start()
        return carry

    lax.fori_loop(1, n_space, send_p1, 0)
    buf1[s] = g_ref[s]

    def wait_p1(k, carry):
        space_wait(buf1, send1, recv1, k)
        return carry

    lax.fori_loop(1, n_space, wait_p1, 0)
    acc = buf1[0]
    for j in range(1, n_space):
        acc = acc + buf1[j]
    buf2[t] = acc

    copies = []
    for k in range(1, n_tm):
        a = lax.rem(t + k, n_tm)
        c = pltpu.make_async_remote_copy(
            src_ref=buf2.at[t], dst_ref=buf2.at[t], send_sem=send2.at[k], recv_sem=recv2.at[t],
            device_id=(s, a), device_id_type=MESH,
        )
        c.start()
        copies.append(c)
    for k in range(1, n_tm):
        j = lax.rem(t + k, n_tm)
        pltpu.make_async_remote_copy(
            src_ref=buf2.at[j], dst_ref=buf2.at[j], send_sem=send2.at[k], recv_sem=recv2.at[j],
            device_id=(s, j), device_id_type=MESH,
        ).wait_recv()
    for c in copies:
        c.wait_send()
    acc = buf2[0]
    for j in range(1, n_tm):
        acc = acc + buf2[j]
    buf3[s] = acc

    def send_p3(k, carry):
        space_copy(lambda b: buf3.at[s], buf3, send3, recv3, k).start()
        return carry

    lax.fori_loop(1, n_space, send_p3, 0)

    def wait_p3(k, carry):
        space_wait(buf3, send3, recv3, k)
        return carry

    lax.fori_loop(1, n_space, wait_p3, 0)

    def drain(k, carry):
        space_copy(lambda b: g_ref.at[b], buf1, send1, recv1, k).wait_send()
        space_copy(lambda b: buf3.at[s], buf3, send3, recv3, k).wait_send()
        return carry

    lax.fori_loop(1, n_space, drain, 0)
    out_ref[...] = buf3[...]


def allreduce(gram):
    n_space = lax.axis_size("space")
    n_tm = lax.axis_size("tm")
    size = gram.shape[0]
    chunks = gram.reshape(n_space, size // n_space, size)
    shape = chunks.shape
    out = pl.pallas_call(
        functools.partial(allreduce_kernel, n_space, n_tm),
        out_shape=jax.ShapeDtypeStruct(shape, jnp.float32),
        in_specs=[pl.BlockSpec(memory_space=pltpu.VMEM)],
        out_specs=pl.BlockSpec(memory_space=pltpu.VMEM),
        scratch_shapes=[
            pltpu.VMEM(shape, jnp.float32),
            pltpu.VMEM((n_tm,) + shape[1:], jnp.float32),
            pltpu.VMEM(shape, jnp.float32),
            pltpu.SemaphoreType.DMA((n_space,)),
            pltpu.SemaphoreType.DMA((n_space,)),
            pltpu.SemaphoreType.DMA((n_tm,)),
            pltpu.SemaphoreType.DMA((n_tm,)),
            pltpu.SemaphoreType.DMA((n_space,)),
            pltpu.SemaphoreType.DMA((n_space,)),
        ],
        compiler_params=pltpu.CompilerParams(collective_id=0, has_side_effects=True),
    )(chunks)
    return out.reshape(size, size)


def a2a_kernel(n_tm, src_at, dst_at, x_ref, out_ref, buf, send, recv, own):
    s = lax.axis_index("space")
    t = lax.axis_index("tm")
    barrier = pltpu.get_barrier_semaphore()
    for k in range(1, n_tm):
        a = lax.rem(t + k, n_tm)
        pl.semaphore_signal(barrier, inc=1, device_id=(s, a), device_id_type=MESH)
    pl.semaphore_wait(barrier, n_tm - 1)
    copies = []
    for k in range(1, n_tm):
        a = lax.rem(t + k, n_tm)
        c = pltpu.make_async_remote_copy(
            src_ref=src_at(x_ref, a), dst_ref=dst_at(buf, t), send_sem=send.at[k], recv_sem=recv.at[t],
            device_id=(s, a), device_id_type=MESH,
        )
        c.start()
        copies.append(c)
    mine = pltpu.make_async_copy(src_at(x_ref, t), dst_at(buf, t), own.at[0])
    mine.start()
    mine.wait()
    for k in range(1, n_tm):
        j = lax.rem(t + k, n_tm)
        pltpu.make_async_remote_copy(
            src_ref=src_at(x_ref, j), dst_ref=dst_at(buf, j), send_sem=send.at[k], recv_sem=recv.at[j],
            device_id=(s, j), device_id_type=MESH,
        ).wait_recv()
    for c in copies:
        c.wait_send()
    out_ref[...] = buf[...]


def all_to_all(x, out_shape, src_at, dst_at, cid):
    n_tm = lax.axis_size("tm")
    return pl.pallas_call(
        functools.partial(a2a_kernel, n_tm, src_at, dst_at),
        out_shape=jax.ShapeDtypeStruct(out_shape, x.dtype),
        in_specs=[pl.BlockSpec(memory_space=pltpu.VMEM)],
        out_specs=pl.BlockSpec(memory_space=pltpu.VMEM),
        scratch_shapes=[
            pltpu.VMEM(out_shape, x.dtype),
            pltpu.SemaphoreType.DMA((n_tm,)),
            pltpu.SemaphoreType.DMA((n_tm,)),
            pltpu.SemaphoreType.DMA((1,)),
        ],
        compiler_params=pltpu.CompilerParams(collective_id=cid, has_side_effects=True),
    )(x)


def lanes(a, width):
    return pl.ds(pl.multiple_of(a * width, width), width)


def bdot(x, y):
    return jnp.einsum("nab,nbc->nac", x, y, precision=HIGH, preferred_element_type=jnp.float32)


def bdot_t(x, y):
    return jnp.einsum("nac,nbc->nab", x, y, precision=HIGH, preferred_element_type=jnp.float32)


def iotas(shape):
    return lax.broadcasted_iota(jnp.int32, shape, 1), lax.broadcasted_iota(jnp.int32, shape, 2)


def merge_coeffs(h):
    n = h.shape[0]
    kt = h[:, :RANK, :] + h[:, RANK:, :]
    row, col = iotas(h.shape)
    dcol = jnp.sum(jnp.where(row == col, h, 0.0), axis=2, keepdims=True)
    scales = jnp.sqrt(dcol[:, :RANK] + dcol[:, RANK:])
    inner = bdot_t(bdot(kt, h), kt)
    row, col = iotas(inner.shape)
    eye = jnp.where(row == col, 1.0, 0.0)

    def step(j, carry):
        a, r = carry
        at_row = row == j
        at_col = col == j
        a_row = jnp.sum(jnp.where(at_row, a, 0.0), axis=1, keepdims=True)
        r_row = jnp.sum(jnp.where(at_row, r, 0.0), axis=1, keepdims=True)
        a_col = jnp.sum(jnp.where(at_col, a, 0.0), axis=2, keepdims=True)
        pivot = jnp.sum(jnp.where(at_col[:, :1], a_row, 0.0), axis=2, keepdims=True)
        factor = jnp.where(row[:, :, :1] > j, a_col / pivot, 0.0)
        return a - factor * a_row, r - factor * r_row

    a, r = lax.fori_loop(0, RANK, step, (inner, eye * jnp.ones((n, 1, 1), jnp.float32)))
    diag_u = jnp.sum(jnp.where(row == col, a, 0.0), axis=2, keepdims=True)
    return bdot(r * (scales / jnp.sqrt(diag_u)), kt)


def place(x, offset, width):
    n, _, w = x.shape
    row, col = iotas((n, w, width))
    return bdot(x, jnp.where(col == row + offset, 1.0, 0.0))


def tree_kernel(h0_ref, g1_ref, g2_ref, out_ref):
    ct = merge_coeffs(h0_ref[...])
    basis = ct
    for g_ref in (g1_ref, g2_ref):
        n = g_ref.shape[0]
        w = basis.shape[2]
        pairs = basis.reshape(n, 2, RANK, w)
        bt = jnp.concatenate(
            [place(pairs[:, 0], 0, 2 * w), place(pairs[:, 1], w, 2 * w)], axis=1
        )
        h = bdot_t(bdot(bt, g_ref[...]), bt)
        basis = bdot(merge_coeffs(h), bt)
    out_ref[...] = basis


def tree_pallas(gram, leaves):
    size = 2 * RANK
    h0 = jnp.stack([gram[k * size : (k + 1) * size, k * size : (k + 1) * size] for k in range(leaves // 2)])
    big = 2 * size
    g1 = jnp.stack([gram[k * big : (k + 1) * big, k * big : (k + 1) * big] for k in range(leaves // 4)])
    g2 = gram[None]
    out = pl.pallas_call(
        tree_kernel,
        out_shape=jax.ShapeDtypeStruct((1, RANK, leaves * RANK), jnp.float32),
        in_specs=[pl.BlockSpec(memory_space=pltpu.VMEM)] * 3,
        out_specs=pl.BlockSpec(memory_space=pltpu.VMEM),
    )(h0, g1, g2)
    return out[0]


def local(velocity):
    rows = velocity.shape[2]
    span_v = halo_rows(velocity[:, 1], 2).astype(jnp.float32)
    stream_u = velocity[:, 0].astype(jnp.float32)
    dv_dx = (
        8.0 * (span_v[:, 3 : rows + 3] - span_v[:, 1 : rows + 1])
        - (span_v[:, 4:] - span_v[:, :rows])
    ) / 12.0
    vorticity = (dv_dx - spanwise(stream_u)).astype(jnp.bfloat16)
    blocks = lax.axis_size("tm")
    cols = vorticity.shape[2]
    width = cols // blocks
    cells = all_to_all(
        vorticity,
        (blocks,) + vorticity.shape[:2] + (width,),
        lambda ref, a: ref.at[:, :, lanes(a, width)],
        lambda ref, j: ref.at[j],
        1,
    ).reshape(blocks * RANK, rows, width)
    gram = jnp.einsum("axz,bxz->ab", cells, cells, preferred_element_type=jnp.float32)
    gram = allreduce(gram)
    basis_t = tree_pallas(gram, blocks)
    part = jnp.einsum("ba,axz->bxz", basis_t, cells.astype(jnp.float32), precision=HIGH)
    share = RANK // blocks
    modes = all_to_all(
        part,
        (share, rows, cols),
        lambda ref, a: ref.at[pl.ds(a * share, share)],
        lambda ref, j: ref.at[:, :, lanes(j, width)],
        2,
    )
    return (vorticity, modes)


def solution(mesh):
    in_specs = (P("tm", None, "space", None),)
    out_specs = (P("tm", "space", None), P("tm", "space", None))
    return jax.shard_map(local, mesh=mesh, in_specs=in_specs, out_specs=out_specs, check_vma=False)
```

```python
import functools

import jax
import jax.numpy as jnp
from jax import lax
from jax.experimental import pallas as pl
from jax.experimental.pallas import tpu as pltpu
from jax.sharding import PartitionSpec as P

RANK = 32
HIGH = lax.Precision.HIGHEST


def halo_rows(block, width):
    count = lax.axis_size("space")
    forward = [(i, (i + 1) % count) for i in range(count)]
    backward = [(target, source) for source, target in forward]
    rows = block.shape[1]
    low = lax.ppermute(block[:, rows - width :], "space", forward)
    high = lax.ppermute(block[:, :width], "space", backward)
    return jnp.concatenate([low, block, high], axis=1)


def spanwise(field):
    ahead = jnp.roll(field, -1, 2)
    behind = jnp.roll(field, 1, 2)
    ahead_two = jnp.roll(field, -2, 2)
    behind_two = jnp.roll(field, 2, 2)
    return (8.0 * (ahead - behind) - (ahead_two - behind_two)) / 12.0


MESH = pl.DeviceIdType.MESH


def allreduce_kernel(n_space, n_tm, g_ref, out_ref, buf1, buf2, buf3, send1, recv1, send2, recv2, send3, recv3):
    s = lax.axis_index("space")
    t = lax.axis_index("tm")

    barrier = pltpu.get_barrier_semaphore()

    def greet_space(k, carry):
        b = lax.rem(s + k, n_space)
        pl.semaphore_signal(barrier, inc=1, device_id=(b, t), device_id_type=MESH)
        return carry

    def greet_tm(k, carry):
        a = lax.rem(t + k, n_tm)
        pl.semaphore_signal(barrier, inc=1, device_id=(s, a), device_id_type=MESH)
        return carry

    lax.fori_loop(1, n_space, greet_space, 0)
    lax.fori_loop(1, n_tm, greet_tm, 0)
    pl.semaphore_wait(barrier, (n_space - 1) + (n_tm - 1))

    def space_copy(src, dst_buf, send, recv, k):
        b = lax.rem(s + k, n_space)
        return pltpu.make_async_remote_copy(
            src_ref=src(b), dst_ref=dst_buf.at[s], send_sem=send.at[k], recv_sem=recv.at[s],
            device_id=(b, t), device_id_type=MESH,
        )

    def space_wait(dst_buf, send, recv, k):
        j = lax.rem(s + k, n_space)
        pltpu.make_async_remote_copy(
            src_ref=dst_buf.at[j], dst_ref=dst_buf.at[j], send_sem=send.at[k], recv_sem=recv.at[j],
            device_id=(j, t), device_id_type=MESH,
        ).wait_recv()

    def send_p1(k, carry):
        space_copy(lambda b: g_ref.at[b], buf1, send1, recv1, k).start()
        return carry

    lax.fori_loop(1, n_space, send_p1, 0)
    buf1[s] = g_ref[s]

    def wait_p1(k, carry):
        space_wait(buf1, send1, recv1, k)
        return carry

    lax.fori_loop(1, n_space, wait_p1, 0)
    acc = buf1[0]
    for j in range(1, n_space):
        acc = acc + buf1[j]
    buf2[t] = acc

    copies = []
    for k in range(1, n_tm):
        a = lax.rem(t + k, n_tm)
        c = pltpu.make_async_remote_copy(
            src_ref=buf2.at[t], dst_ref=buf2.at[t], send_sem=send2.at[k], recv_sem=recv2.at[t],
            device_id=(s, a), device_id_type=MESH,
        )
        c.start()
        copies.append(c)
    for k in range(1, n_tm):
        j = lax.rem(t + k, n_tm)
        pltpu.make_async_remote_copy(
            src_ref=buf2.at[j], dst_ref=buf2.at[j], send_sem=send2.at[k], recv_sem=recv2.at[j],
            device_id=(s, j), device_id_type=MESH,
        ).wait_recv()
    for c in copies:
        c.wait_send()
    acc = buf2[0]
    for j in range(1, n_tm):
        acc = acc + buf2[j]
    buf3[s] = acc

    def send_p3(k, carry):
        space_copy(lambda b: buf3.at[s], buf3, send3, recv3, k).start()
        return carry

    lax.fori_loop(1, n_space, send_p3, 0)

    def wait_p3(k, carry):
        space_wait(buf3, send3, recv3, k)
        return carry

    lax.fori_loop(1, n_space, wait_p3, 0)

    def drain(k, carry):
        space_copy(lambda b: g_ref.at[b], buf1, send1, recv1, k).wait_send()
        space_copy(lambda b: buf3.at[s], buf3, send3, recv3, k).wait_send()
        return carry

    lax.fori_loop(1, n_space, drain, 0)
    out_ref[...] = buf3[...]


def allreduce(gram):
    n_space = lax.axis_size("space")
    n_tm = lax.axis_size("tm")
    size = gram.shape[0]
    chunks = gram.reshape(n_space, size // n_space, size)
    shape = chunks.shape
    out = pl.pallas_call(
        functools.partial(allreduce_kernel, n_space, n_tm),
        out_shape=jax.ShapeDtypeStruct(shape, jnp.float32),
        in_specs=[pl.BlockSpec(memory_space=pltpu.VMEM)],
        out_specs=pl.BlockSpec(memory_space=pltpu.VMEM),
        scratch_shapes=[
            pltpu.VMEM(shape, jnp.float32),
            pltpu.VMEM((n_tm,) + shape[1:], jnp.float32),
            pltpu.VMEM(shape, jnp.float32),
            pltpu.SemaphoreType.DMA((n_space,)),
            pltpu.SemaphoreType.DMA((n_space,)),
            pltpu.SemaphoreType.DMA((n_tm,)),
            pltpu.SemaphoreType.DMA((n_tm,)),
            pltpu.SemaphoreType.DMA((n_space,)),
            pltpu.SemaphoreType.DMA((n_space,)),
        ],
        compiler_params=pltpu.CompilerParams(collective_id=0, has_side_effects=True),
    )(chunks)
    return out.reshape(size, size)


def a2a_kernel(n_tm, src_at, dst_at, x_ref, out_ref, buf, send, recv, own):
    s = lax.axis_index("space")
    t = lax.axis_index("tm")
    barrier = pltpu.get_barrier_semaphore()
    for k in range(1, n_tm):
        a = lax.rem(t + k, n_tm)
        pl.semaphore_signal(barrier, inc=1, device_id=(s, a), device_id_type=MESH)
    pl.semaphore_wait(barrier, n_tm - 1)
    copies = []
    for k in range(1, n_tm):
        a = lax.rem(t + k, n_tm)
        c = pltpu.make_async_remote_copy(
            src_ref=src_at(x_ref, a), dst_ref=dst_at(buf, t), send_sem=send.at[k], recv_sem=recv.at[t],
            device_id=(s, a), device_id_type=MESH,
        )
        c.start()
        copies.append(c)
    mine = pltpu.make_async_copy(src_at(x_ref, t), dst_at(buf, t), own.at[0])
    mine.start()
    mine.wait()
    for k in range(1, n_tm):
        j = lax.rem(t + k, n_tm)
        pltpu.make_async_remote_copy(
            src_ref=src_at(x_ref, j), dst_ref=dst_at(buf, j), send_sem=send.at[k], recv_sem=recv.at[j],
            device_id=(s, j), device_id_type=MESH,
        ).wait_recv()
    for c in copies:
        c.wait_send()
    out_ref[...] = buf[...]


def all_to_all(x, out_shape, src_at, dst_at, cid):
    n_tm = lax.axis_size("tm")
    return pl.pallas_call(
        functools.partial(a2a_kernel, n_tm, src_at, dst_at),
        out_shape=jax.ShapeDtypeStruct(out_shape, x.dtype),
        in_specs=[pl.BlockSpec(memory_space=pltpu.VMEM)],
        out_specs=pl.BlockSpec(memory_space=pltpu.VMEM),
        scratch_shapes=[
            pltpu.VMEM(out_shape, x.dtype),
            pltpu.SemaphoreType.DMA((n_tm,)),
            pltpu.SemaphoreType.DMA((n_tm,)),
            pltpu.SemaphoreType.DMA((1,)),
        ],
        compiler_params=pltpu.CompilerParams(collective_id=cid, has_side_effects=True),
    )(x)


def lanes(a, width):
    return pl.ds(pl.multiple_of(a * width, width), width)


def bdot(x, y):
    return jnp.einsum("nab,nbc->nac", x, y, precision=HIGH, preferred_element_type=jnp.float32)


def bdot_t(x, y):
    return jnp.einsum("nac,nbc->nab", x, y, precision=HIGH, preferred_element_type=jnp.float32)


def iotas(shape):
    return lax.broadcasted_iota(jnp.int32, shape, 1), lax.broadcasted_iota(jnp.int32, shape, 2)


def merge_coeffs(h):
    n = h.shape[0]
    kt = h[:, :RANK, :] + h[:, RANK:, :]
    row, col = iotas(h.shape)
    dcol = jnp.sum(jnp.where(row == col, h, 0.0), axis=2, keepdims=True)
    scales = jnp.sqrt(dcol[:, :RANK] + dcol[:, RANK:])
    inner = bdot_t(bdot(kt, h), kt)
    row, col = iotas(inner.shape)
    eye = jnp.where(row == col, 1.0, 0.0)

    def step(j, carry):
        a, r = carry
        at_row = row == j
        at_col = col == j
        a_row = jnp.sum(jnp.where(at_row, a, 0.0), axis=1, keepdims=True)
        r_row = jnp.sum(jnp.where(at_row, r, 0.0), axis=1, keepdims=True)
        a_col = jnp.sum(jnp.where(at_col, a, 0.0), axis=2, keepdims=True)
        pivot = jnp.sum(jnp.where(at_col[:, :1], a_row, 0.0), axis=2, keepdims=True)
        factor = jnp.where(row[:, :, :1] > j, a_col / pivot, 0.0)
        return a - factor * a_row, r - factor * r_row

    a, r = lax.fori_loop(0, RANK, step, (inner, eye * jnp.ones((n, 1, 1), jnp.float32)))
    diag_u = jnp.sum(jnp.where(row == col, a, 0.0), axis=2, keepdims=True)
    return bdot(r * (scales / jnp.sqrt(diag_u)), kt)


def place(x, offset, width):
    n, _, w = x.shape
    row, col = iotas((n, w, width))
    return bdot(x, jnp.where(col == row + offset, 1.0, 0.0))


def tree_levels(g_ref):
    size = 2 * RANK
    leaves = g_ref.shape[0] // RANK
    picks = []
    for k in range(leaves // 2):
        lane0 = (k * size) // 128 * 128
        block = g_ref[k * size : (k + 1) * size, lane0 : lane0 + 128][None]
        picks.append(place(block, -(k * size - lane0), size))
    basis = merge_coeffs(jnp.concatenate(picks, axis=0))
    while basis.shape[0] > 1:
        n = basis.shape[0] // 2
        w = basis.shape[2]
        pairs = basis.reshape(n, 2, RANK, w)
        bt = jnp.concatenate(
            [place(pairs[:, 0], 0, 2 * w), place(pairs[:, 1], w, 2 * w)], axis=1
        )
        gs = jnp.concatenate(
            [g_ref[k * 2 * w : (k + 1) * 2 * w, k * 2 * w : (k + 1) * 2 * w][None] for k in range(n)],
            axis=0,
        )
        h = bdot_t(bdot(bt, gs), bt)
        basis = bdot(merge_coeffs(h), bt)
    return basis[0]


def finish_kernel(n_tm, g_ref, w_ref, out_ref, part_ref, buf, send, recv, own):
    s = lax.axis_index("space")
    t = lax.axis_index("tm")
    barrier = pltpu.get_barrier_semaphore()
    for k in range(1, n_tm):
        a = lax.rem(t + k, n_tm)
        pl.semaphore_signal(barrier, inc=1, device_id=(s, a), device_id_type=MESH)
    basis_t = tree_levels(g_ref)
    for x in range(w_ref.shape[0]):
        part_ref[x] = jnp.dot(
            basis_t, w_ref[x].astype(jnp.float32), precision=HIGH, preferred_element_type=jnp.float32
        )
    share = part_ref.shape[1] // n_tm
    width = w_ref.shape[2]
    src_at = lambda a: part_ref.at[:, pl.ds(a * share, share), :]
    dst_at = lambda j: buf.at[:, :, lanes(j, width)]
    pl.semaphore_wait(barrier, n_tm - 1)
    copies = []
    for k in range(1, n_tm):
        a = lax.rem(t + k, n_tm)
        c = pltpu.make_async_remote_copy(
            src_ref=src_at(a), dst_ref=dst_at(t), send_sem=send.at[k], recv_sem=recv.at[t],
            device_id=(s, a), device_id_type=MESH,
        )
        c.start()
        copies.append(c)
    mine = pltpu.make_async_copy(src_at(t), dst_at(t), own.at[0])
    mine.start()
    mine.wait()
    for k in range(1, n_tm):
        j = lax.rem(t + k, n_tm)
        pltpu.make_async_remote_copy(
            src_ref=src_at(j), dst_ref=dst_at(j), send_sem=send.at[k], recv_sem=recv.at[j],
            device_id=(s, j), device_id_type=MESH,
        ).wait_recv()
    for c in copies:
        c.wait_send()
    out_ref[...] = buf[...]


def finish(gram, cells_x):
    n_tm = lax.axis_size("tm")
    rows, _, width = cells_x.shape
    share = RANK // n_tm
    out_shape = (rows, share, width * n_tm)
    return pl.pallas_call(
        functools.partial(finish_kernel, n_tm),
        out_shape=jax.ShapeDtypeStruct(out_shape, jnp.float32),
        in_specs=[pl.BlockSpec(memory_space=pltpu.VMEM)] * 2,
        out_specs=pl.BlockSpec(memory_space=pltpu.VMEM),
        scratch_shapes=[
            pltpu.VMEM((rows, RANK, width), jnp.float32),
            pltpu.VMEM(out_shape, jnp.float32),
            pltpu.SemaphoreType.DMA((n_tm,)),
            pltpu.SemaphoreType.DMA((n_tm,)),
            pltpu.SemaphoreType.DMA((1,)),
        ],
        compiler_params=pltpu.CompilerParams(collective_id=2, has_side_effects=True),
    )(gram, cells_x)


def local(velocity):
    rows = velocity.shape[2]
    span_v = halo_rows(velocity[:, 1], 2).astype(jnp.float32)
    stream_u = velocity[:, 0].astype(jnp.float32)
    dv_dx = (
        8.0 * (span_v[:, 3 : rows + 3] - span_v[:, 1 : rows + 1])
        - (span_v[:, 4:] - span_v[:, :rows])
    ) / 12.0
    vorticity = (dv_dx - spanwise(stream_u)).astype(jnp.bfloat16)
    blocks = lax.axis_size("tm")
    cols = vorticity.shape[2]
    width = cols // blocks
    vort_x = jnp.swapaxes(vorticity, 0, 1)
    cells_x = all_to_all(
        vort_x,
        (rows, blocks * RANK, width),
        lambda ref, a: ref.at[:, :, lanes(a, width)],
        lambda ref, j: ref.at[:, pl.ds(j * RANK, RANK), :],
        1,
    )
    gram = jnp.einsum("xaz,xbz->ab", cells_x, cells_x, preferred_element_type=jnp.float32)
    gram = allreduce(gram)
    modes = jnp.swapaxes(finish(gram, cells_x), 0, 1)
    return (vorticity, modes)


def solution(mesh):
    in_specs = (P("tm", None, "space", None),)
    out_specs = (P("tm", "space", None), P("tm", "space", None))
    return jax.shard_map(local, mesh=mesh, in_specs=in_specs, out_specs=out_specs, check_vma=False)
```

```python
import functools

import jax
import jax.numpy as jnp
from jax import lax
from jax.experimental import pallas as pl
from jax.experimental.pallas import tpu as pltpu
from jax.sharding import PartitionSpec as P

RANK = 32
HIGH = lax.Precision.HIGHEST


def halo_rows(block, width):
    count = lax.axis_size("space")
    forward = [(i, (i + 1) % count) for i in range(count)]
    backward = [(target, source) for source, target in forward]
    rows = block.shape[1]
    low = lax.ppermute(block[:, rows - width :], "space", forward)
    high = lax.ppermute(block[:, :width], "space", backward)
    return jnp.concatenate([low, block, high], axis=1)


def spanwise(field):
    ahead = jnp.roll(field, -1, 2)
    behind = jnp.roll(field, 1, 2)
    ahead_two = jnp.roll(field, -2, 2)
    behind_two = jnp.roll(field, 2, 2)
    return (8.0 * (ahead - behind) - (ahead_two - behind_two)) / 12.0


MESH = pl.DeviceIdType.MESH


def allreduce_kernel(n_space, n_tm, g_ref, out_ref, buf1, buf2, buf3, send1, recv1, send2, recv2, send3, recv3):
    s = lax.axis_index("space")
    t = lax.axis_index("tm")

    barrier = pltpu.get_barrier_semaphore()

    def greet_space(k, carry):
        b = lax.rem(s + k, n_space)
        pl.semaphore_signal(barrier, inc=1, device_id=(b, t), device_id_type=MESH)
        return carry

    def greet_tm(k, carry):
        a = lax.rem(t + k, n_tm)
        pl.semaphore_signal(barrier, inc=1, device_id=(s, a), device_id_type=MESH)
        return carry

    lax.fori_loop(1, n_space, greet_space, 0)
    lax.fori_loop(1, n_tm, greet_tm, 0)
    pl.semaphore_wait(barrier, (n_space - 1) + (n_tm - 1))

    def space_copy(src, dst_buf, send, recv, k):
        b = lax.rem(s + k, n_space)
        return pltpu.make_async_remote_copy(
            src_ref=src(b), dst_ref=dst_buf.at[s], send_sem=send.at[k], recv_sem=recv.at[s],
            device_id=(b, t), device_id_type=MESH,
        )

    def space_wait(dst_buf, send, recv, k):
        j = lax.rem(s + k, n_space)
        pltpu.make_async_remote_copy(
            src_ref=dst_buf.at[j], dst_ref=dst_buf.at[j], send_sem=send.at[k], recv_sem=recv.at[j],
            device_id=(j, t), device_id_type=MESH,
        ).wait_recv()

    def send_p1(k, carry):
        space_copy(lambda b: g_ref.at[b], buf1, send1, recv1, k).start()
        return carry

    lax.fori_loop(1, n_space, send_p1, 0)
    buf1[s] = g_ref[s]

    def wait_p1(k, carry):
        space_wait(buf1, send1, recv1, k)
        return carry

    lax.fori_loop(1, n_space, wait_p1, 0)
    acc = buf1[0]
    for j in range(1, n_space):
        acc = acc + buf1[j]
    buf2[t] = acc

    copies = []
    for k in range(1, n_tm):
        a = lax.rem(t + k, n_tm)
        c = pltpu.make_async_remote_copy(
            src_ref=buf2.at[t], dst_ref=buf2.at[t], send_sem=send2.at[k], recv_sem=recv2.at[t],
            device_id=(s, a), device_id_type=MESH,
        )
        c.start()
        copies.append(c)
    for k in range(1, n_tm):
        j = lax.rem(t + k, n_tm)
        pltpu.make_async_remote_copy(
            src_ref=buf2.at[j], dst_ref=buf2.at[j], send_sem=send2.at[k], recv_sem=recv2.at[j],
            device_id=(s, j), device_id_type=MESH,
        ).wait_recv()
    for c in copies:
        c.wait_send()
    acc = buf2[0]
    for j in range(1, n_tm):
        acc = acc + buf2[j]
    buf3[s] = acc

    def send_p3(k, carry):
        space_copy(lambda b: buf3.at[s], buf3, send3, recv3, k).start()
        return carry

    lax.fori_loop(1, n_space, send_p3, 0)

    def wait_p3(k, carry):
        space_wait(buf3, send3, recv3, k)
        return carry

    lax.fori_loop(1, n_space, wait_p3, 0)

    def drain(k, carry):
        space_copy(lambda b: g_ref.at[b], buf1, send1, recv1, k).wait_send()
        space_copy(lambda b: buf3.at[s], buf3, send3, recv3, k).wait_send()
        return carry

    lax.fori_loop(1, n_space, drain, 0)
    out_ref[...] = buf3[...]


def allreduce(gram):
    n_space = lax.axis_size("space")
    n_tm = lax.axis_size("tm")
    size = gram.shape[0]
    chunks = gram.reshape(n_space, size // n_space, size)
    shape = chunks.shape
    out = pl.pallas_call(
        functools.partial(allreduce_kernel, n_space, n_tm),
        out_shape=jax.ShapeDtypeStruct(shape, jnp.float32),
        in_specs=[pl.BlockSpec(memory_space=pltpu.VMEM)],
        out_specs=pl.BlockSpec(memory_space=pltpu.VMEM),
        scratch_shapes=[
            pltpu.VMEM(shape, jnp.float32),
            pltpu.VMEM((n_tm,) + shape[1:], jnp.float32),
            pltpu.VMEM(shape, jnp.float32),
            pltpu.SemaphoreType.DMA((n_space,)),
            pltpu.SemaphoreType.DMA((n_space,)),
            pltpu.SemaphoreType.DMA((n_tm,)),
            pltpu.SemaphoreType.DMA((n_tm,)),
            pltpu.SemaphoreType.DMA((n_space,)),
            pltpu.SemaphoreType.DMA((n_space,)),
        ],
        compiler_params=pltpu.CompilerParams(collective_id=0, has_side_effects=True),
    )(chunks)
    return out.reshape(size, size)


def a2a_kernel(n_tm, src_at, dst_at, x_ref, out_ref, buf, send, recv, own):
    s = lax.axis_index("space")
    t = lax.axis_index("tm")
    barrier = pltpu.get_barrier_semaphore()
    for k in range(1, n_tm):
        a = lax.rem(t + k, n_tm)
        pl.semaphore_signal(barrier, inc=1, device_id=(s, a), device_id_type=MESH)
    pl.semaphore_wait(barrier, n_tm - 1)
    copies = []
    for k in range(1, n_tm):
        a = lax.rem(t + k, n_tm)
        c = pltpu.make_async_remote_copy(
            src_ref=src_at(x_ref, a), dst_ref=dst_at(buf, t), send_sem=send.at[k], recv_sem=recv.at[t],
            device_id=(s, a), device_id_type=MESH,
        )
        c.start()
        copies.append(c)
    mine = pltpu.make_async_copy(src_at(x_ref, t), dst_at(buf, t), own.at[0])
    mine.start()
    mine.wait()
    for k in range(1, n_tm):
        j = lax.rem(t + k, n_tm)
        pltpu.make_async_remote_copy(
            src_ref=src_at(x_ref, j), dst_ref=dst_at(buf, j), send_sem=send.at[k], recv_sem=recv.at[j],
            device_id=(s, j), device_id_type=MESH,
        ).wait_recv()
    for c in copies:
        c.wait_send()
    out_ref[...] = buf[...]


def all_to_all(x, out_shape, src_at, dst_at, cid):
    n_tm = lax.axis_size("tm")
    return pl.pallas_call(
        functools.partial(a2a_kernel, n_tm, src_at, dst_at),
        out_shape=jax.ShapeDtypeStruct(out_shape, x.dtype),
        in_specs=[pl.BlockSpec(memory_space=pltpu.VMEM)],
        out_specs=pl.BlockSpec(memory_space=pltpu.VMEM),
        scratch_shapes=[
            pltpu.VMEM(out_shape, x.dtype),
            pltpu.SemaphoreType.DMA((n_tm,)),
            pltpu.SemaphoreType.DMA((n_tm,)),
            pltpu.SemaphoreType.DMA((1,)),
        ],
        compiler_params=pltpu.CompilerParams(collective_id=cid, has_side_effects=True),
    )(x)


def lanes(a, width):
    return pl.ds(pl.multiple_of(a * width, width), width)


def bdot(x, y):
    return jnp.einsum("nab,nbc->nac", x, y, precision=HIGH, preferred_element_type=jnp.float32)


def bdot_t(x, y):
    return jnp.einsum("nac,nbc->nab", x, y, precision=HIGH, preferred_element_type=jnp.float32)


def iotas(shape):
    return lax.broadcasted_iota(jnp.int32, shape, 1), lax.broadcasted_iota(jnp.int32, shape, 2)


def merge_coeffs(h):
    n = h.shape[0]
    kt = h[:, :RANK, :] + h[:, RANK:, :]
    row, col = iotas(h.shape)
    dcol = jnp.sum(jnp.where(row == col, h, 0.0), axis=2, keepdims=True)
    scales = jnp.sqrt(dcol[:, :RANK] + dcol[:, RANK:])
    inner = bdot_t(bdot(kt, h), kt)
    row, col = iotas(inner.shape)
    eye = jnp.where(row == col, 1.0, 0.0)

    def step(j, carry):
        a, r = carry
        at_row = row == j
        at_col = col == j
        a_row = jnp.sum(jnp.where(at_row, a, 0.0), axis=1, keepdims=True)
        r_row = jnp.sum(jnp.where(at_row, r, 0.0), axis=1, keepdims=True)
        a_col = jnp.sum(jnp.where(at_col, a, 0.0), axis=2, keepdims=True)
        pivot = jnp.sum(jnp.where(at_col[:, :1], a_row, 0.0), axis=2, keepdims=True)
        factor = jnp.where(row[:, :, :1] > j, a_col / pivot, 0.0)
        return a - factor * a_row, r - factor * r_row

    a, r = lax.fori_loop(0, RANK, step, (inner, eye * jnp.ones((n, 1, 1), jnp.float32)), unroll=True)
    diag_u = jnp.sum(jnp.where(row == col, a, 0.0), axis=2, keepdims=True)
    return bdot(r * (scales / jnp.sqrt(diag_u)), kt)


def place(x, offset, width):
    n, _, w = x.shape
    row, col = iotas((n, w, width))
    return bdot(x, jnp.where(col == row + offset, 1.0, 0.0))


def tree_levels(g_ref):
    size = 2 * RANK
    leaves = g_ref.shape[0] // RANK
    picks = []
    for k in range(leaves // 2):
        lane0 = (k * size) // 128 * 128
        block = g_ref[k * size : (k + 1) * size, lane0 : lane0 + 128][None]
        picks.append(place(block, -(k * size - lane0), size))
    basis = merge_coeffs(jnp.concatenate(picks, axis=0))
    while basis.shape[0] > 1:
        n = basis.shape[0] // 2
        w = basis.shape[2]
        pairs = basis.reshape(n, 2, RANK, w)
        bt = jnp.concatenate(
            [place(pairs[:, 0], 0, 2 * w), place(pairs[:, 1], w, 2 * w)], axis=1
        )
        gs = jnp.concatenate(
            [g_ref[k * 2 * w : (k + 1) * 2 * w, k * 2 * w : (k + 1) * 2 * w][None] for k in range(n)],
            axis=0,
        )
        h = bdot_t(bdot(bt, gs), bt)
        basis = bdot(merge_coeffs(h), bt)
    return basis[0]


def finish_kernel(n_tm, g_ref, w_ref, out_ref, part_ref, buf, send, recv, own):
    s = lax.axis_index("space")
    t = lax.axis_index("tm")
    barrier = pltpu.get_barrier_semaphore()
    for k in range(1, n_tm):
        a = lax.rem(t + k, n_tm)
        pl.semaphore_signal(barrier, inc=1, device_id=(s, a), device_id_type=MESH)
    basis_t = tree_levels(g_ref)
    for x in range(w_ref.shape[0]):
        part_ref[x] = jnp.dot(
            basis_t, w_ref[x].astype(jnp.float32), precision=HIGH, preferred_element_type=jnp.float32
        )
    share = part_ref.shape[1] // n_tm
    width = w_ref.shape[2]
    src_at = lambda a: part_ref.at[:, pl.ds(a * share, share), :]
    dst_at = lambda j: buf.at[:, :, lanes(j, width)]
    pl.semaphore_wait(barrier, n_tm - 1)
    copies = []
    for k in range(1, n_tm):
        a = lax.rem(t + k, n_tm)
        c = pltpu.make_async_remote_copy(
            src_ref=src_at(a), dst_ref=dst_at(t), send_sem=send.at[k], recv_sem=recv.at[t],
            device_id=(s, a), device_id_type=MESH,
        )
        c.start()
        copies.append(c)
    mine = pltpu.make_async_copy(src_at(t), dst_at(t), own.at[0])
    mine.start()
    mine.wait()
    for k in range(1, n_tm):
        j = lax.rem(t + k, n_tm)
        pltpu.make_async_remote_copy(
            src_ref=src_at(j), dst_ref=dst_at(j), send_sem=send.at[k], recv_sem=recv.at[j],
            device_id=(s, j), device_id_type=MESH,
        ).wait_recv()
    for c in copies:
        c.wait_send()
    out_ref[...] = buf[...]


def finish(gram, cells_x):
    n_tm = lax.axis_size("tm")
    rows, _, width = cells_x.shape
    share = RANK // n_tm
    out_shape = (rows, share, width * n_tm)
    return pl.pallas_call(
        functools.partial(finish_kernel, n_tm),
        out_shape=jax.ShapeDtypeStruct(out_shape, jnp.float32),
        in_specs=[pl.BlockSpec(memory_space=pltpu.VMEM)] * 2,
        out_specs=pl.BlockSpec(memory_space=pltpu.VMEM),
        scratch_shapes=[
            pltpu.VMEM((rows, RANK, width), jnp.float32),
            pltpu.VMEM(out_shape, jnp.float32),
            pltpu.SemaphoreType.DMA((n_tm,)),
            pltpu.SemaphoreType.DMA((n_tm,)),
            pltpu.SemaphoreType.DMA((1,)),
        ],
        compiler_params=pltpu.CompilerParams(collective_id=2, has_side_effects=True),
    )(gram, cells_x)


def local(velocity):
    rows = velocity.shape[2]
    span_v = halo_rows(velocity[:, 1], 2).astype(jnp.float32)
    stream_u = velocity[:, 0].astype(jnp.float32)
    dv_dx = (
        8.0 * (span_v[:, 3 : rows + 3] - span_v[:, 1 : rows + 1])
        - (span_v[:, 4:] - span_v[:, :rows])
    ) / 12.0
    vorticity = (dv_dx - spanwise(stream_u)).astype(jnp.bfloat16)
    blocks = lax.axis_size("tm")
    cols = vorticity.shape[2]
    width = cols // blocks
    vort_x = jnp.swapaxes(vorticity, 0, 1)
    cells_x = all_to_all(
        vort_x,
        (rows, blocks * RANK, width),
        lambda ref, a: ref.at[:, :, lanes(a, width)],
        lambda ref, j: ref.at[:, pl.ds(j * RANK, RANK), :],
        1,
    )
    gram = jnp.einsum("xaz,xbz->ab", cells_x, cells_x, preferred_element_type=jnp.float32)
    gram = allreduce(gram)
    modes = jnp.swapaxes(finish(gram, cells_x), 0, 1)
    return (vorticity, modes)


def solution(mesh):
    in_specs = (P("tm", None, "space", None),)
    out_specs = (P("tm", "space", None), P("tm", "space", None))
    return jax.shard_map(local, mesh=mesh, in_specs=in_specs, out_specs=out_specs, check_vma=False)
```

```python
import functools

import jax
import jax.numpy as jnp
from jax import lax
from jax.experimental import pallas as pl
from jax.experimental.pallas import tpu as pltpu
from jax.sharding import PartitionSpec as P

RANK = 32
HIGH = lax.Precision.HIGHEST


def halo_rows(block, width):
    count = lax.axis_size("space")
    forward = [(i, (i + 1) % count) for i in range(count)]
    backward = [(target, source) for source, target in forward]
    rows = block.shape[1]
    low = lax.ppermute(block[:, rows - width :], "space", forward)
    high = lax.ppermute(block[:, :width], "space", backward)
    return jnp.concatenate([low, block, high], axis=1)


def spanwise(field):
    ahead = jnp.roll(field, -1, 2)
    behind = jnp.roll(field, 1, 2)
    ahead_two = jnp.roll(field, -2, 2)
    behind_two = jnp.roll(field, 2, 2)
    return (8.0 * (ahead - behind) - (ahead_two - behind_two)) / 12.0


MESH = pl.DeviceIdType.MESH


def greet_all(n_space, n_tm):
    s = lax.axis_index("space")
    t = lax.axis_index("tm")
    barrier = pltpu.get_barrier_semaphore()

    def greet_space(k, carry):
        b = lax.rem(s + k, n_space)
        pl.semaphore_signal(barrier, inc=1, device_id=(b, t), device_id_type=MESH)
        return carry

    def greet_tm(k, carry):
        a = lax.rem(t + k, n_tm)
        pl.semaphore_signal(barrier, inc=1, device_id=(s, a), device_id_type=MESH)
        return carry

    lax.fori_loop(1, n_space, greet_space, 0)
    lax.fori_loop(1, n_tm, greet_tm, 0)
    pl.semaphore_wait(barrier, (n_space - 1) + (n_tm - 1))


def allreduce_body(n_space, n_tm, g_ref, out_ref, buf1, buf2, buf3, send1, recv1, send2, recv2, send3, recv3):
    s = lax.axis_index("space")
    t = lax.axis_index("tm")

    def space_copy(src, dst_buf, send, recv, k):
        b = lax.rem(s + k, n_space)
        return pltpu.make_async_remote_copy(
            src_ref=src(b), dst_ref=dst_buf.at[s], send_sem=send.at[k], recv_sem=recv.at[s],
            device_id=(b, t), device_id_type=MESH,
        )

    def space_wait(dst_buf, send, recv, k):
        j = lax.rem(s + k, n_space)
        pltpu.make_async_remote_copy(
            src_ref=dst_buf.at[j], dst_ref=dst_buf.at[j], send_sem=send.at[k], recv_sem=recv.at[j],
            device_id=(j, t), device_id_type=MESH,
        ).wait_recv()

    def send_p1(k, carry):
        space_copy(lambda b: g_ref.at[b], buf1, send1, recv1, k).start()
        return carry

    lax.fori_loop(1, n_space, send_p1, 0)
    buf1[s] = g_ref[s]

    def wait_p1(k, carry):
        space_wait(buf1, send1, recv1, k)
        return carry

    lax.fori_loop(1, n_space, wait_p1, 0)
    acc = buf1[0]
    for j in range(1, n_space):
        acc = acc + buf1[j]
    buf2[t] = acc

    copies = []
    for k in range(1, n_tm):
        a = lax.rem(t + k, n_tm)
        c = pltpu.make_async_remote_copy(
            src_ref=buf2.at[t], dst_ref=buf2.at[t], send_sem=send2.at[k], recv_sem=recv2.at[t],
            device_id=(s, a), device_id_type=MESH,
        )
        c.start()
        copies.append(c)
    for k in range(1, n_tm):
        j = lax.rem(t + k, n_tm)
        pltpu.make_async_remote_copy(
            src_ref=buf2.at[j], dst_ref=buf2.at[j], send_sem=send2.at[k], recv_sem=recv2.at[j],
            device_id=(s, j), device_id_type=MESH,
        ).wait_recv()
    for c in copies:
        c.wait_send()
    acc = buf2[0]
    for j in range(1, n_tm):
        acc = acc + buf2[j]
    buf3[s] = acc

    def send_p3(k, carry):
        space_copy(lambda b: buf3.at[s], buf3, send3, recv3, k).start()
        return carry

    lax.fori_loop(1, n_space, send_p3, 0)

    def wait_p3(k, carry):
        space_wait(buf3, send3, recv3, k)
        return carry

    lax.fori_loop(1, n_space, wait_p3, 0)

    def drain(k, carry):
        space_copy(lambda b: g_ref.at[b], buf1, send1, recv1, k).wait_send()
        space_copy(lambda b: buf3.at[s], buf3, send3, recv3, k).wait_send()
        return carry

    lax.fori_loop(1, n_space, drain, 0)
    out_ref[...] = buf3[...]


def a2a_body(n_tm, src_at, dst_at, x_ref, buf, send, recv, own):
    s = lax.axis_index("space")
    t = lax.axis_index("tm")
    copies = []
    for k in range(1, n_tm):
        a = lax.rem(t + k, n_tm)
        c = pltpu.make_async_remote_copy(
            src_ref=src_at(x_ref, a), dst_ref=dst_at(buf, t), send_sem=send.at[k], recv_sem=recv.at[t],
            device_id=(s, a), device_id_type=MESH,
        )
        c.start()
        copies.append(c)
    mine = pltpu.make_async_copy(src_at(x_ref, t), dst_at(buf, t), own.at[0])
    mine.start()
    mine.wait()
    for k in range(1, n_tm):
        j = lax.rem(t + k, n_tm)
        pltpu.make_async_remote_copy(
            src_ref=src_at(x_ref, j), dst_ref=dst_at(buf, j), send_sem=send.at[k], recv_sem=recv.at[j],
            device_id=(s, j), device_id_type=MESH,
        ).wait_recv()
    for c in copies:
        c.wait_send()


def front_kernel(n_space, n_tm, x_ref, cells_ref, g_out_ref, cells, gpart, buf1, buf2, buf3, *sems):
    send, recv, own = sems[:3]
    greet_all(n_space, n_tm)
    rows, _, cols = x_ref.shape
    width = cols // n_tm
    a2a_body(
        n_tm,
        lambda ref, a: ref.at[:, :, lanes(a, width)],
        lambda ref, j: ref.at[:, pl.ds(j * RANK, RANK), :],
        x_ref, cells, send, recv, own,
    )
    size = cells.shape[1]
    gram = jnp.zeros((size, size), jnp.float32)
    for x in range(rows):
        w = cells[x]
        gram = gram + lax.dot_general(
            w, w, (((1,), (1,)), ((), ())), preferred_element_type=jnp.float32
        )
    gpart[...] = gram.reshape(gpart.shape)
    allreduce_body(n_space, n_tm, gpart, g_out_ref, buf1, buf2, buf3, *sems[3:])
    cells_ref[...] = cells[...]


def front(vort_x):
    n_space = lax.axis_size("space")
    n_tm = lax.axis_size("tm")
    rows, _, cols = vort_x.shape
    size = n_tm * RANK
    cells_shape = (rows, size, cols // n_tm)
    chunks = (n_space, size // n_space, size)
    cells_x, gram = pl.pallas_call(
        functools.partial(front_kernel, n_space, n_tm),
        out_shape=(
            jax.ShapeDtypeStruct(cells_shape, vort_x.dtype),
            jax.ShapeDtypeStruct(chunks, jnp.float32),
        ),
        in_specs=[pl.BlockSpec(memory_space=pltpu.VMEM)],
        out_specs=(pl.BlockSpec(memory_space=pltpu.VMEM), pl.BlockSpec(memory_space=pltpu.VMEM)),
        scratch_shapes=[
            pltpu.VMEM(cells_shape, vort_x.dtype),
            pltpu.VMEM(chunks, jnp.float32),
            pltpu.VMEM(chunks, jnp.float32),
            pltpu.VMEM((n_tm,) + chunks[1:], jnp.float32),
            pltpu.VMEM(chunks, jnp.float32),
            pltpu.SemaphoreType.DMA((n_tm,)),
            pltpu.SemaphoreType.DMA((n_tm,)),
            pltpu.SemaphoreType.DMA((1,)),
            pltpu.SemaphoreType.DMA((n_space,)),
            pltpu.SemaphoreType.DMA((n_space,)),
            pltpu.SemaphoreType.DMA((n_tm,)),
            pltpu.SemaphoreType.DMA((n_tm,)),
            pltpu.SemaphoreType.DMA((n_space,)),
            pltpu.SemaphoreType.DMA((n_space,)),
        ],
        compiler_params=pltpu.CompilerParams(collective_id=0, has_side_effects=True),
    )(vort_x)
    return cells_x, gram.reshape(size, size)


def lanes(a, width):
    return pl.ds(pl.multiple_of(a * width, width), width)


def bdot(x, y):
    return jnp.einsum("nab,nbc->nac", x, y, precision=HIGH, preferred_element_type=jnp.float32)


def bdot_t(x, y):
    return jnp.einsum("nac,nbc->nab", x, y, precision=HIGH, preferred_element_type=jnp.float32)


def iotas(shape):
    return lax.broadcasted_iota(jnp.int32, shape, 1), lax.broadcasted_iota(jnp.int32, shape, 2)


def merge_coeffs(h):
    n = h.shape[0]
    kt = h[:, :RANK, :] + h[:, RANK:, :]
    row, col = iotas(h.shape)
    dcol = jnp.sum(jnp.where(row == col, h, 0.0), axis=2, keepdims=True)
    scales = jnp.sqrt(dcol[:, :RANK] + dcol[:, RANK:])
    inner = bdot_t(bdot(kt, h), kt)
    row, col = iotas(inner.shape)
    eye = jnp.where(row == col, 1.0, 0.0)

    def step(j, carry):
        a, r = carry
        at_row = row == j
        at_col = col == j
        a_row = jnp.sum(jnp.where(at_row, a, 0.0), axis=1, keepdims=True)
        r_row = jnp.sum(jnp.where(at_row, r, 0.0), axis=1, keepdims=True)
        a_col = jnp.sum(jnp.where(at_col, a, 0.0), axis=2, keepdims=True)
        pivot = jnp.sum(jnp.where(at_col[:, :1], a_row, 0.0), axis=2, keepdims=True)
        factor = jnp.where(row[:, :, :1] > j, a_col / pivot, 0.0)
        return a - factor * a_row, r - factor * r_row

    a, r = lax.fori_loop(0, RANK, step, (inner, eye * jnp.ones((n, 1, 1), jnp.float32)), unroll=True)
    diag_u = jnp.sum(jnp.where(row == col, a, 0.0), axis=2, keepdims=True)
    return bdot(r * (scales / jnp.sqrt(diag_u)), kt)


def place(x, offset, width):
    n, _, w = x.shape
    row, col = iotas((n, w, width))
    return bdot(x, jnp.where(col == row + offset, 1.0, 0.0))


def tree_levels(g_ref):
    size = 2 * RANK
    leaves = g_ref.shape[0] // RANK
    picks = []
    for k in range(leaves // 2):
        lane0 = (k * size) // 128 * 128
        block = g_ref[k * size : (k + 1) * size, lane0 : lane0 + 128][None]
        picks.append(place(block, -(k * size - lane0), size))
    basis = merge_coeffs(jnp.concatenate(picks, axis=0))
    while basis.shape[0] > 1:
        n = basis.shape[0] // 2
        w = basis.shape[2]
        pairs = basis.reshape(n, 2, RANK, w)
        bt = jnp.concatenate(
            [place(pairs[:, 0], 0, 2 * w), place(pairs[:, 1], w, 2 * w)], axis=1
        )
        gs = jnp.concatenate(
            [g_ref[k * 2 * w : (k + 1) * 2 * w, k * 2 * w : (k + 1) * 2 * w][None] for k in range(n)],
            axis=0,
        )
        h = bdot_t(bdot(bt, gs), bt)
        basis = bdot(merge_coeffs(h), bt)
    return basis[0]


def finish_kernel(n_tm, g_ref, w_ref, out_ref, part_ref, buf, send, recv, own):
    s = lax.axis_index("space")
    t = lax.axis_index("tm")
    barrier = pltpu.get_barrier_semaphore()
    for k in range(1, n_tm):
        a = lax.rem(t + k, n_tm)
        pl.semaphore_signal(barrier, inc=1, device_id=(s, a), device_id_type=MESH)
    basis_t = tree_levels(g_ref)
    for x in range(w_ref.shape[0]):
        part_ref[x] = jnp.dot(
            basis_t, w_ref[x].astype(jnp.float32), precision=HIGH, preferred_element_type=jnp.float32
        )
    share = part_ref.shape[1] // n_tm
    width = w_ref.shape[2]
    src_at = lambda a: part_ref.at[:, pl.ds(a * share, share), :]
    dst_at = lambda j: buf.at[:, :, lanes(j, width)]
    pl.semaphore_wait(barrier, n_tm - 1)
    copies = []
    for k in range(1, n_tm):
        a = lax.rem(t + k, n_tm)
        c = pltpu.make_async_remote_copy(
            src_ref=src_at(a), dst_ref=dst_at(t), send_sem=send.at[k], recv_sem=recv.at[t],
            device_id=(s, a), device_id_type=MESH,
        )
        c.start()
        copies.append(c)
    mine = pltpu.make_async_copy(src_at(t), dst_at(t), own.at[0])
    mine.start()
    mine.wait()
    for k in range(1, n_tm):
        j = lax.rem(t + k, n_tm)
        pltpu.make_async_remote_copy(
            src_ref=src_at(j), dst_ref=dst_at(j), send_sem=send.at[k], recv_sem=recv.at[j],
            device_id=(s, j), device_id_type=MESH,
        ).wait_recv()
    for c in copies:
        c.wait_send()
    out_ref[...] = buf[...]


def finish(gram, cells_x):
    n_tm = lax.axis_size("tm")
    rows, _, width = cells_x.shape
    share = RANK // n_tm
    out_shape = (rows, share, width * n_tm)
    return pl.pallas_call(
        functools.partial(finish_kernel, n_tm),
        out_shape=jax.ShapeDtypeStruct(out_shape, jnp.float32),
        in_specs=[pl.BlockSpec(memory_space=pltpu.VMEM)] * 2,
        out_specs=pl.BlockSpec(memory_space=pltpu.VMEM),
        scratch_shapes=[
            pltpu.VMEM((rows, RANK, width), jnp.float32),
            pltpu.VMEM(out_shape, jnp.float32),
            pltpu.SemaphoreType.DMA((n_tm,)),
            pltpu.SemaphoreType.DMA((n_tm,)),
            pltpu.SemaphoreType.DMA((1,)),
        ],
        compiler_params=pltpu.CompilerParams(collective_id=2, has_side_effects=True),
    )(gram, cells_x)


def local(velocity):
    rows = velocity.shape[2]
    span_v = halo_rows(velocity[:, 1], 2).astype(jnp.float32)
    stream_u = velocity[:, 0].astype(jnp.float32)
    dv_dx = (
        8.0 * (span_v[:, 3 : rows + 3] - span_v[:, 1 : rows + 1])
        - (span_v[:, 4:] - span_v[:, :rows])
    ) / 12.0
    vorticity = (dv_dx - spanwise(stream_u)).astype(jnp.bfloat16)
    blocks = lax.axis_size("tm")
    cols = vorticity.shape[2]
    width = cols // blocks
    vort_x = jnp.swapaxes(vorticity, 0, 1)
    cells_x, gram = front(vort_x)
    modes = jnp.swapaxes(finish(gram, cells_x), 0, 1)
    return (vorticity, modes)


def solution(mesh):
    in_specs = (P("tm", None, "space", None),)
    out_specs = (P("tm", "space", None), P("tm", "space", None))
    return jax.shard_map(local, mesh=mesh, in_specs=in_specs, out_specs=out_specs, check_vma=False)
```

```python
import functools

import jax
import jax.numpy as jnp
from jax import lax
from jax.experimental import pallas as pl
from jax.experimental.pallas import tpu as pltpu
from jax.sharding import PartitionSpec as P

RANK = 32
HIGH = lax.Precision.HIGHEST


def halo_rows(block, width):
    count = lax.axis_size("space")
    forward = [(i, (i + 1) % count) for i in range(count)]
    backward = [(target, source) for source, target in forward]
    rows = block.shape[1]
    low = lax.ppermute(block[:, rows - width :], "space", forward)
    high = lax.ppermute(block[:, :width], "space", backward)
    return jnp.concatenate([low, block, high], axis=1)


def spanwise(field):
    ahead = jnp.roll(field, -1, 2)
    behind = jnp.roll(field, 1, 2)
    ahead_two = jnp.roll(field, -2, 2)
    behind_two = jnp.roll(field, 2, 2)
    return (8.0 * (ahead - behind) - (ahead_two - behind_two)) / 12.0


MESH = pl.DeviceIdType.MESH


def greet_all(n_space, n_tm):
    s = lax.axis_index("space")
    t = lax.axis_index("tm")
    barrier = pltpu.get_barrier_semaphore()

    def greet_space(k, carry):
        b = lax.rem(s + k, n_space)
        pl.semaphore_signal(barrier, inc=1, device_id=(b, t), device_id_type=MESH)
        return carry

    def greet_tm(k, carry):
        a = lax.rem(t + k, n_tm)
        pl.semaphore_signal(barrier, inc=1, device_id=(s, a), device_id_type=MESH)
        return carry

    lax.fori_loop(1, n_space, greet_space, 0)
    lax.fori_loop(1, n_tm, greet_tm, 0)
    pl.semaphore_wait(barrier, (n_space - 1) + (n_tm - 1))


def allreduce_body(n_space, n_tm, g_ref, out_ref, buf1, buf2, buf3, send1, recv1, send2, recv2, send3, recv3):
    s = lax.axis_index("space")
    t = lax.axis_index("tm")

    def space_copy(src, dst_buf, send, recv, k):
        b = lax.rem(s + k, n_space)
        return pltpu.make_async_remote_copy(
            src_ref=src(b), dst_ref=dst_buf.at[s], send_sem=send.at[k], recv_sem=recv.at[s],
            device_id=(b, t), device_id_type=MESH,
        )

    def space_wait(dst_buf, send, recv, k):
        j = lax.rem(s + k, n_space)
        pltpu.make_async_remote_copy(
            src_ref=dst_buf.at[j], dst_ref=dst_buf.at[j], send_sem=send.at[k], recv_sem=recv.at[j],
            device_id=(j, t), device_id_type=MESH,
        ).wait_recv()

    def send_p1(k, carry):
        space_copy(lambda b: g_ref.at[b], buf1, send1, recv1, k).start()
        return carry

    lax.fori_loop(1, n_space, send_p1, 0)
    buf1[s] = g_ref[s]

    def wait_p1(k, carry):
        space_wait(buf1, send1, recv1, k)
        return carry

    lax.fori_loop(1, n_space, wait_p1, 0)
    acc = buf1[0]
    for j in range(1, n_space):
        acc = acc + buf1[j]
    buf2[t] = acc

    copies = []
    for k in range(1, n_tm):
        a = lax.rem(t + k, n_tm)
        c = pltpu.make_async_remote_copy(
            src_ref=buf2.at[t], dst_ref=buf2.at[t], send_sem=send2.at[k], recv_sem=recv2.at[t],
            device_id=(s, a), device_id_type=MESH,
        )
        c.start()
        copies.append(c)
    for k in range(1, n_tm):
        j = lax.rem(t + k, n_tm)
        pltpu.make_async_remote_copy(
            src_ref=buf2.at[j], dst_ref=buf2.at[j], send_sem=send2.at[k], recv_sem=recv2.at[j],
            device_id=(s, j), device_id_type=MESH,
        ).wait_recv()
    for c in copies:
        c.wait_send()
    acc = buf2[0]
    for j in range(1, n_tm):
        acc = acc + buf2[j]
    buf3[s] = acc

    def send_p3(k, carry):
        space_copy(lambda b: buf3.at[s], buf3, send3, recv3, k).start()
        return carry

    lax.fori_loop(1, n_space, send_p3, 0)

    def wait_p3(k, carry):
        space_wait(buf3, send3, recv3, k)
        return carry

    lax.fori_loop(1, n_space, wait_p3, 0)

    def drain(k, carry):
        space_copy(lambda b: g_ref.at[b], buf1, send1, recv1, k).wait_send()
        space_copy(lambda b: buf3.at[s], buf3, send3, recv3, k).wait_send()
        return carry

    lax.fori_loop(1, n_space, drain, 0)
    out_ref[...] = buf3[...]


def a2a_body(n_tm, src_at, dst_at, x_ref, buf, send, recv, own):
    s = lax.axis_index("space")
    t = lax.axis_index("tm")
    copies = []
    for k in range(1, n_tm):
        a = lax.rem(t + k, n_tm)
        c = pltpu.make_async_remote_copy(
            src_ref=src_at(x_ref, a), dst_ref=dst_at(buf, t), send_sem=send.at[k], recv_sem=recv.at[t],
            device_id=(s, a), device_id_type=MESH,
        )
        c.start()
        copies.append(c)
    mine = pltpu.make_async_copy(src_at(x_ref, t), dst_at(buf, t), own.at[0])
    mine.start()
    mine.wait()
    for k in range(1, n_tm):
        j = lax.rem(t + k, n_tm)
        pltpu.make_async_remote_copy(
            src_ref=src_at(x_ref, j), dst_ref=dst_at(buf, j), send_sem=send.at[k], recv_sem=recv.at[j],
            device_id=(s, j), device_id_type=MESH,
        ).wait_recv()
    for c in copies:
        c.wait_send()


def front_kernel(n_space, n_tm, x_ref, cells_ref, g_out_ref, cells, gpart, buf1, buf2, buf3, *sems):
    send, recv, own = sems[:3]
    greet_all(n_space, n_tm)
    rows, _, cols = x_ref.shape
    width = cols // n_tm
    a2a_body(
        n_tm,
        lambda ref, a: ref.at[:, :, lanes(a, width)],
        lambda ref, j: ref.at[:, pl.ds(j * RANK, RANK), :],
        x_ref, cells, send, recv, own,
    )
    size = cells.shape[1]
    gram = jnp.zeros((size, size), jnp.float32)
    for x in range(rows):
        w = cells[x]
        gram = gram + lax.dot_general(
            w, w, (((1,), (1,)), ((), ())), preferred_element_type=jnp.float32
        )
    gpart[...] = gram.reshape(gpart.shape)
    allreduce_body(n_space, n_tm, gpart, g_out_ref, buf1, buf2, buf3, *sems[3:])
    cells_ref[...] = cells[...]


def front(vort_x):
    n_space = lax.axis_size("space")
    n_tm = lax.axis_size("tm")
    rows, _, cols = vort_x.shape
    size = n_tm * RANK
    cells_shape = (rows, size, cols // n_tm)
    chunks = (n_space, size // n_space, size)
    cells_x, gram = pl.pallas_call(
        functools.partial(front_kernel, n_space, n_tm),
        out_shape=(
            jax.ShapeDtypeStruct(cells_shape, vort_x.dtype),
            jax.ShapeDtypeStruct(chunks, jnp.float32),
        ),
        in_specs=[pl.BlockSpec(memory_space=pltpu.VMEM)],
        out_specs=(pl.BlockSpec(memory_space=pltpu.VMEM), pl.BlockSpec(memory_space=pltpu.VMEM)),
        scratch_shapes=[
            pltpu.VMEM(cells_shape, vort_x.dtype),
            pltpu.VMEM(chunks, jnp.float32),
            pltpu.VMEM(chunks, jnp.float32),
            pltpu.VMEM((n_tm,) + chunks[1:], jnp.float32),
            pltpu.VMEM(chunks, jnp.float32),
            pltpu.SemaphoreType.DMA((n_tm,)),
            pltpu.SemaphoreType.DMA((n_tm,)),
            pltpu.SemaphoreType.DMA((1,)),
            pltpu.SemaphoreType.DMA((n_space,)),
            pltpu.SemaphoreType.DMA((n_space,)),
            pltpu.SemaphoreType.DMA((n_tm,)),
            pltpu.SemaphoreType.DMA((n_tm,)),
            pltpu.SemaphoreType.DMA((n_space,)),
            pltpu.SemaphoreType.DMA((n_space,)),
        ],
        compiler_params=pltpu.CompilerParams(collective_id=0, has_side_effects=True),
    )(vort_x)
    return cells_x, gram.reshape(size, size)


def lanes(a, width):
    return pl.ds(pl.multiple_of(a * width, width), width)


def bdot(x, y):
    return jnp.einsum("nab,nbc->nac", x, y, precision=HIGH, preferred_element_type=jnp.float32)


def bdot_t(x, y):
    return jnp.einsum("nac,nbc->nab", x, y, precision=HIGH, preferred_element_type=jnp.float32)


def iotas(shape):
    return lax.broadcasted_iota(jnp.int32, shape, 1), lax.broadcasted_iota(jnp.int32, shape, 2)


def merge_coeffs(h):
    n = h.shape[0]
    kt = h[:, :RANK, :] + h[:, RANK:, :]
    row, col = iotas(h.shape)
    dcol = jnp.sum(jnp.where(row == col, h, 0.0), axis=2, keepdims=True)
    scales = jnp.sqrt(dcol[:, :RANK] + dcol[:, RANK:])
    inner = bdot_t(bdot(kt, h), kt)
    row, col = iotas(inner.shape)
    eye = jnp.where(row == col, 1.0, 0.0)

    a = inner
    r = eye * jnp.ones((n, 1, 1), jnp.float32)
    below = row[:, :, :1]
    for j in range(RANK):
        a_row = a[:, j : j + 1, :]
        r_row = r[:, j : j + 1, :]
        factor = jnp.where(below > j, a[:, :, j : j + 1] / a_row[:, :, j : j + 1], 0.0)
        a = a - factor * a_row
        r = r - factor * r_row
    diag_u = jnp.sum(jnp.where(row == col, a, 0.0), axis=2, keepdims=True)
    return bdot(r * (scales / jnp.sqrt(diag_u)), kt)


def place(x, offset, width):
    n, _, w = x.shape
    row, col = iotas((n, w, width))
    return bdot(x, jnp.where(col == row + offset, 1.0, 0.0))


def tree_levels(g_ref):
    size = 2 * RANK
    leaves = g_ref.shape[0] // RANK
    picks = []
    for k in range(leaves // 2):
        lane0 = (k * size) // 128 * 128
        block = g_ref[k * size : (k + 1) * size, lane0 : lane0 + 128][None]
        picks.append(place(block, -(k * size - lane0), size))
    basis = merge_coeffs(jnp.concatenate(picks, axis=0))
    while basis.shape[0] > 1:
        n = basis.shape[0] // 2
        w = basis.shape[2]
        pairs = basis.reshape(n, 2, RANK, w)
        bt = jnp.concatenate(
            [place(pairs[:, 0], 0, 2 * w), place(pairs[:, 1], w, 2 * w)], axis=1
        )
        gs = jnp.concatenate(
            [g_ref[k * 2 * w : (k + 1) * 2 * w, k * 2 * w : (k + 1) * 2 * w][None] for k in range(n)],
            axis=0,
        )
        h = bdot_t(bdot(bt, gs), bt)
        basis = bdot(merge_coeffs(h), bt)
    return basis[0]


def finish_kernel(n_tm, g_ref, w_ref, out_ref, part_ref, buf, send, recv, own):
    s = lax.axis_index("space")
    t = lax.axis_index("tm")
    barrier = pltpu.get_barrier_semaphore()
    for k in range(1, n_tm):
        a = lax.rem(t + k, n_tm)
        pl.semaphore_signal(barrier, inc=1, device_id=(s, a), device_id_type=MESH)
    basis_t = tree_levels(g_ref)
    for x in range(w_ref.shape[0]):
        part_ref[x] = jnp.dot(
            basis_t, w_ref[x].astype(jnp.float32), precision=HIGH, preferred_element_type=jnp.float32
        )
    share = part_ref.shape[1] // n_tm
    width = w_ref.shape[2]
    src_at = lambda a: part_ref.at[:, pl.ds(a * share, share), :]
    dst_at = lambda j: buf.at[:, :, lanes(j, width)]
    pl.semaphore_wait(barrier, n_tm - 1)
    copies = []
    for k in range(1, n_tm):
        a = lax.rem(t + k, n_tm)
        c = pltpu.make_async_remote_copy(
            src_ref=src_at(a), dst_ref=dst_at(t), send_sem=send.at[k], recv_sem=recv.at[t],
            device_id=(s, a), device_id_type=MESH,
        )
        c.start()
        copies.append(c)
    mine = pltpu.make_async_copy(src_at(t), dst_at(t), own.at[0])
    mine.start()
    mine.wait()
    for k in range(1, n_tm):
        j = lax.rem(t + k, n_tm)
        pltpu.make_async_remote_copy(
            src_ref=src_at(j), dst_ref=dst_at(j), send_sem=send.at[k], recv_sem=recv.at[j],
            device_id=(s, j), device_id_type=MESH,
        ).wait_recv()
    for c in copies:
        c.wait_send()
    out_ref[...] = buf[...]


def finish(gram, cells_x):
    n_tm = lax.axis_size("tm")
    rows, _, width = cells_x.shape
    share = RANK // n_tm
    out_shape = (rows, share, width * n_tm)
    return pl.pallas_call(
        functools.partial(finish_kernel, n_tm),
        out_shape=jax.ShapeDtypeStruct(out_shape, jnp.float32),
        in_specs=[pl.BlockSpec(memory_space=pltpu.VMEM)] * 2,
        out_specs=pl.BlockSpec(memory_space=pltpu.VMEM),
        scratch_shapes=[
            pltpu.VMEM((rows, RANK, width), jnp.float32),
            pltpu.VMEM(out_shape, jnp.float32),
            pltpu.SemaphoreType.DMA((n_tm,)),
            pltpu.SemaphoreType.DMA((n_tm,)),
            pltpu.SemaphoreType.DMA((1,)),
        ],
        compiler_params=pltpu.CompilerParams(collective_id=2, has_side_effects=True),
    )(gram, cells_x)


def local(velocity):
    rows = velocity.shape[2]
    span_v = halo_rows(velocity[:, 1], 2).astype(jnp.float32)
    stream_u = velocity[:, 0].astype(jnp.float32)
    dv_dx = (
        8.0 * (span_v[:, 3 : rows + 3] - span_v[:, 1 : rows + 1])
        - (span_v[:, 4:] - span_v[:, :rows])
    ) / 12.0
    vorticity = (dv_dx - spanwise(stream_u)).astype(jnp.bfloat16)
    blocks = lax.axis_size("tm")
    cols = vorticity.shape[2]
    width = cols // blocks
    vort_x = jnp.swapaxes(vorticity, 0, 1)
    cells_x, gram = front(vort_x)
    modes = jnp.swapaxes(finish(gram, cells_x), 0, 1)
    return (vorticity, modes)


def solution(mesh):
    in_specs = (P("tm", None, "space", None),)
    out_specs = (P("tm", "space", None), P("tm", "space", None))
    return jax.shard_map(local, mesh=mesh, in_specs=in_specs, out_specs=out_specs, check_vma=False)
```

```python
import functools

import jax
import jax.numpy as jnp
from jax import lax
from jax.experimental import pallas as pl
from jax.experimental.pallas import tpu as pltpu
from jax.sharding import PartitionSpec as P

RANK = 32
HIGH = lax.Precision.HIGHEST


def halo_rows(block, width):
    count = lax.axis_size("space")
    forward = [(i, (i + 1) % count) for i in range(count)]
    backward = [(target, source) for source, target in forward]
    rows = block.shape[1]
    low = lax.ppermute(block[:, rows - width :], "space", forward)
    high = lax.ppermute(block[:, :width], "space", backward)
    return jnp.concatenate([low, block, high], axis=1)


def spanwise(field):
    ahead = jnp.roll(field, -1, 2)
    behind = jnp.roll(field, 1, 2)
    ahead_two = jnp.roll(field, -2, 2)
    behind_two = jnp.roll(field, 2, 2)
    return (8.0 * (ahead - behind) - (ahead_two - behind_two)) / 12.0


MESH = pl.DeviceIdType.MESH


def greet_all(n_space, n_tm):
    s = lax.axis_index("space")
    t = lax.axis_index("tm")
    barrier = pltpu.get_barrier_semaphore()

    def greet_space(k, carry):
        b = lax.rem(s + k, n_space)
        pl.semaphore_signal(barrier, inc=1, device_id=(b, t), device_id_type=MESH)
        return carry

    def greet_tm(k, carry):
        a = lax.rem(t + k, n_tm)
        pl.semaphore_signal(barrier, inc=1, device_id=(s, a), device_id_type=MESH)
        return carry

    lax.fori_loop(1, n_space, greet_space, 0)
    lax.fori_loop(1, n_tm, greet_tm, 0)
    pl.semaphore_wait(barrier, (n_space - 1) + (n_tm - 1))


def allreduce_body(n_space, n_tm, g_ref, out_ref, buf1, buf2, buf3, send1, recv1, send2, recv2, send3, recv3):
    s = lax.axis_index("space")
    t = lax.axis_index("tm")

    def space_copy(src, dst_buf, send, recv, k):
        b = lax.rem(s + k, n_space)
        return pltpu.make_async_remote_copy(
            src_ref=src(b), dst_ref=dst_buf.at[s], send_sem=send.at[k], recv_sem=recv.at[s],
            device_id=(b, t), device_id_type=MESH,
        )

    def space_wait(dst_buf, send, recv, k):
        j = lax.rem(s + k, n_space)
        pltpu.make_async_remote_copy(
            src_ref=dst_buf.at[j], dst_ref=dst_buf.at[j], send_sem=send.at[k], recv_sem=recv.at[j],
            device_id=(j, t), device_id_type=MESH,
        ).wait_recv()

    def send_p1(k, carry):
        space_copy(lambda b: g_ref.at[b], buf1, send1, recv1, k).start()
        return carry

    lax.fori_loop(1, n_space, send_p1, 0)
    buf1[s] = g_ref[s]

    def wait_p1(k, carry):
        space_wait(buf1, send1, recv1, k)
        return carry

    lax.fori_loop(1, n_space, wait_p1, 0)
    acc = buf1[0]
    for j in range(1, n_space):
        acc = acc + buf1[j]
    buf2[t] = acc

    copies = []
    for k in range(1, n_tm):
        a = lax.rem(t + k, n_tm)
        c = pltpu.make_async_remote_copy(
            src_ref=buf2.at[t], dst_ref=buf2.at[t], send_sem=send2.at[k], recv_sem=recv2.at[t],
            device_id=(s, a), device_id_type=MESH,
        )
        c.start()
        copies.append(c)
    for k in range(1, n_tm):
        j = lax.rem(t + k, n_tm)
        pltpu.make_async_remote_copy(
            src_ref=buf2.at[j], dst_ref=buf2.at[j], send_sem=send2.at[k], recv_sem=recv2.at[j],
            device_id=(s, j), device_id_type=MESH,
        ).wait_recv()
    for c in copies:
        c.wait_send()
    acc = buf2[0]
    for j in range(1, n_tm):
        acc = acc + buf2[j]
    buf3[s] = acc

    def send_p3(k, carry):
        space_copy(lambda b: buf3.at[s], buf3, send3, recv3, k).start()
        return carry

    lax.fori_loop(1, n_space, send_p3, 0)

    def wait_p3(k, carry):
        space_wait(buf3, send3, recv3, k)
        return carry

    lax.fori_loop(1, n_space, wait_p3, 0)

    def drain(k, carry):
        space_copy(lambda b: g_ref.at[b], buf1, send1, recv1, k).wait_send()
        space_copy(lambda b: buf3.at[s], buf3, send3, recv3, k).wait_send()
        return carry

    lax.fori_loop(1, n_space, drain, 0)
    out_ref[...] = buf3[...]


def a2a_body(n_tm, src_at, dst_at, x_ref, buf, send, recv, own):
    s = lax.axis_index("space")
    t = lax.axis_index("tm")
    copies = []
    for k in range(1, n_tm):
        a = lax.rem(t + k, n_tm)
        c = pltpu.make_async_remote_copy(
            src_ref=src_at(x_ref, a), dst_ref=dst_at(buf, t), send_sem=send.at[k], recv_sem=recv.at[t],
            device_id=(s, a), device_id_type=MESH,
        )
        c.start()
        copies.append(c)
    mine = pltpu.make_async_copy(src_at(x_ref, t), dst_at(buf, t), own.at[0])
    mine.start()
    mine.wait()
    for k in range(1, n_tm):
        j = lax.rem(t + k, n_tm)
        pltpu.make_async_remote_copy(
            src_ref=src_at(x_ref, j), dst_ref=dst_at(buf, j), send_sem=send.at[k], recv_sem=recv.at[j],
            device_id=(s, j), device_id_type=MESH,
        ).wait_recv()
    for c in copies:
        c.wait_send()


def front_kernel(n_space, n_tm, x_ref, cells_ref, g_out_ref, cells, gpart, buf1, buf2, buf3, *sems):
    send, recv, own = sems[:3]
    greet_all(n_space, n_tm)
    rows, _, cols = x_ref.shape
    width = cols // n_tm
    a2a_body(
        n_tm,
        lambda ref, a: ref.at[:, :, lanes(a, width)],
        lambda ref, j: ref.at[:, pl.ds(j * RANK, RANK), :],
        x_ref, cells, send, recv, own,
    )
    size = cells.shape[1]
    gram = jnp.zeros((size, size), jnp.float32)
    for x in range(rows):
        w = cells[x]
        gram = gram + lax.dot_general(
            w, w, (((1,), (1,)), ((), ())), preferred_element_type=jnp.float32
        )
    gpart[...] = gram.reshape(gpart.shape)
    allreduce_body(n_space, n_tm, gpart, g_out_ref, buf1, buf2, buf3, *sems[3:])
    cells_ref[...] = cells[...]


def front(vort_x):
    n_space = lax.axis_size("space")
    n_tm = lax.axis_size("tm")
    rows, _, cols = vort_x.shape
    size = n_tm * RANK
    cells_shape = (rows, size, cols // n_tm)
    chunks = (n_space, size // n_space, size)
    cells_x, gram = pl.pallas_call(
        functools.partial(front_kernel, n_space, n_tm),
        out_shape=(
            jax.ShapeDtypeStruct(cells_shape, vort_x.dtype),
            jax.ShapeDtypeStruct(chunks, jnp.float32),
        ),
        in_specs=[pl.BlockSpec(memory_space=pltpu.VMEM)],
        out_specs=(pl.BlockSpec(memory_space=pltpu.VMEM), pl.BlockSpec(memory_space=pltpu.VMEM)),
        scratch_shapes=[
            pltpu.VMEM(cells_shape, vort_x.dtype),
            pltpu.VMEM(chunks, jnp.float32),
            pltpu.VMEM(chunks, jnp.float32),
            pltpu.VMEM((n_tm,) + chunks[1:], jnp.float32),
            pltpu.VMEM(chunks, jnp.float32),
            pltpu.SemaphoreType.DMA((n_tm,)),
            pltpu.SemaphoreType.DMA((n_tm,)),
            pltpu.SemaphoreType.DMA((1,)),
            pltpu.SemaphoreType.DMA((n_space,)),
            pltpu.SemaphoreType.DMA((n_space,)),
            pltpu.SemaphoreType.DMA((n_tm,)),
            pltpu.SemaphoreType.DMA((n_tm,)),
            pltpu.SemaphoreType.DMA((n_space,)),
            pltpu.SemaphoreType.DMA((n_space,)),
        ],
        compiler_params=pltpu.CompilerParams(collective_id=0, has_side_effects=True),
    )(vort_x)
    return cells_x, gram.reshape(size, size)


def lanes(a, width):
    return pl.ds(pl.multiple_of(a * width, width), width)


def bdot(x, y):
    return jnp.einsum("nab,nbc->nac", x, y, precision=HIGH, preferred_element_type=jnp.float32)


def bdot_t(x, y):
    return jnp.einsum("nac,nbc->nab", x, y, precision=HIGH, preferred_element_type=jnp.float32)


def iotas(shape):
    return lax.broadcasted_iota(jnp.int32, shape, 1), lax.broadcasted_iota(jnp.int32, shape, 2)


def merge_coeffs(h):
    n = h.shape[0]
    kt = h[:, :RANK, :] + h[:, RANK:, :]
    row, col = iotas(h.shape)
    dcol = jnp.sum(jnp.where(row == col, h, 0.0), axis=2, keepdims=True)
    scales = jnp.sqrt(dcol[:, :RANK] + dcol[:, RANK:])
    inner = bdot_t(bdot(kt, h), kt)
    row, col = iotas(inner.shape)

    a = inner
    r = kt
    below = row[:, :, :1]
    for j in range(RANK):
        a_row = a[:, j : j + 1, :]
        r_row = r[:, j : j + 1, :]
        factor = jnp.where(below > j, a[:, :, j : j + 1] / a_row[:, :, j : j + 1], 0.0)
        a = a - factor * a_row
        r = r - factor * r_row
    diag_u = jnp.sum(jnp.where(row == col, a, 0.0), axis=2, keepdims=True)
    return r * (scales / jnp.sqrt(diag_u))


def place(x, offset, width):
    n, _, w = x.shape
    row, col = iotas((n, w, width))
    return bdot(x, jnp.where(col == row + offset, 1.0, 0.0))


def tree_levels(g_ref):
    size = 2 * RANK
    leaves = g_ref.shape[0] // RANK
    picks = []
    for k in range(leaves // 2):
        lane0 = (k * size) // 128 * 128
        block = g_ref[k * size : (k + 1) * size, lane0 : lane0 + 128][None]
        picks.append(place(block, -(k * size - lane0), size))
    basis = merge_coeffs(jnp.concatenate(picks, axis=0))
    while basis.shape[0] > 1:
        n = basis.shape[0] // 2
        w = basis.shape[2]
        pairs = basis.reshape(n, 2, RANK, w)
        bt = jnp.concatenate(
            [place(pairs[:, 0], 0, 2 * w), place(pairs[:, 1], w, 2 * w)], axis=1
        )
        gs = jnp.concatenate(
            [g_ref[k * 2 * w : (k + 1) * 2 * w, k * 2 * w : (k + 1) * 2 * w][None] for k in range(n)],
            axis=0,
        )
        h = bdot_t(bdot(bt, gs), bt)
        basis = bdot(merge_coeffs(h), bt)
    return basis[0]


def finish_kernel(n_tm, g_ref, w_ref, out_ref, part_ref, buf, send, recv, own):
    s = lax.axis_index("space")
    t = lax.axis_index("tm")
    barrier = pltpu.get_barrier_semaphore()
    for k in range(1, n_tm):
        a = lax.rem(t + k, n_tm)
        pl.semaphore_signal(barrier, inc=1, device_id=(s, a), device_id_type=MESH)
    basis_t = tree_levels(g_ref)
    for x in range(w_ref.shape[0]):
        part_ref[x] = jnp.dot(
            basis_t, w_ref[x].astype(jnp.float32), precision=HIGH, preferred_element_type=jnp.float32
        )
    share = part_ref.shape[1] // n_tm
    width = w_ref.shape[2]
    src_at = lambda a: part_ref.at[:, pl.ds(a * share, share), :]
    dst_at = lambda j: buf.at[:, :, lanes(j, width)]
    pl.semaphore_wait(barrier, n_tm - 1)
    copies = []
    for k in range(1, n_tm):
        a = lax.rem(t + k, n_tm)
        c = pltpu.make_async_remote_copy(
            src_ref=src_at(a), dst_ref=dst_at(t), send_sem=send.at[k], recv_sem=recv.at[t],
            device_id=(s, a), device_id_type=MESH,
        )
        c.start()
        copies.append(c)
    mine = pltpu.make_async_copy(src_at(t), dst_at(t), own.at[0])
    mine.start()
    mine.wait()
    for k in range(1, n_tm):
        j = lax.rem(t + k, n_tm)
        pltpu.make_async_remote_copy(
            src_ref=src_at(j), dst_ref=dst_at(j), send_sem=send.at[k], recv_sem=recv.at[j],
            device_id=(s, j), device_id_type=MESH,
        ).wait_recv()
    for c in copies:
        c.wait_send()
    out_ref[...] = buf[...]


def finish(gram, cells_x):
    n_tm = lax.axis_size("tm")
    rows, _, width = cells_x.shape
    share = RANK // n_tm
    out_shape = (rows, share, width * n_tm)
    return pl.pallas_call(
        functools.partial(finish_kernel, n_tm),
        out_shape=jax.ShapeDtypeStruct(out_shape, jnp.float32),
        in_specs=[pl.BlockSpec(memory_space=pltpu.VMEM)] * 2,
        out_specs=pl.BlockSpec(memory_space=pltpu.VMEM),
        scratch_shapes=[
            pltpu.VMEM((rows, RANK, width), jnp.float32),
            pltpu.VMEM(out_shape, jnp.float32),
            pltpu.SemaphoreType.DMA((n_tm,)),
            pltpu.SemaphoreType.DMA((n_tm,)),
            pltpu.SemaphoreType.DMA((1,)),
        ],
        compiler_params=pltpu.CompilerParams(collective_id=2, has_side_effects=True),
    )(gram, cells_x)


def local(velocity):
    rows = velocity.shape[2]
    span_v = halo_rows(velocity[:, 1], 2).astype(jnp.float32)
    stream_u = velocity[:, 0].astype(jnp.float32)
    dv_dx = (
        8.0 * (span_v[:, 3 : rows + 3] - span_v[:, 1 : rows + 1])
        - (span_v[:, 4:] - span_v[:, :rows])
    ) / 12.0
    vorticity = (dv_dx - spanwise(stream_u)).astype(jnp.bfloat16)
    blocks = lax.axis_size("tm")
    cols = vorticity.shape[2]
    width = cols // blocks
    vort_x = jnp.swapaxes(vorticity, 0, 1)
    cells_x, gram = front(vort_x)
    modes = jnp.swapaxes(finish(gram, cells_x), 0, 1)
    return (vorticity, modes)


def solution(mesh):
    in_specs = (P("tm", None, "space", None),)
    out_specs = (P("tm", "space", None), P("tm", "space", None))
    return jax.shard_map(local, mesh=mesh, in_specs=in_specs, out_specs=out_specs, check_vma=False)
```

```python
import functools

import jax
import jax.numpy as jnp
from jax import lax
from jax.experimental import pallas as pl
from jax.experimental.pallas import tpu as pltpu
from jax.sharding import PartitionSpec as P

RANK = 32
HIGH = lax.Precision.HIGHEST


def halo_rows(block, width):
    count = lax.axis_size("space")
    forward = [(i, (i + 1) % count) for i in range(count)]
    backward = [(target, source) for source, target in forward]
    rows = block.shape[1]
    low = lax.ppermute(block[:, rows - width :], "space", forward)
    high = lax.ppermute(block[:, :width], "space", backward)
    return jnp.concatenate([low, block, high], axis=1)


def spanwise(field):
    ahead = jnp.roll(field, -1, 2)
    behind = jnp.roll(field, 1, 2)
    ahead_two = jnp.roll(field, -2, 2)
    behind_two = jnp.roll(field, 2, 2)
    return (8.0 * (ahead - behind) - (ahead_two - behind_two)) / 12.0


MESH = pl.DeviceIdType.MESH


def greet_all(n_space, n_tm):
    s = lax.axis_index("space")
    t = lax.axis_index("tm")
    barrier = pltpu.get_barrier_semaphore()

    def greet_space(k, carry):
        b = lax.rem(s + k, n_space)
        pl.semaphore_signal(barrier, inc=1, device_id=(b, t), device_id_type=MESH)
        return carry

    def greet_tm(k, carry):
        a = lax.rem(t + k, n_tm)
        pl.semaphore_signal(barrier, inc=1, device_id=(s, a), device_id_type=MESH)
        return carry

    lax.fori_loop(1, n_space, greet_space, 0)
    lax.fori_loop(1, n_tm, greet_tm, 0)
    pl.semaphore_wait(barrier, (n_space - 1) + (n_tm - 1))


def allreduce_body(n_space, n_tm, g_ref, out_ref, buf1, buf2, buf3, send1, recv1, send2, recv2, send3, recv3):
    s = lax.axis_index("space")
    t = lax.axis_index("tm")

    def space_copy(src, dst_buf, send, recv, k):
        b = lax.rem(s + k, n_space)
        return pltpu.make_async_remote_copy(
            src_ref=src(b), dst_ref=dst_buf.at[s], send_sem=send.at[k], recv_sem=recv.at[s],
            device_id=(b, t), device_id_type=MESH,
        )

    def space_wait(dst_buf, send, recv, k):
        j = lax.rem(s + k, n_space)
        pltpu.make_async_remote_copy(
            src_ref=dst_buf.at[j], dst_ref=dst_buf.at[j], send_sem=send.at[k], recv_sem=recv.at[j],
            device_id=(j, t), device_id_type=MESH,
        ).wait_recv()

    def send_p1(k, carry):
        space_copy(lambda b: g_ref.at[b], buf1, send1, recv1, k).start()
        return carry

    lax.fori_loop(1, n_space, send_p1, 0)
    buf1[s] = g_ref[s]

    def wait_p1(k, carry):
        space_wait(buf1, send1, recv1, k)
        return carry

    lax.fori_loop(1, n_space, wait_p1, 0)
    acc = buf1[0]
    for j in range(1, n_space):
        acc = acc + buf1[j]
    buf2[t] = acc

    copies = []
    for k in range(1, n_tm):
        a = lax.rem(t + k, n_tm)
        c = pltpu.make_async_remote_copy(
            src_ref=buf2.at[t], dst_ref=buf2.at[t], send_sem=send2.at[k], recv_sem=recv2.at[t],
            device_id=(s, a), device_id_type=MESH,
        )
        c.start()
        copies.append(c)
    for k in range(1, n_tm):
        j = lax.rem(t + k, n_tm)
        pltpu.make_async_remote_copy(
            src_ref=buf2.at[j], dst_ref=buf2.at[j], send_sem=send2.at[k], recv_sem=recv2.at[j],
            device_id=(s, j), device_id_type=MESH,
        ).wait_recv()
    for c in copies:
        c.wait_send()
    acc = buf2[0]
    for j in range(1, n_tm):
        acc = acc + buf2[j]
    buf3[s] = acc

    def send_p3(k, carry):
        space_copy(lambda b: buf3.at[s], buf3, send3, recv3, k).start()
        return carry

    lax.fori_loop(1, n_space, send_p3, 0)

    def wait_p3(k, carry):
        space_wait(buf3, send3, recv3, k)
        return carry

    lax.fori_loop(1, n_space, wait_p3, 0)

    def drain(k, carry):
        space_copy(lambda b: g_ref.at[b], buf1, send1, recv1, k).wait_send()
        space_copy(lambda b: buf3.at[s], buf3, send3, recv3, k).wait_send()
        return carry

    lax.fori_loop(1, n_space, drain, 0)
    out_ref[...] = buf3[...]


def a2a_body(n_tm, src_at, dst_at, x_ref, buf, send, recv, own):
    s = lax.axis_index("space")
    t = lax.axis_index("tm")
    copies = []
    for k in range(1, n_tm):
        a = lax.rem(t + k, n_tm)
        c = pltpu.make_async_remote_copy(
            src_ref=src_at(x_ref, a), dst_ref=dst_at(buf, t), send_sem=send.at[k], recv_sem=recv.at[t],
            device_id=(s, a), device_id_type=MESH,
        )
        c.start()
        copies.append(c)
    mine = pltpu.make_async_copy(src_at(x_ref, t), dst_at(buf, t), own.at[0])
    mine.start()
    mine.wait()
    for k in range(1, n_tm):
        j = lax.rem(t + k, n_tm)
        pltpu.make_async_remote_copy(
            src_ref=src_at(x_ref, j), dst_ref=dst_at(buf, j), send_sem=send.at[k], recv_sem=recv.at[j],
            device_id=(s, j), device_id_type=MESH,
        ).wait_recv()
    for c in copies:
        c.wait_send()


def front_kernel(n_space, n_tm, x_ref, cells_ref, g_out_ref, cells, gpart, buf1, buf2, buf3, *sems):
    send, recv, own = sems[:3]
    greet_all(n_space, n_tm)
    rows, _, cols = x_ref.shape
    width = cols // n_tm
    a2a_body(
        n_tm,
        lambda ref, a: ref.at[:, :, lanes(a, width)],
        lambda ref, j: ref.at[:, pl.ds(j * RANK, RANK), :],
        x_ref, cells, send, recv, own,
    )
    size = cells.shape[1]
    gram = jnp.zeros((size, size), jnp.float32)
    for x in range(rows):
        w = cells[x]
        gram = gram + lax.dot_general(
            w, w, (((1,), (1,)), ((), ())), preferred_element_type=jnp.float32
        )
    gpart[...] = gram.reshape(gpart.shape)
    allreduce_body(n_space, n_tm, gpart, g_out_ref, buf1, buf2, buf3, *sems[3:])
    cells_ref[...] = cells[...]


def front(vort_x):
    n_space = lax.axis_size("space")
    n_tm = lax.axis_size("tm")
    rows, _, cols = vort_x.shape
    size = n_tm * RANK
    cells_shape = (rows, size, cols // n_tm)
    chunks = (n_space, size // n_space, size)
    cells_x, gram = pl.pallas_call(
        functools.partial(front_kernel, n_space, n_tm),
        out_shape=(
            jax.ShapeDtypeStruct(cells_shape, vort_x.dtype),
            jax.ShapeDtypeStruct(chunks, jnp.float32),
        ),
        in_specs=[pl.BlockSpec(memory_space=pltpu.VMEM)],
        out_specs=(pl.BlockSpec(memory_space=pltpu.VMEM), pl.BlockSpec(memory_space=pltpu.VMEM)),
        scratch_shapes=[
            pltpu.VMEM(cells_shape, vort_x.dtype),
            pltpu.VMEM(chunks, jnp.float32),
            pltpu.VMEM(chunks, jnp.float32),
            pltpu.VMEM((n_tm,) + chunks[1:], jnp.float32),
            pltpu.VMEM(chunks, jnp.float32),
            pltpu.SemaphoreType.DMA((n_tm,)),
            pltpu.SemaphoreType.DMA((n_tm,)),
            pltpu.SemaphoreType.DMA((1,)),
            pltpu.SemaphoreType.DMA((n_space,)),
            pltpu.SemaphoreType.DMA((n_space,)),
            pltpu.SemaphoreType.DMA((n_tm,)),
            pltpu.SemaphoreType.DMA((n_tm,)),
            pltpu.SemaphoreType.DMA((n_space,)),
            pltpu.SemaphoreType.DMA((n_space,)),
        ],
        compiler_params=pltpu.CompilerParams(collective_id=0, has_side_effects=True),
    )(vort_x)
    return cells_x, gram.reshape(size, size)


def lanes(a, width):
    return pl.ds(pl.multiple_of(a * width, width), width)


def bdot(x, y):
    return jnp.einsum("nab,nbc->nac", x, y, precision=HIGH, preferred_element_type=jnp.float32)


def bdot_t(x, y):
    return jnp.einsum("nac,nbc->nab", x, y, precision=HIGH, preferred_element_type=jnp.float32)


def iotas(shape):
    return lax.broadcasted_iota(jnp.int32, shape, 1), lax.broadcasted_iota(jnp.int32, shape, 2)


def merge_coeffs(h):
    n = h.shape[0]
    kt = h[:, :RANK, :] + h[:, RANK:, :]
    row, col = iotas(h.shape)
    dcol = jnp.sum(jnp.where(row == col, h, 0.0), axis=2, keepdims=True)
    scales = jnp.sqrt(dcol[:, :RANK] + dcol[:, RANK:])
    inner = bdot_t(bdot(kt, h), kt)
    row, col = iotas(inner.shape)

    a = inner
    r = kt
    below = row[:, :, :1]
    for j in range(RANK):
        a_row = a[:, j : j + 1, :]
        r_row = r[:, j : j + 1, :]
        factor = jnp.where(below > j, a[:, :, j : j + 1] / a_row[:, :, j : j + 1], 0.0)
        a = a - factor * a_row
        r = r - factor * r_row
    diag_u = jnp.sum(jnp.where(row == col, a, 0.0), axis=2, keepdims=True)
    return r * (scales / jnp.sqrt(diag_u))


def place(x, offset, width):
    n, _, w = x.shape
    row, col = iotas((n, w, width))
    return bdot(x, jnp.where(col == row + offset, 1.0, 0.0))


def tree_levels(g_ref):
    size = 2 * RANK
    leaves = g_ref.shape[0] // RANK
    picks = []
    for k in range(leaves // 2):
        lane0 = (k * size) // 128 * 128
        block = g_ref[k * size : (k + 1) * size, lane0 : lane0 + 128][None]
        picks.append(place(block, -(k * size - lane0), size))
    basis = merge_coeffs(jnp.concatenate(picks, axis=0))
    while basis.shape[0] > 1:
        n = basis.shape[0] // 2
        w = basis.shape[2]
        pairs = basis.reshape(n, 2, RANK, w)
        bt = jnp.concatenate(
            [place(pairs[:, 0], 0, 2 * w), place(pairs[:, 1], w, 2 * w)], axis=1
        )
        gs = jnp.concatenate(
            [g_ref[k * 2 * w : (k + 1) * 2 * w, k * 2 * w : (k + 1) * 2 * w][None] for k in range(n)],
            axis=0,
        )
        h = bdot_t(bdot(bt, gs), bt)
        basis = bdot(merge_coeffs(h), bt)
    return basis[0]


def finish_kernel(n_tm, g_ref, w_ref, out_ref, part_ref, buf, send, recv, own):
    s = lax.axis_index("space")
    t = lax.axis_index("tm")
    barrier = pltpu.get_barrier_semaphore()
    for k in range(1, n_tm):
        a = lax.rem(t + k, n_tm)
        pl.semaphore_signal(barrier, inc=1, device_id=(s, a), device_id_type=MESH)
    basis_t = tree_levels(g_ref)
    hi = basis_t.astype(jnp.bfloat16)
    rest = basis_t - hi.astype(jnp.float32)
    mid = rest.astype(jnp.bfloat16)
    lo = (rest - mid.astype(jnp.float32)).astype(jnp.bfloat16)
    pieces = jnp.concatenate([hi, mid, lo], axis=0)
    for x in range(w_ref.shape[0]):
        terms = jnp.dot(pieces, w_ref[x], preferred_element_type=jnp.float32)
        part_ref[x] = (terms[:RANK] + terms[RANK : 2 * RANK]) + terms[2 * RANK :]
    share = part_ref.shape[1] // n_tm
    width = w_ref.shape[2]
    src_at = lambda a: part_ref.at[:, pl.ds(a * share, share), :]
    dst_at = lambda j: buf.at[:, :, lanes(j, width)]
    pl.semaphore_wait(barrier, n_tm - 1)
    copies = []
    for k in range(1, n_tm):
        a = lax.rem(t + k, n_tm)
        c = pltpu.make_async_remote_copy(
            src_ref=src_at(a), dst_ref=dst_at(t), send_sem=send.at[k], recv_sem=recv.at[t],
            device_id=(s, a), device_id_type=MESH,
        )
        c.start()
        copies.append(c)
    mine = pltpu.make_async_copy(src_at(t), dst_at(t), own.at[0])
    mine.start()
    mine.wait()
    for k in range(1, n_tm):
        j = lax.rem(t + k, n_tm)
        pltpu.make_async_remote_copy(
            src_ref=src_at(j), dst_ref=dst_at(j), send_sem=send.at[k], recv_sem=recv.at[j],
            device_id=(s, j), device_id_type=MESH,
        ).wait_recv()
    for c in copies:
        c.wait_send()
    out_ref[...] = buf[...]


def finish(gram, cells_x):
    n_tm = lax.axis_size("tm")
    rows, _, width = cells_x.shape
    share = RANK // n_tm
    out_shape = (rows, share, width * n_tm)
    return pl.pallas_call(
        functools.partial(finish_kernel, n_tm),
        out_shape=jax.ShapeDtypeStruct(out_shape, jnp.float32),
        in_specs=[pl.BlockSpec(memory_space=pltpu.VMEM)] * 2,
        out_specs=pl.BlockSpec(memory_space=pltpu.VMEM),
        scratch_shapes=[
            pltpu.VMEM((rows, RANK, width), jnp.float32),
            pltpu.VMEM(out_shape, jnp.float32),
            pltpu.SemaphoreType.DMA((n_tm,)),
            pltpu.SemaphoreType.DMA((n_tm,)),
            pltpu.SemaphoreType.DMA((1,)),
        ],
        compiler_params=pltpu.CompilerParams(collective_id=2, has_side_effects=True),
    )(gram, cells_x)


def local(velocity):
    rows = velocity.shape[2]
    span_v = halo_rows(velocity[:, 1], 2).astype(jnp.float32)
    stream_u = velocity[:, 0].astype(jnp.float32)
    dv_dx = (
        8.0 * (span_v[:, 3 : rows + 3] - span_v[:, 1 : rows + 1])
        - (span_v[:, 4:] - span_v[:, :rows])
    ) / 12.0
    vorticity = (dv_dx - spanwise(stream_u)).astype(jnp.bfloat16)
    blocks = lax.axis_size("tm")
    cols = vorticity.shape[2]
    width = cols // blocks
    vort_x = jnp.swapaxes(vorticity, 0, 1)
    cells_x, gram = front(vort_x)
    modes = jnp.swapaxes(finish(gram, cells_x), 0, 1)
    return (vorticity, modes)


def solution(mesh):
    in_specs = (P("tm", None, "space", None),)
    out_specs = (P("tm", "space", None), P("tm", "space", None))
    return jax.shard_map(local, mesh=mesh, in_specs=in_specs, out_specs=out_specs, check_vma=False)
```

```python
import functools

import jax
import jax.numpy as jnp
from jax import lax
from jax.experimental import pallas as pl
from jax.experimental.pallas import tpu as pltpu
from jax.sharding import PartitionSpec as P

RANK = 32
HIGH = lax.Precision.HIGHEST


def halo_rows(block, width):
    count = lax.axis_size("space")
    forward = [(i, (i + 1) % count) for i in range(count)]
    backward = [(target, source) for source, target in forward]
    rows = block.shape[1]
    low = lax.ppermute(block[:, rows - width :], "space", forward)
    high = lax.ppermute(block[:, :width], "space", backward)
    return jnp.concatenate([low, block, high], axis=1)


MESH = pl.DeviceIdType.MESH


def greet_all(n_space, n_tm):
    s = lax.axis_index("space")
    t = lax.axis_index("tm")
    barrier = pltpu.get_barrier_semaphore()

    def greet_space(k, carry):
        b = lax.rem(s + k, n_space)
        pl.semaphore_signal(barrier, inc=1, device_id=(b, t), device_id_type=MESH)
        return carry

    def greet_tm(k, carry):
        a = lax.rem(t + k, n_tm)
        pl.semaphore_signal(barrier, inc=1, device_id=(s, a), device_id_type=MESH)
        return carry

    lax.fori_loop(1, n_space, greet_space, 0)
    lax.fori_loop(1, n_tm, greet_tm, 0)
    pl.semaphore_wait(barrier, (n_space - 1) + (n_tm - 1))


def allreduce_body(n_space, n_tm, g_ref, out_ref, buf1, buf2, buf3, send1, recv1, send2, recv2, send3, recv3):
    s = lax.axis_index("space")
    t = lax.axis_index("tm")

    def space_copy(src, dst_buf, send, recv, k):
        b = lax.rem(s + k, n_space)
        return pltpu.make_async_remote_copy(
            src_ref=src(b), dst_ref=dst_buf.at[s], send_sem=send.at[k], recv_sem=recv.at[s],
            device_id=(b, t), device_id_type=MESH,
        )

    def space_wait(dst_buf, send, recv, k):
        j = lax.rem(s + k, n_space)
        pltpu.make_async_remote_copy(
            src_ref=dst_buf.at[j], dst_ref=dst_buf.at[j], send_sem=send.at[k], recv_sem=recv.at[j],
            device_id=(j, t), device_id_type=MESH,
        ).wait_recv()

    def send_p1(k, carry):
        space_copy(lambda b: g_ref.at[b], buf1, send1, recv1, k).start()
        return carry

    lax.fori_loop(1, n_space, send_p1, 0)
    buf1[s] = g_ref[s]

    def wait_p1(k, carry):
        space_wait(buf1, send1, recv1, k)
        return carry

    lax.fori_loop(1, n_space, wait_p1, 0)
    acc = buf1[0]
    for j in range(1, n_space):
        acc = acc + buf1[j]
    buf2[t] = acc

    copies = []
    for k in range(1, n_tm):
        a = lax.rem(t + k, n_tm)
        c = pltpu.make_async_remote_copy(
            src_ref=buf2.at[t], dst_ref=buf2.at[t], send_sem=send2.at[k], recv_sem=recv2.at[t],
            device_id=(s, a), device_id_type=MESH,
        )
        c.start()
        copies.append(c)
    for k in range(1, n_tm):
        j = lax.rem(t + k, n_tm)
        pltpu.make_async_remote_copy(
            src_ref=buf2.at[j], dst_ref=buf2.at[j], send_sem=send2.at[k], recv_sem=recv2.at[j],
            device_id=(s, j), device_id_type=MESH,
        ).wait_recv()
    for c in copies:
        c.wait_send()
    acc = buf2[0]
    for j in range(1, n_tm):
        acc = acc + buf2[j]
    buf3[s] = acc

    def send_p3(k, carry):
        space_copy(lambda b: buf3.at[s], buf3, send3, recv3, k).start()
        return carry

    lax.fori_loop(1, n_space, send_p3, 0)

    def wait_p3(k, carry):
        space_wait(buf3, send3, recv3, k)
        return carry

    lax.fori_loop(1, n_space, wait_p3, 0)

    def drain(k, carry):
        space_copy(lambda b: g_ref.at[b], buf1, send1, recv1, k).wait_send()
        space_copy(lambda b: buf3.at[s], buf3, send3, recv3, k).wait_send()
        return carry

    lax.fori_loop(1, n_space, drain, 0)
    out_ref[...] = buf3[...]


def a2a_body(n_tm, src_at, dst_at, x_ref, buf, send, recv, own):
    s = lax.axis_index("space")
    t = lax.axis_index("tm")
    copies = []
    for k in range(1, n_tm):
        a = lax.rem(t + k, n_tm)
        c = pltpu.make_async_remote_copy(
            src_ref=src_at(x_ref, a), dst_ref=dst_at(buf, t), send_sem=send.at[k], recv_sem=recv.at[t],
            device_id=(s, a), device_id_type=MESH,
        )
        c.start()
        copies.append(c)
    mine = pltpu.make_async_copy(src_at(x_ref, t), dst_at(buf, t), own.at[0])
    mine.start()
    mine.wait()
    for k in range(1, n_tm):
        j = lax.rem(t + k, n_tm)
        pltpu.make_async_remote_copy(
            src_ref=src_at(x_ref, j), dst_ref=dst_at(buf, j), send_sem=send.at[k], recv_sem=recv.at[j],
            device_id=(s, j), device_id_type=MESH,
        ).wait_recv()
    for c in copies:
        c.wait_send()


def front_kernel(n_space, n_tm, x_ref, cells_ref, g_out_ref, cells, gpart, buf1, buf2, buf3, *sems):
    send, recv, own = sems[:3]
    greet_all(n_space, n_tm)
    rows, _, cols = x_ref.shape
    width = cols // n_tm
    a2a_body(
        n_tm,
        lambda ref, a: ref.at[:, :, lanes(a, width)],
        lambda ref, j: ref.at[:, pl.ds(j * RANK, RANK), :],
        x_ref, cells, send, recv, own,
    )
    size = cells.shape[1]
    gram = jnp.zeros((size, size), jnp.float32)
    for x in range(rows):
        w = cells[x]
        gram = gram + lax.dot_general(
            w, w, (((1,), (1,)), ((), ())), preferred_element_type=jnp.float32
        )
    gpart[...] = gram.reshape(gpart.shape)
    allreduce_body(n_space, n_tm, gpart, g_out_ref, buf1, buf2, buf3, *sems[3:])
    cells_ref[...] = cells[...]


def front(vort_x):
    n_space = lax.axis_size("space")
    n_tm = lax.axis_size("tm")
    rows, _, cols = vort_x.shape
    size = n_tm * RANK
    cells_shape = (rows, size, cols // n_tm)
    chunks = (n_space, size // n_space, size)
    cells_x, gram = pl.pallas_call(
        functools.partial(front_kernel, n_space, n_tm),
        out_shape=(
            jax.ShapeDtypeStruct(cells_shape, vort_x.dtype),
            jax.ShapeDtypeStruct(chunks, jnp.float32),
        ),
        in_specs=[pl.BlockSpec(memory_space=pltpu.VMEM)],
        out_specs=(pl.BlockSpec(memory_space=pltpu.VMEM), pl.BlockSpec(memory_space=pltpu.VMEM)),
        scratch_shapes=[
            pltpu.VMEM(cells_shape, vort_x.dtype),
            pltpu.VMEM(chunks, jnp.float32),
            pltpu.VMEM(chunks, jnp.float32),
            pltpu.VMEM((n_tm,) + chunks[1:], jnp.float32),
            pltpu.VMEM(chunks, jnp.float32),
            pltpu.SemaphoreType.DMA((n_tm,)),
            pltpu.SemaphoreType.DMA((n_tm,)),
            pltpu.SemaphoreType.DMA((1,)),
            pltpu.SemaphoreType.DMA((n_space,)),
            pltpu.SemaphoreType.DMA((n_space,)),
            pltpu.SemaphoreType.DMA((n_tm,)),
            pltpu.SemaphoreType.DMA((n_tm,)),
            pltpu.SemaphoreType.DMA((n_space,)),
            pltpu.SemaphoreType.DMA((n_space,)),
        ],
        compiler_params=pltpu.CompilerParams(collective_id=0, has_side_effects=True),
    )(vort_x)
    return cells_x, gram.reshape(size, size)


def lanes(a, width):
    return pl.ds(pl.multiple_of(a * width, width), width)


def bdot(x, y):
    return jnp.einsum("nab,nbc->nac", x, y, precision=HIGH, preferred_element_type=jnp.float32)


def bdot_t(x, y):
    return jnp.einsum("nac,nbc->nab", x, y, precision=HIGH, preferred_element_type=jnp.float32)


def iotas(shape):
    return lax.broadcasted_iota(jnp.int32, shape, 1), lax.broadcasted_iota(jnp.int32, shape, 2)


def merge_coeffs(h):
    n = h.shape[0]
    kt = h[:, :RANK, :] + h[:, RANK:, :]
    row, col = iotas(h.shape)
    dcol = jnp.sum(jnp.where(row == col, h, 0.0), axis=2, keepdims=True)
    scales = jnp.sqrt(dcol[:, :RANK] + dcol[:, RANK:])
    inner = bdot_t(bdot(kt, h), kt)
    row, col = iotas(inner.shape)

    a = inner
    r = kt
    below = row[:, :, :1]
    for j in range(RANK):
        a_row = a[:, j : j + 1, :]
        r_row = r[:, j : j + 1, :]
        factor = jnp.where(below > j, a[:, :, j : j + 1] / a_row[:, :, j : j + 1], 0.0)
        a = a - factor * a_row
        r = r - factor * r_row
    diag_u = jnp.sum(jnp.where(row == col, a, 0.0), axis=2, keepdims=True)
    return r * (scales / jnp.sqrt(diag_u))


def place(x, offset, width):
    n, _, w = x.shape
    row, col = iotas((n, w, width))
    return bdot(x, jnp.where(col == row + offset, 1.0, 0.0))


def tree_levels(g_ref):
    size = 2 * RANK
    leaves = g_ref.shape[0] // RANK
    picks = []
    for k in range(leaves // 2):
        lane0 = (k * size) // 128 * 128
        block = g_ref[k * size : (k + 1) * size, lane0 : lane0 + 128][None]
        picks.append(place(block, -(k * size - lane0), size))
    basis = merge_coeffs(jnp.concatenate(picks, axis=0))
    while basis.shape[0] > 1:
        n = basis.shape[0] // 2
        w = basis.shape[2]
        pairs = basis.reshape(n, 2, RANK, w)
        bt = jnp.concatenate(
            [place(pairs[:, 0], 0, 2 * w), place(pairs[:, 1], w, 2 * w)], axis=1
        )
        gs = jnp.concatenate(
            [g_ref[k * 2 * w : (k + 1) * 2 * w, k * 2 * w : (k + 1) * 2 * w][None] for k in range(n)],
            axis=0,
        )
        h = bdot_t(bdot(bt, gs), bt)
        basis = bdot(merge_coeffs(h), bt)
    return basis[0]


def finish_kernel(n_tm, g_ref, w_ref, out_ref, part_ref, buf, send, recv, own):
    s = lax.axis_index("space")
    t = lax.axis_index("tm")
    barrier = pltpu.get_barrier_semaphore()
    for k in range(1, n_tm):
        a = lax.rem(t + k, n_tm)
        pl.semaphore_signal(barrier, inc=1, device_id=(s, a), device_id_type=MESH)
    basis_t = tree_levels(g_ref)
    hi = basis_t.astype(jnp.bfloat16)
    rest = basis_t - hi.astype(jnp.float32)
    mid = rest.astype(jnp.bfloat16)
    lo = (rest - mid.astype(jnp.float32)).astype(jnp.bfloat16)
    pieces = jnp.concatenate([hi, mid, lo], axis=0)
    for x in range(w_ref.shape[0]):
        terms = jnp.dot(pieces, w_ref[x], preferred_element_type=jnp.float32)
        part_ref[x] = (terms[:RANK] + terms[RANK : 2 * RANK]) + terms[2 * RANK :]
    share = part_ref.shape[1] // n_tm
    width = w_ref.shape[2]
    src_at = lambda a: part_ref.at[:, pl.ds(a * share, share), :]
    dst_at = lambda j: buf.at[:, :, lanes(j, width)]
    pl.semaphore_wait(barrier, n_tm - 1)
    copies = []
    for k in range(1, n_tm):
        a = lax.rem(t + k, n_tm)
        c = pltpu.make_async_remote_copy(
            src_ref=src_at(a), dst_ref=dst_at(t), send_sem=send.at[k], recv_sem=recv.at[t],
            device_id=(s, a), device_id_type=MESH,
        )
        c.start()
        copies.append(c)
    mine = pltpu.make_async_copy(src_at(t), dst_at(t), own.at[0])
    mine.start()
    mine.wait()
    for k in range(1, n_tm):
        j = lax.rem(t + k, n_tm)
        pltpu.make_async_remote_copy(
            src_ref=src_at(j), dst_ref=dst_at(j), send_sem=send.at[k], recv_sem=recv.at[j],
            device_id=(s, j), device_id_type=MESH,
        ).wait_recv()
    for c in copies:
        c.wait_send()
    out_ref[...] = buf[...]


def finish(gram, cells_x):
    n_tm = lax.axis_size("tm")
    rows, _, width = cells_x.shape
    share = RANK // n_tm
    out_shape = (rows, share, width * n_tm)
    return pl.pallas_call(
        functools.partial(finish_kernel, n_tm),
        out_shape=jax.ShapeDtypeStruct(out_shape, jnp.float32),
        in_specs=[pl.BlockSpec(memory_space=pltpu.VMEM)] * 2,
        out_specs=pl.BlockSpec(memory_space=pltpu.VMEM),
        scratch_shapes=[
            pltpu.VMEM((rows, RANK, width), jnp.float32),
            pltpu.VMEM(out_shape, jnp.float32),
            pltpu.SemaphoreType.DMA((n_tm,)),
            pltpu.SemaphoreType.DMA((n_tm,)),
            pltpu.SemaphoreType.DMA((1,)),
        ],
        compiler_params=pltpu.CompilerParams(collective_id=2, has_side_effects=True),
    )(gram, cells_x)


def local(velocity):
    rows = velocity.shape[2]
    span_v = halo_rows(velocity[:, 1], 2)
    stream_u = velocity[:, 0]
    f32 = lambda x: x.astype(jnp.float32)
    dv_dx = (
        8.0 * (f32(span_v[:, 3 : rows + 3]) - f32(span_v[:, 1 : rows + 1]))
        - (f32(span_v[:, 4:]) - f32(span_v[:, :rows]))
    ) / 12.0
    du_dz = (
        8.0 * (f32(jnp.roll(stream_u, -1, 2)) - f32(jnp.roll(stream_u, 1, 2)))
        - (f32(jnp.roll(stream_u, -2, 2)) - f32(jnp.roll(stream_u, 2, 2)))
    ) / 12.0
    vorticity = (dv_dx - du_dz).astype(jnp.bfloat16)
    blocks = lax.axis_size("tm")
    cols = vorticity.shape[2]
    width = cols // blocks
    vort_x = jnp.swapaxes(vorticity, 0, 1)
    cells_x, gram = front(vort_x)
    modes = jnp.swapaxes(finish(gram, cells_x), 0, 1)
    return (vorticity, modes)


def solution(mesh):
    in_specs = (P("tm", None, "space", None),)
    out_specs = (P("tm", "space", None), P("tm", "space", None))
    return jax.shard_map(local, mesh=mesh, in_specs=in_specs, out_specs=out_specs, check_vma=False)
```

```python
import functools

import jax
import jax.numpy as jnp
from jax import lax
from jax.experimental import pallas as pl
from jax.experimental.pallas import tpu as pltpu
from jax.sharding import PartitionSpec as P

RANK = 32
HIGH = lax.Precision.HIGHEST


def halo_rows(block, width):
    count = lax.axis_size("space")
    forward = [(i, (i + 1) % count) for i in range(count)]
    backward = [(target, source) for source, target in forward]
    rows = block.shape[1]
    low = lax.ppermute(block[:, rows - width :], "space", forward)
    high = lax.ppermute(block[:, :width], "space", backward)
    return jnp.concatenate([low, block, high], axis=1)


def spanwise(field):
    ahead = jnp.roll(field, -1, 2)
    behind = jnp.roll(field, 1, 2)
    ahead_two = jnp.roll(field, -2, 2)
    behind_two = jnp.roll(field, 2, 2)
    return (8.0 * (ahead - behind) - (ahead_two - behind_two)) / 12.0


MESH = pl.DeviceIdType.MESH


def greet_all(n_space, n_tm):
    s = lax.axis_index("space")
    t = lax.axis_index("tm")
    barrier = pltpu.get_barrier_semaphore()

    def greet_space(k, carry):
        b = lax.rem(s + k, n_space)
        pl.semaphore_signal(barrier, inc=1, device_id=(b, t), device_id_type=MESH)
        return carry

    def greet_tm(k, carry):
        a = lax.rem(t + k, n_tm)
        pl.semaphore_signal(barrier, inc=1, device_id=(s, a), device_id_type=MESH)
        return carry

    lax.fori_loop(1, n_space, greet_space, 0)
    lax.fori_loop(1, n_tm, greet_tm, 0)
    pl.semaphore_wait(barrier, (n_space - 1) + (n_tm - 1))


def allreduce_body(n_space, n_tm, g_ref, out_ref, buf1, buf2, buf3, send1, recv1, send2, recv2, send3, recv3):
    s = lax.axis_index("space")
    t = lax.axis_index("tm")

    def space_copy(src, dst_buf, send, recv, k):
        b = lax.rem(s + k, n_space)
        return pltpu.make_async_remote_copy(
            src_ref=src(b), dst_ref=dst_buf.at[s], send_sem=send.at[k], recv_sem=recv.at[s],
            device_id=(b, t), device_id_type=MESH,
        )

    def space_wait(dst_buf, send, recv, k):
        j = lax.rem(s + k, n_space)
        pltpu.make_async_remote_copy(
            src_ref=dst_buf.at[j], dst_ref=dst_buf.at[j], send_sem=send.at[k], recv_sem=recv.at[j],
            device_id=(j, t), device_id_type=MESH,
        ).wait_recv()

    def send_p1(k, carry):
        space_copy(lambda b: g_ref.at[b], buf1, send1, recv1, k).start()
        return carry

    lax.fori_loop(1, n_space, send_p1, 0)
    buf1[s] = g_ref[s]

    def wait_p1(k, carry):
        space_wait(buf1, send1, recv1, k)
        return carry

    lax.fori_loop(1, n_space, wait_p1, 0)
    acc = buf1[0]
    for j in range(1, n_space):
        acc = acc + buf1[j]
    buf2[t] = acc

    copies = []
    for k in range(1, n_tm):
        a = lax.rem(t + k, n_tm)
        c = pltpu.make_async_remote_copy(
            src_ref=buf2.at[t], dst_ref=buf2.at[t], send_sem=send2.at[k], recv_sem=recv2.at[t],
            device_id=(s, a), device_id_type=MESH,
        )
        c.start()
        copies.append(c)
    for k in range(1, n_tm):
        j = lax.rem(t + k, n_tm)
        pltpu.make_async_remote_copy(
            src_ref=buf2.at[j], dst_ref=buf2.at[j], send_sem=send2.at[k], recv_sem=recv2.at[j],
            device_id=(s, j), device_id_type=MESH,
        ).wait_recv()
    for c in copies:
        c.wait_send()
    acc = buf2[0]
    for j in range(1, n_tm):
        acc = acc + buf2[j]
    buf3[s] = acc

    def send_p3(k, carry):
        space_copy(lambda b: buf3.at[s], buf3, send3, recv3, k).start()
        return carry

    lax.fori_loop(1, n_space, send_p3, 0)

    def wait_p3(k, carry):
        space_wait(buf3, send3, recv3, k)
        return carry

    lax.fori_loop(1, n_space, wait_p3, 0)

    def drain(k, carry):
        space_copy(lambda b: g_ref.at[b], buf1, send1, recv1, k).wait_send()
        space_copy(lambda b: buf3.at[s], buf3, send3, recv3, k).wait_send()
        return carry

    lax.fori_loop(1, n_space, drain, 0)
    out_ref[...] = buf3[...]


def a2a_body(n_tm, src_at, dst_at, x_ref, buf, send, recv, own):
    s = lax.axis_index("space")
    t = lax.axis_index("tm")
    copies = []
    for k in range(1, n_tm):
        a = lax.rem(t + k, n_tm)
        c = pltpu.make_async_remote_copy(
            src_ref=src_at(x_ref, a), dst_ref=dst_at(buf, t), send_sem=send.at[k], recv_sem=recv.at[t],
            device_id=(s, a), device_id_type=MESH,
        )
        c.start()
        copies.append(c)
    mine = pltpu.make_async_copy(src_at(x_ref, t), dst_at(buf, t), own.at[0])
    mine.start()
    mine.wait()
    for k in range(1, n_tm):
        j = lax.rem(t + k, n_tm)
        pltpu.make_async_remote_copy(
            src_ref=src_at(x_ref, j), dst_ref=dst_at(buf, j), send_sem=send.at[k], recv_sem=recv.at[j],
            device_id=(s, j), device_id_type=MESH,
        ).wait_recv()
    for c in copies:
        c.wait_send()


def front_kernel(n_space, n_tm, x_ref, modes_ref, cells, gpart, buf1, buf2, buf3, gfull, part, gathered, *sems):
    send, recv, own = sems[:3]
    greet_all(n_space, n_tm)
    rows, _, cols = x_ref.shape
    width = cols // n_tm
    a2a_body(
        n_tm,
        lambda ref, a: ref.at[:, :, lanes(a, width)],
        lambda ref, j: ref.at[:, pl.ds(j * RANK, RANK), :],
        x_ref, cells, send, recv, own,
    )
    size = cells.shape[1]
    gram = jnp.zeros((size, size), jnp.float32)
    for x in range(rows):
        w = cells[x]
        gram = gram + lax.dot_general(
            w, w, (((1,), (1,)), ((), ())), preferred_element_type=jnp.float32
        )
    gpart[...] = gram.reshape(gpart.shape)
    allreduce_body(n_space, n_tm, gpart, buf1, buf1, buf2, buf3, *sems[3:9])
    gfull[...] = buf3[...].reshape(gfull.shape)
    finish_body(n_tm, gfull, cells, modes_ref, part, gathered, *sems[9:])


def front(vort_x):
    n_space = lax.axis_size("space")
    n_tm = lax.axis_size("tm")
    rows, _, cols = vort_x.shape
    size = n_tm * RANK
    width = cols // n_tm
    cells_shape = (rows, size, width)
    chunks = (n_space, size // n_space, size)
    out_shape = (rows, RANK // n_tm, cols)
    return pl.pallas_call(
        functools.partial(front_kernel, n_space, n_tm),
        out_shape=jax.ShapeDtypeStruct(out_shape, jnp.float32),
        in_specs=[pl.BlockSpec(memory_space=pltpu.VMEM)],
        out_specs=pl.BlockSpec(memory_space=pltpu.VMEM),
        scratch_shapes=[
            pltpu.VMEM(cells_shape, vort_x.dtype),
            pltpu.VMEM(chunks, jnp.float32),
            pltpu.VMEM(chunks, jnp.float32),
            pltpu.VMEM((n_tm,) + chunks[1:], jnp.float32),
            pltpu.VMEM(chunks, jnp.float32),
            pltpu.VMEM((size, size), jnp.float32),
            pltpu.VMEM((rows, RANK, width), jnp.float32),
            pltpu.VMEM(out_shape, jnp.float32),
            pltpu.SemaphoreType.DMA((n_tm,)),
            pltpu.SemaphoreType.DMA((n_tm,)),
            pltpu.SemaphoreType.DMA((1,)),
            pltpu.SemaphoreType.DMA((n_space,)),
            pltpu.SemaphoreType.DMA((n_space,)),
            pltpu.SemaphoreType.DMA((n_tm,)),
            pltpu.SemaphoreType.DMA((n_tm,)),
            pltpu.SemaphoreType.DMA((n_space,)),
            pltpu.SemaphoreType.DMA((n_space,)),
            pltpu.SemaphoreType.DMA((n_tm,)),
            pltpu.SemaphoreType.DMA((n_tm,)),
            pltpu.SemaphoreType.DMA((1,)),
        ],
        compiler_params=pltpu.CompilerParams(collective_id=0, has_side_effects=True),
    )(vort_x)


def lanes(a, width):
    return pl.ds(pl.multiple_of(a * width, width), width)


def bdot(x, y):
    return jnp.einsum("nab,nbc->nac", x, y, precision=HIGH, preferred_element_type=jnp.float32)


def bdot_t(x, y):
    return jnp.einsum("nac,nbc->nab", x, y, precision=HIGH, preferred_element_type=jnp.float32)


def iotas(shape):
    return lax.broadcasted_iota(jnp.int32, shape, 1), lax.broadcasted_iota(jnp.int32, shape, 2)


def merge_coeffs(h):
    n = h.shape[0]
    kt = h[:, :RANK, :] + h[:, RANK:, :]
    row, col = iotas(h.shape)
    dcol = jnp.sum(jnp.where(row == col, h, 0.0), axis=2, keepdims=True)
    scales = jnp.sqrt(dcol[:, :RANK] + dcol[:, RANK:])
    inner = bdot_t(bdot(kt, h), kt)
    row, col = iotas(inner.shape)

    a = inner
    r = kt
    below = row[:, :, :1]
    for j in range(RANK):
        a_row = a[:, j : j + 1, :]
        r_row = r[:, j : j + 1, :]
        factor = jnp.where(below > j, a[:, :, j : j + 1] / a_row[:, :, j : j + 1], 0.0)
        a = a - factor * a_row
        r = r - factor * r_row
    diag_u = jnp.sum(jnp.where(row == col, a, 0.0), axis=2, keepdims=True)
    return r * (scales / jnp.sqrt(diag_u))


def place(x, offset, width):
    n, _, w = x.shape
    row, col = iotas((n, w, width))
    return bdot(x, jnp.where(col == row + offset, 1.0, 0.0))


def tree_levels(g_ref):
    size = 2 * RANK
    leaves = g_ref.shape[0] // RANK
    picks = []
    for k in range(leaves // 2):
        lane0 = (k * size) // 128 * 128
        block = g_ref[k * size : (k + 1) * size, lane0 : lane0 + 128][None]
        picks.append(place(block, -(k * size - lane0), size))
    basis = merge_coeffs(jnp.concatenate(picks, axis=0))
    while basis.shape[0] > 1:
        n = basis.shape[0] // 2
        w = basis.shape[2]
        pairs = basis.reshape(n, 2, RANK, w)
        bt = jnp.concatenate(
            [place(pairs[:, 0], 0, 2 * w), place(pairs[:, 1], w, 2 * w)], axis=1
        )
        gs = jnp.concatenate(
            [g_ref[k * 2 * w : (k + 1) * 2 * w, k * 2 * w : (k + 1) * 2 * w][None] for k in range(n)],
            axis=0,
        )
        h = bdot_t(bdot(bt, gs), bt)
        basis = bdot(merge_coeffs(h), bt)
    return basis[0]


def finish_body(n_tm, g_ref, w_ref, out_ref, part_ref, buf, send, recv, own):
    s = lax.axis_index("space")
    t = lax.axis_index("tm")
    basis_t = tree_levels(g_ref)
    hi = basis_t.astype(jnp.bfloat16)
    rest = basis_t - hi.astype(jnp.float32)
    mid = rest.astype(jnp.bfloat16)
    lo = (rest - mid.astype(jnp.float32)).astype(jnp.bfloat16)
    pieces = jnp.concatenate([hi, mid, lo], axis=0)
    for x in range(w_ref.shape[0]):
        terms = jnp.dot(pieces, w_ref[x], preferred_element_type=jnp.float32)
        part_ref[x] = (terms[:RANK] + terms[RANK : 2 * RANK]) + terms[2 * RANK :]
    share = part_ref.shape[1] // n_tm
    width = w_ref.shape[2]
    src_at = lambda a: part_ref.at[:, pl.ds(a * share, share), :]
    dst_at = lambda j: buf.at[:, :, lanes(j, width)]
    copies = []
    for k in range(1, n_tm):
        a = lax.rem(t + k, n_tm)
        c = pltpu.make_async_remote_copy(
            src_ref=src_at(a), dst_ref=dst_at(t), send_sem=send.at[k], recv_sem=recv.at[t],
            device_id=(s, a), device_id_type=MESH,
        )
        c.start()
        copies.append(c)
    mine = pltpu.make_async_copy(src_at(t), dst_at(t), own.at[0])
    mine.start()
    mine.wait()
    for k in range(1, n_tm):
        j = lax.rem(t + k, n_tm)
        pltpu.make_async_remote_copy(
            src_ref=src_at(j), dst_ref=dst_at(j), send_sem=send.at[k], recv_sem=recv.at[j],
            device_id=(s, j), device_id_type=MESH,
        ).wait_recv()
    for c in copies:
        c.wait_send()
    out_ref[...] = buf[...]


def local(velocity):
    rows = velocity.shape[2]
    span_v = halo_rows(velocity[:, 1], 2).astype(jnp.float32)
    stream_u = velocity[:, 0].astype(jnp.float32)
    dv_dx = (
        8.0 * (span_v[:, 3 : rows + 3] - span_v[:, 1 : rows + 1])
        - (span_v[:, 4:] - span_v[:, :rows])
    ) / 12.0
    vorticity = (dv_dx - spanwise(stream_u)).astype(jnp.bfloat16)
    blocks = lax.axis_size("tm")
    cols = vorticity.shape[2]
    width = cols // blocks
    vort_x = jnp.swapaxes(vorticity, 0, 1)
    modes = jnp.swapaxes(front(vort_x), 0, 1)
    return (vorticity, modes)


def solution(mesh):
    in_specs = (P("tm", None, "space", None),)
    out_specs = (P("tm", "space", None), P("tm", "space", None))
    return jax.shard_map(local, mesh=mesh, in_specs=in_specs, out_specs=out_specs, check_vma=False)
```

```python
import functools

import jax
import jax.numpy as jnp
from jax import lax
from jax.experimental import pallas as pl
from jax.experimental.pallas import tpu as pltpu
from jax.sharding import PartitionSpec as P

RANK = 32
HIGH = lax.Precision.HIGHEST


def halo_rows(block, width):
    count = lax.axis_size("space")
    forward = [(i, (i + 1) % count) for i in range(count)]
    backward = [(target, source) for source, target in forward]
    rows = block.shape[1]
    low = lax.ppermute(block[:, rows - width :], "space", forward)
    high = lax.ppermute(block[:, :width], "space", backward)
    return jnp.concatenate([low, block, high], axis=1)


def spanwise(field):
    ahead = jnp.roll(field, -1, 2)
    behind = jnp.roll(field, 1, 2)
    ahead_two = jnp.roll(field, -2, 2)
    behind_two = jnp.roll(field, 2, 2)
    return (8.0 * (ahead - behind) - (ahead_two - behind_two)) / 12.0


MESH = pl.DeviceIdType.MESH


def greet_all(n_space, n_tm):
    s = lax.axis_index("space")
    t = lax.axis_index("tm")
    barrier = pltpu.get_barrier_semaphore()

    def greet_space(k, carry):
        b = lax.rem(s + k, n_space)
        pl.semaphore_signal(barrier, inc=1, device_id=(b, t), device_id_type=MESH)
        return carry

    def greet_tm(k, carry):
        a = lax.rem(t + k, n_tm)
        pl.semaphore_signal(barrier, inc=1, device_id=(s, a), device_id_type=MESH)
        return carry

    lax.fori_loop(1, n_space, greet_space, 0)
    lax.fori_loop(1, n_tm, greet_tm, 0)
    pl.semaphore_wait(barrier, (n_space - 1) + (n_tm - 1))


def allreduce_body(n_space, n_tm, g_ref, out_ref, buf1, buf2, buf3, send1, recv1, send2, recv2, send3, recv3):
    s = lax.axis_index("space")
    t = lax.axis_index("tm")

    def space_copy(src, dst_buf, send, recv, k):
        b = lax.rem(s + k, n_space)
        return pltpu.make_async_remote_copy(
            src_ref=src(b), dst_ref=dst_buf.at[s], send_sem=send.at[k], recv_sem=recv.at[s],
            device_id=(b, t), device_id_type=MESH,
        )

    def space_wait(dst_buf, send, recv, k):
        j = lax.rem(s + k, n_space)
        pltpu.make_async_remote_copy(
            src_ref=dst_buf.at[j], dst_ref=dst_buf.at[j], send_sem=send.at[k], recv_sem=recv.at[j],
            device_id=(j, t), device_id_type=MESH,
        ).wait_recv()

    def send_p1(k, carry):
        space_copy(lambda b: g_ref.at[b], buf1, send1, recv1, k).start()
        return carry

    lax.fori_loop(1, n_space, send_p1, 0)
    buf1[s] = g_ref[s]

    def wait_p1(k, carry):
        space_wait(buf1, send1, recv1, k)
        return carry

    lax.fori_loop(1, n_space, wait_p1, 0)
    acc = buf1[0]
    for j in range(1, n_space):
        acc = acc + buf1[j]
    buf2[t] = acc

    copies = []
    for k in range(1, n_tm):
        a = lax.rem(t + k, n_tm)
        c = pltpu.make_async_remote_copy(
            src_ref=buf2.at[t], dst_ref=buf2.at[t], send_sem=send2.at[k], recv_sem=recv2.at[t],
            device_id=(s, a), device_id_type=MESH,
        )
        c.start()
        copies.append(c)
    for k in range(1, n_tm):
        j = lax.rem(t + k, n_tm)
        pltpu.make_async_remote_copy(
            src_ref=buf2.at[j], dst_ref=buf2.at[j], send_sem=send2.at[k], recv_sem=recv2.at[j],
            device_id=(s, j), device_id_type=MESH,
        ).wait_recv()
    for c in copies:
        c.wait_send()
    acc = buf2[0]
    for j in range(1, n_tm):
        acc = acc + buf2[j]
    buf3[s] = acc

    def send_p3(k, carry):
        space_copy(lambda b: buf3.at[s], buf3, send3, recv3, k).start()
        return carry

    lax.fori_loop(1, n_space, send_p3, 0)

    def wait_p3(k, carry):
        space_wait(buf3, send3, recv3, k)
        return carry

    lax.fori_loop(1, n_space, wait_p3, 0)

    def drain(k, carry):
        space_copy(lambda b: g_ref.at[b], buf1, send1, recv1, k).wait_send()
        space_copy(lambda b: buf3.at[s], buf3, send3, recv3, k).wait_send()
        return carry

    lax.fori_loop(1, n_space, drain, 0)
    if out_ref is not None:
        out_ref[...] = buf3[...]


def a2a_body(n_tm, src_at, dst_at, x_ref, buf, send, recv, own):
    s = lax.axis_index("space")
    t = lax.axis_index("tm")
    copies = []
    for k in range(1, n_tm):
        a = lax.rem(t + k, n_tm)
        c = pltpu.make_async_remote_copy(
            src_ref=src_at(x_ref, a), dst_ref=dst_at(buf, t), send_sem=send.at[k], recv_sem=recv.at[t],
            device_id=(s, a), device_id_type=MESH,
        )
        c.start()
        copies.append(c)
    mine = pltpu.make_async_copy(src_at(x_ref, t), dst_at(buf, t), own.at[0])
    mine.start()
    mine.wait()
    for k in range(1, n_tm):
        j = lax.rem(t + k, n_tm)
        pltpu.make_async_remote_copy(
            src_ref=src_at(x_ref, j), dst_ref=dst_at(buf, j), send_sem=send.at[k], recv_sem=recv.at[j],
            device_id=(s, j), device_id_type=MESH,
        ).wait_recv()
    for c in copies:
        c.wait_send()


def front_kernel(n_space, n_tm, x_ref, modes_ref, cells, gpart, buf1, buf2, buf3, part, gathered, *sems):
    send, recv, own = sems[:3]
    greet_all(n_space, n_tm)
    rows, _, cols = x_ref.shape
    width = cols // n_tm
    a2a_body(
        n_tm,
        lambda ref, a: ref.at[:, :, lanes(a, width)],
        lambda ref, j: ref.at[:, pl.ds(j * RANK, RANK), :],
        x_ref, cells, send, recv, own,
    )
    size = cells.shape[1]
    gram = jnp.zeros((size, size), jnp.float32)
    for x in range(rows):
        w = cells[x]
        gram = gram + lax.dot_general(
            w, w, (((1,), (1,)), ((), ())), preferred_element_type=jnp.float32
        )
    gpart[...] = gram.reshape(gpart.shape)
    allreduce_body(n_space, n_tm, gpart, None, buf1, buf2, buf3, *sems[3:9])
    finish_body(n_tm, buf3, cells, modes_ref, part, gathered, *sems[9:])


def front(vort_x):
    n_space = lax.axis_size("space")
    n_tm = lax.axis_size("tm")
    rows, _, cols = vort_x.shape
    size = n_tm * RANK
    width = cols // n_tm
    cells_shape = (rows, size, width)
    chunks = (n_space, size // n_space, size)
    out_shape = (rows, RANK // n_tm, cols)
    return pl.pallas_call(
        functools.partial(front_kernel, n_space, n_tm),
        out_shape=jax.ShapeDtypeStruct(out_shape, jnp.float32),
        in_specs=[pl.BlockSpec(memory_space=pltpu.VMEM)],
        out_specs=pl.BlockSpec(memory_space=pltpu.VMEM),
        scratch_shapes=[
            pltpu.VMEM(cells_shape, vort_x.dtype),
            pltpu.VMEM(chunks, jnp.float32),
            pltpu.VMEM(chunks, jnp.float32),
            pltpu.VMEM((n_tm,) + chunks[1:], jnp.float32),
            pltpu.VMEM(chunks, jnp.float32),
            pltpu.VMEM((rows, RANK, width), jnp.float32),
            pltpu.VMEM(out_shape, jnp.float32),
            pltpu.SemaphoreType.DMA((n_tm,)),
            pltpu.SemaphoreType.DMA((n_tm,)),
            pltpu.SemaphoreType.DMA((1,)),
            pltpu.SemaphoreType.DMA((n_space,)),
            pltpu.SemaphoreType.DMA((n_space,)),
            pltpu.SemaphoreType.DMA((n_tm,)),
            pltpu.SemaphoreType.DMA((n_tm,)),
            pltpu.SemaphoreType.DMA((n_space,)),
            pltpu.SemaphoreType.DMA((n_space,)),
            pltpu.SemaphoreType.DMA((n_tm,)),
            pltpu.SemaphoreType.DMA((n_tm,)),
            pltpu.SemaphoreType.DMA((1,)),
            pltpu.SemaphoreType.DMA((n_tm,)),
        ],
        compiler_params=pltpu.CompilerParams(collective_id=0, has_side_effects=True),
    )(vort_x)


def lanes(a, width):
    return pl.ds(pl.multiple_of(a * width, width), width)


def bdot(x, y):
    return jnp.einsum("nab,nbc->nac", x, y, precision=HIGH, preferred_element_type=jnp.float32)


def bdot_t(x, y):
    return jnp.einsum("nac,nbc->nab", x, y, precision=HIGH, preferred_element_type=jnp.float32)


def iotas(shape):
    return lax.broadcasted_iota(jnp.int32, shape, 1), lax.broadcasted_iota(jnp.int32, shape, 2)


def merge_coeffs(h):
    n = h.shape[0]
    kt = h[:, :RANK, :] + h[:, RANK:, :]
    row, col = iotas(h.shape)
    dcol = jnp.sum(jnp.where(row == col, h, 0.0), axis=2, keepdims=True)
    scales = jnp.sqrt(dcol[:, :RANK] + dcol[:, RANK:])
    inner = bdot_t(bdot(kt, h), kt)
    row, col = iotas(inner.shape)

    a = inner
    r = kt
    below = row[:, :, :1]
    for j in range(RANK):
        a_row = a[:, j : j + 1, :]
        r_row = r[:, j : j + 1, :]
        factor = jnp.where(below > j, a[:, :, j : j + 1] / a_row[:, :, j : j + 1], 0.0)
        a = a - factor * a_row
        r = r - factor * r_row
    diag_u = jnp.sum(jnp.where(row == col, a, 0.0), axis=2, keepdims=True)
    return r * (scales / jnp.sqrt(diag_u))


def place(x, offset, width):
    n, _, w = x.shape
    row, col = iotas((n, w, width))
    return bdot(x, jnp.where(col == row + offset, 1.0, 0.0))


def g_rows(g_ref, r0, r1):
    c = g_ref.shape[1]
    lo, hi = r0 // c, -(-r1 // c)
    return g_ref[lo:hi].reshape((hi - lo) * c, g_ref.shape[2])[r0 - lo * c : r1 - lo * c]


def tree_levels(g_ref):
    size = 2 * RANK
    leaves = g_ref.shape[2] // RANK
    picks = []
    for k in range(leaves // 2):
        lane0 = (k * size) // 128 * 128
        block = g_rows(g_ref, k * size, (k + 1) * size)[:, lane0 : lane0 + 128][None]
        picks.append(place(block, -(k * size - lane0), size))
    basis = merge_coeffs(jnp.concatenate(picks, axis=0))
    while basis.shape[0] > 1:
        n = basis.shape[0] // 2
        w = basis.shape[2]
        pairs = basis.reshape(n, 2, RANK, w)
        bt = jnp.concatenate(
            [place(pairs[:, 0], 0, 2 * w), place(pairs[:, 1], w, 2 * w)], axis=1
        )
        gs = jnp.concatenate(
            [g_rows(g_ref, k * 2 * w, (k + 1) * 2 * w)[:, k * 2 * w : (k + 1) * 2 * w][None] for k in range(n)],
            axis=0,
        )
        h = bdot_t(bdot(bt, gs), bt)
        basis = bdot(merge_coeffs(h), bt)
    return basis[0]


def finish_body(n_tm, g_ref, w_ref, out_ref, part_ref, buf, send, recv, own, send_late):
    s = lax.axis_index("space")
    t = lax.axis_index("tm")
    basis_t = tree_levels(g_ref)
    hi = basis_t.astype(jnp.bfloat16)
    rest = basis_t - hi.astype(jnp.float32)
    mid = rest.astype(jnp.bfloat16)
    lo = (rest - mid.astype(jnp.float32)).astype(jnp.bfloat16)
    pieces = jnp.concatenate([hi, mid, lo], axis=0)
    rows = w_ref.shape[0]
    share = part_ref.shape[1] // n_tm
    width = w_ref.shape[2]
    src_at = lambda a, r0, nr: part_ref.at[pl.ds(r0, nr), pl.ds(a * share, share), :]
    dst_at = lambda j, r0, nr: buf.at[pl.ds(r0, nr), :, lanes(j, width)]
    halves = ((0, rows // 2, send), (rows // 2, rows - rows // 2, send_late))
    copies = []
    for r0, nr, sems in halves:
        for x in range(r0, r0 + nr):
            terms = jnp.dot(pieces, w_ref[x], preferred_element_type=jnp.float32)
            part_ref[x] = (terms[:RANK] + terms[RANK : 2 * RANK]) + terms[2 * RANK :]
        for k in range(1, n_tm):
            a = lax.rem(t + k, n_tm)
            c = pltpu.make_async_remote_copy(
                src_ref=src_at(a, r0, nr), dst_ref=dst_at(t, r0, nr), send_sem=sems.at[k], recv_sem=recv.at[t],
                device_id=(s, a), device_id_type=MESH,
            )
            c.start()
            copies.append(c)
    mine = pltpu.make_async_copy(src_at(t, 0, rows), dst_at(t, 0, rows), own.at[0])
    mine.start()
    mine.wait()
    for k in range(1, n_tm):
        j = lax.rem(t + k, n_tm)
        pltpu.make_async_remote_copy(
            src_ref=src_at(j, 0, rows), dst_ref=dst_at(j, 0, rows), send_sem=send.at[k], recv_sem=recv.at[j],
            device_id=(s, j), device_id_type=MESH,
        ).wait_recv()
    for c in copies:
        c.wait_send()
    out_ref[...] = buf[...]


def local(velocity):
    rows = velocity.shape[2]
    span_v = halo_rows(velocity[:, 1], 2).astype(jnp.float32)
    stream_u = velocity[:, 0].astype(jnp.float32)
    dv_dx = (
        8.0 * (span_v[:, 3 : rows + 3] - span_v[:, 1 : rows + 1])
        - (span_v[:, 4:] - span_v[:, :rows])
    ) / 12.0
    vorticity = (dv_dx - spanwise(stream_u)).astype(jnp.bfloat16)
    blocks = lax.axis_size("tm")
    cols = vorticity.shape[2]
    width = cols // blocks
    vort_x = jnp.swapaxes(vorticity, 0, 1)
    modes = jnp.swapaxes(front(vort_x), 0, 1)
    return (vorticity, modes)


def solution(mesh):
    in_specs = (P("tm", None, "space", None),)
    out_specs = (P("tm", "space", None), P("tm", "space", None))
    return jax.shard_map(local, mesh=mesh, in_specs=in_specs, out_specs=out_specs, check_vma=False)
```

```python
import functools

import jax
import jax.numpy as jnp
from jax import lax
from jax.experimental import pallas as pl
from jax.experimental.pallas import tpu as pltpu
from jax.sharding import PartitionSpec as P

RANK = 32
HIGH = lax.Precision.HIGHEST


def halo_rows(block, width):
    count = lax.axis_size("space")
    forward = [(i, (i + 1) % count) for i in range(count)]
    backward = [(target, source) for source, target in forward]
    rows = block.shape[1]
    low = lax.ppermute(block[:, rows - width :], "space", forward)
    high = lax.ppermute(block[:, :width], "space", backward)
    return jnp.concatenate([low, block, high], axis=1)


def spanwise(field):
    ahead = jnp.roll(field, -1, 2)
    behind = jnp.roll(field, 1, 2)
    ahead_two = jnp.roll(field, -2, 2)
    behind_two = jnp.roll(field, 2, 2)
    return (8.0 * (ahead - behind) - (ahead_two - behind_two)) / 12.0


MESH = pl.DeviceIdType.MESH


def greet_all(n_space, n_tm):
    s = lax.axis_index("space")
    t = lax.axis_index("tm")
    barrier = pltpu.get_barrier_semaphore()

    def greet_space(k, carry):
        b = lax.rem(s + k, n_space)
        pl.semaphore_signal(barrier, inc=1, device_id=(b, t), device_id_type=MESH)
        return carry

    def greet_tm(k, carry):
        a = lax.rem(t + k, n_tm)
        pl.semaphore_signal(barrier, inc=1, device_id=(s, a), device_id_type=MESH)
        return carry

    lax.fori_loop(1, n_space, greet_space, 0)
    lax.fori_loop(1, n_tm, greet_tm, 0)
    pl.semaphore_wait(barrier, (n_space - 1) + (n_tm - 1))


def allreduce_body(n_space, n_tm, g_ref, out_ref, buf1, buf2, buf3, send1, recv1, send2, recv2, send3, recv3):
    s = lax.axis_index("space")
    t = lax.axis_index("tm")

    def space_copy(src, dst_buf, send, recv, k):
        b = lax.rem(s + k, n_space)
        return pltpu.make_async_remote_copy(
            src_ref=src(b), dst_ref=dst_buf.at[s], send_sem=send.at[k], recv_sem=recv.at[s],
            device_id=(b, t), device_id_type=MESH,
        )

    def space_wait(dst_buf, send, recv, k):
        j = lax.rem(s + k, n_space)
        pltpu.make_async_remote_copy(
            src_ref=dst_buf.at[j], dst_ref=dst_buf.at[j], send_sem=send.at[k], recv_sem=recv.at[j],
            device_id=(j, t), device_id_type=MESH,
        ).wait_recv()

    def send_p1(k, carry):
        space_copy(lambda b: g_ref.at[b], buf1, send1, recv1, k).start()
        return carry

    lax.fori_loop(1, n_space, send_p1, 0)
    buf1[s] = g_ref[s]

    def wait_p1(k, carry):
        space_wait(buf1, send1, recv1, k)
        return carry

    lax.fori_loop(1, n_space, wait_p1, 0)
    acc = buf1[0]
    for j in range(1, n_space):
        acc = acc + buf1[j]
    buf2[t] = acc

    copies = []
    for k in range(1, n_tm):
        a = lax.rem(t + k, n_tm)
        c = pltpu.make_async_remote_copy(
            src_ref=buf2.at[t], dst_ref=buf2.at[t], send_sem=send2.at[k], recv_sem=recv2.at[t],
            device_id=(s, a), device_id_type=MESH,
        )
        c.start()
        copies.append(c)
    for k in range(1, n_tm):
        j = lax.rem(t + k, n_tm)
        pltpu.make_async_remote_copy(
            src_ref=buf2.at[j], dst_ref=buf2.at[j], send_sem=send2.at[k], recv_sem=recv2.at[j],
            device_id=(s, j), device_id_type=MESH,
        ).wait_recv()
    for c in copies:
        c.wait_send()
    acc = buf2[0]
    for j in range(1, n_tm):
        acc = acc + buf2[j]
    buf3[s] = acc

    def send_p3(k, carry):
        space_copy(lambda b: buf3.at[s], buf3, send3, recv3, k).start()
        return carry

    lax.fori_loop(1, n_space, send_p3, 0)

    def wait_p3(k, carry):
        space_wait(buf3, send3, recv3, k)
        return carry

    lax.fori_loop(1, n_space, wait_p3, 0)

    def drain(k, carry):
        space_copy(lambda b: g_ref.at[b], buf1, send1, recv1, k).wait_send()
        space_copy(lambda b: buf3.at[s], buf3, send3, recv3, k).wait_send()
        return carry

    lax.fori_loop(1, n_space, drain, 0)
    out_ref[...] = buf3[...]


def a2a_body(n_tm, src_at, dst_at, x_ref, buf, send, recv, own):
    s = lax.axis_index("space")
    t = lax.axis_index("tm")
    copies = []
    for k in range(1, n_tm):
        a = lax.rem(t + k, n_tm)
        c = pltpu.make_async_remote_copy(
            src_ref=src_at(x_ref, a), dst_ref=dst_at(buf, t), send_sem=send.at[k], recv_sem=recv.at[t],
            device_id=(s, a), device_id_type=MESH,
        )
        c.start()
        copies.append(c)
    mine = pltpu.make_async_copy(src_at(x_ref, t), dst_at(buf, t), own.at[0])
    mine.start()
    mine.wait()
    for k in range(1, n_tm):
        j = lax.rem(t + k, n_tm)
        pltpu.make_async_remote_copy(
            src_ref=src_at(x_ref, j), dst_ref=dst_at(buf, j), send_sem=send.at[k], recv_sem=recv.at[j],
            device_id=(s, j), device_id_type=MESH,
        ).wait_recv()
    for c in copies:
        c.wait_send()


def front_kernel(n_space, n_tm, x_ref, modes_ref, cells, gpart, buf1, buf2, buf3, gfull, part, gathered, *sems):
    send, recv, own = sems[:3]
    greet_all(n_space, n_tm)
    rows, _, cols = x_ref.shape
    width = cols // n_tm
    a2a_body(
        n_tm,
        lambda ref, a: ref.at[:, :, lanes(a, width)],
        lambda ref, j: ref.at[:, pl.ds(j * RANK, RANK), :],
        x_ref, cells, send, recv, own,
    )
    size = cells.shape[1]
    gram = jnp.zeros((size, size), jnp.float32)
    for x in range(rows):
        w = cells[x]
        gram = gram + lax.dot_general(
            w, w, (((1,), (1,)), ((), ())), preferred_element_type=jnp.float32
        )
    gpart[...] = gram.reshape(gpart.shape)
    allreduce_body(n_space, n_tm, gpart, buf1, buf1, buf2, buf3, *sems[3:9])
    gfull[...] = buf3[...].reshape(gfull.shape)
    finish_body(n_tm, gfull, cells, modes_ref, part, gathered, *sems[9:])


def front(vort_x):
    n_space = lax.axis_size("space")
    n_tm = lax.axis_size("tm")
    rows, _, cols = vort_x.shape
    size = n_tm * RANK
    width = cols // n_tm
    cells_shape = (rows, size, width)
    chunks = (n_space, size // n_space, size)
    out_shape = (rows, RANK // n_tm, cols)
    return pl.pallas_call(
        functools.partial(front_kernel, n_space, n_tm),
        out_shape=jax.ShapeDtypeStruct(out_shape, jnp.float32),
        in_specs=[pl.BlockSpec(memory_space=pltpu.VMEM)],
        out_specs=pl.BlockSpec(memory_space=pltpu.VMEM),
        scratch_shapes=[
            pltpu.VMEM(cells_shape, vort_x.dtype),
            pltpu.VMEM(chunks, jnp.float32),
            pltpu.VMEM(chunks, jnp.float32),
            pltpu.VMEM((n_tm,) + chunks[1:], jnp.float32),
            pltpu.VMEM(chunks, jnp.float32),
            pltpu.VMEM((size, size), jnp.float32),
            pltpu.VMEM((rows, RANK, width), jnp.float32),
            pltpu.VMEM(out_shape, jnp.float32),
            pltpu.SemaphoreType.DMA((n_tm,)),
            pltpu.SemaphoreType.DMA((n_tm,)),
            pltpu.SemaphoreType.DMA((1,)),
            pltpu.SemaphoreType.DMA((n_space,)),
            pltpu.SemaphoreType.DMA((n_space,)),
            pltpu.SemaphoreType.DMA((n_tm,)),
            pltpu.SemaphoreType.DMA((n_tm,)),
            pltpu.SemaphoreType.DMA((n_space,)),
            pltpu.SemaphoreType.DMA((n_space,)),
            pltpu.SemaphoreType.DMA((n_tm,)),
            pltpu.SemaphoreType.DMA((n_tm,)),
            pltpu.SemaphoreType.DMA((1,)),
        ],
        compiler_params=pltpu.CompilerParams(collective_id=0, has_side_effects=True),
    )(vort_x)


def lanes(a, width):
    return pl.ds(pl.multiple_of(a * width, width), width)


def bdot(x, y):
    return jnp.einsum("nab,nbc->nac", x, y, precision=HIGH, preferred_element_type=jnp.float32)


def bdot_t(x, y):
    return jnp.einsum("nac,nbc->nab", x, y, precision=HIGH, preferred_element_type=jnp.float32)


def iotas(shape):
    return lax.broadcasted_iota(jnp.int32, shape, 1), lax.broadcasted_iota(jnp.int32, shape, 2)


def merge_coeffs(h):
    n = h.shape[0]
    kt = h[:, :RANK, :] + h[:, RANK:, :]
    row, col = iotas(h.shape)
    dcol = jnp.sum(jnp.where(row == col, h, 0.0), axis=2, keepdims=True)
    scales = jnp.sqrt(dcol[:, :RANK] + dcol[:, RANK:])
    inner = bdot_t(bdot(kt, h), kt)
    row, col = iotas(inner.shape)

    a = inner
    r = kt
    below = row[:, :, :1]
    for j in range(RANK):
        a_row = a[:, j : j + 1, :]
        r_row = r[:, j : j + 1, :]
        factor = jnp.where(below > j, a[:, :, j : j + 1] / a_row[:, :, j : j + 1], 0.0)
        a = a - factor * a_row
        r = r - factor * r_row
    diag_u = jnp.sum(jnp.where(row == col, a, 0.0), axis=2, keepdims=True)
    return r * (scales / jnp.sqrt(diag_u))


def split3(x):
    hi = x.astype(jnp.bfloat16)
    rest = x - hi.astype(jnp.float32)
    mid = rest.astype(jnp.bfloat16)
    lo = (rest - mid.astype(jnp.float32)).astype(jnp.bfloat16)
    return hi, mid, lo


def place(x, offset, width):
    n, r, w = x.shape
    row, col = iotas((n, w, width))
    pick = jnp.where(col == row + offset, 1.0, 0.0).astype(jnp.bfloat16)
    terms = jnp.einsum(
        "nab,nbc->nac", jnp.concatenate(split3(x), axis=1), pick, preferred_element_type=jnp.float32
    )
    return (terms[:, :r] + terms[:, r : 2 * r]) + terms[:, 2 * r :]


def tree_levels(g_ref):
    size = 2 * RANK
    leaves = g_ref.shape[0] // RANK
    picks = []
    for k in range(leaves // 2):
        lane0 = (k * size) // 128 * 128
        block = g_ref[k * size : (k + 1) * size, lane0 : lane0 + 128][None]
        picks.append(place(block, -(k * size - lane0), size))
    basis = merge_coeffs(jnp.concatenate(picks, axis=0))
    while basis.shape[0] > 1:
        n = basis.shape[0] // 2
        w = basis.shape[2]
        pairs = basis.reshape(n, 2, RANK, w)
        bt = jnp.concatenate(
            [place(pairs[:, 0], 0, 2 * w), place(pairs[:, 1], w, 2 * w)], axis=1
        )
        gs = jnp.concatenate(
            [g_ref[k * 2 * w : (k + 1) * 2 * w, k * 2 * w : (k + 1) * 2 * w][None] for k in range(n)],
            axis=0,
        )
        h = bdot_t(bdot(bt, gs), bt)
        basis = bdot(merge_coeffs(h), bt)
    return basis[0]


def finish_body(n_tm, g_ref, w_ref, out_ref, part_ref, buf, send, recv, own):
    s = lax.axis_index("space")
    t = lax.axis_index("tm")
    basis_t = tree_levels(g_ref)
    hi = basis_t.astype(jnp.bfloat16)
    rest = basis_t - hi.astype(jnp.float32)
    mid = rest.astype(jnp.bfloat16)
    lo = (rest - mid.astype(jnp.float32)).astype(jnp.bfloat16)
    pieces = jnp.concatenate([hi, mid, lo], axis=0)
    for x in range(w_ref.shape[0]):
        terms = jnp.dot(pieces, w_ref[x], preferred_element_type=jnp.float32)
        part_ref[x] = (terms[:RANK] + terms[RANK : 2 * RANK]) + terms[2 * RANK :]
    share = part_ref.shape[1] // n_tm
    width = w_ref.shape[2]
    src_at = lambda a: part_ref.at[:, pl.ds(a * share, share), :]
    dst_at = lambda j: buf.at[:, :, lanes(j, width)]
    copies = []
    for k in range(1, n_tm):
        a = lax.rem(t + k, n_tm)
        c = pltpu.make_async_remote_copy(
            src_ref=src_at(a), dst_ref=dst_at(t), send_sem=send.at[k], recv_sem=recv.at[t],
            device_id=(s, a), device_id_type=MESH,
        )
        c.start()
        copies.append(c)
    mine = pltpu.make_async_copy(src_at(t), dst_at(t), own.at[0])
    mine.start()
    mine.wait()
    for k in range(1, n_tm):
        j = lax.rem(t + k, n_tm)
        pltpu.make_async_remote_copy(
            src_ref=src_at(j), dst_ref=dst_at(j), send_sem=send.at[k], recv_sem=recv.at[j],
            device_id=(s, j), device_id_type=MESH,
        ).wait_recv()
    for c in copies:
        c.wait_send()
    out_ref[...] = buf[...]


def local(velocity):
    rows = velocity.shape[2]
    span_v = halo_rows(velocity[:, 1], 2).astype(jnp.float32)
    stream_u = velocity[:, 0].astype(jnp.float32)
    dv_dx = (
        8.0 * (span_v[:, 3 : rows + 3] - span_v[:, 1 : rows + 1])
        - (span_v[:, 4:] - span_v[:, :rows])
    ) / 12.0
    vorticity = (dv_dx - spanwise(stream_u)).astype(jnp.bfloat16)
    blocks = lax.axis_size("tm")
    cols = vorticity.shape[2]
    width = cols // blocks
    vort_x = jnp.swapaxes(vorticity, 0, 1)
    modes = jnp.swapaxes(front(vort_x), 0, 1)
    return (vorticity, modes)


def solution(mesh):
    in_specs = (P("tm", None, "space", None),)
    out_specs = (P("tm", "space", None), P("tm", "space", None))
    return jax.shard_map(local, mesh=mesh, in_specs=in_specs, out_specs=out_specs, check_vma=False)
```

```python
import functools

import jax
import jax.numpy as jnp
from jax import lax
from jax.experimental import pallas as pl
from jax.experimental.pallas import tpu as pltpu
from jax.sharding import PartitionSpec as P

RANK = 32
HIGH = lax.Precision.HIGHEST


def halo_rows(block, width):
    count = lax.axis_size("space")
    forward = [(i, (i + 1) % count) for i in range(count)]
    backward = [(target, source) for source, target in forward]
    rows = block.shape[1]
    low = lax.ppermute(block[:, rows - width :], "space", forward)
    high = lax.ppermute(block[:, :width], "space", backward)
    return jnp.concatenate([low, block, high], axis=1)


def spanwise(field):
    ahead = jnp.roll(field, -1, 2)
    behind = jnp.roll(field, 1, 2)
    ahead_two = jnp.roll(field, -2, 2)
    behind_two = jnp.roll(field, 2, 2)
    return (8.0 * (ahead - behind) - (ahead_two - behind_two)) / 12.0


MESH = pl.DeviceIdType.MESH


def greet_all(n_space, n_tm):
    s = lax.axis_index("space")
    t = lax.axis_index("tm")
    barrier = pltpu.get_barrier_semaphore()

    def greet_space(k, carry):
        b = lax.rem(s + k, n_space)
        pl.semaphore_signal(barrier, inc=1, device_id=(b, t), device_id_type=MESH)
        return carry

    def greet_tm(k, carry):
        a = lax.rem(t + k, n_tm)
        pl.semaphore_signal(barrier, inc=1, device_id=(s, a), device_id_type=MESH)
        return carry

    lax.fori_loop(1, n_space, greet_space, 0)
    lax.fori_loop(1, n_tm, greet_tm, 0)
    pl.semaphore_wait(barrier, (n_space - 1) + (n_tm - 1))


def allreduce_body(n_space, n_tm, g_ref, out_ref, buf1, buf2, buf3, send1, recv1, send2, recv2, send3, recv3):
    s = lax.axis_index("space")
    t = lax.axis_index("tm")

    def space_copy(src, dst_buf, send, recv, k):
        b = lax.rem(s + k, n_space)
        return pltpu.make_async_remote_copy(
            src_ref=src(b), dst_ref=dst_buf.at[s], send_sem=send.at[k], recv_sem=recv.at[s],
            device_id=(b, t), device_id_type=MESH,
        )

    def space_wait(dst_buf, send, recv, k):
        j = lax.rem(s + k, n_space)
        pltpu.make_async_remote_copy(
            src_ref=dst_buf.at[j], dst_ref=dst_buf.at[j], send_sem=send.at[k], recv_sem=recv.at[j],
            device_id=(j, t), device_id_type=MESH,
        ).wait_recv()

    def send_p1(k, carry):
        space_copy(lambda b: g_ref.at[b], buf1, send1, recv1, k).start()
        return carry

    lax.fori_loop(1, n_space, send_p1, 0)
    buf1[s] = g_ref[s]

    def wait_p1(k, carry):
        space_wait(buf1, send1, recv1, k)
        return carry

    lax.fori_loop(1, n_space, wait_p1, 0)
    acc = buf1[0]
    for j in range(1, n_space):
        acc = acc + buf1[j]
    buf2[t] = acc

    copies = []
    for k in range(1, n_tm):
        a = lax.rem(t + k, n_tm)
        c = pltpu.make_async_remote_copy(
            src_ref=buf2.at[t], dst_ref=buf2.at[t], send_sem=send2.at[k], recv_sem=recv2.at[t],
            device_id=(s, a), device_id_type=MESH,
        )
        c.start()
        copies.append(c)
    for k in range(1, n_tm):
        j = lax.rem(t + k, n_tm)
        pltpu.make_async_remote_copy(
            src_ref=buf2.at[j], dst_ref=buf2.at[j], send_sem=send2.at[k], recv_sem=recv2.at[j],
            device_id=(s, j), device_id_type=MESH,
        ).wait_recv()
    for c in copies:
        c.wait_send()
    acc = buf2[0]
    for j in range(1, n_tm):
        acc = acc + buf2[j]
    buf3[s] = acc

    def send_p3(k, carry):
        space_copy(lambda b: buf3.at[s], buf3, send3, recv3, k).start()
        return carry

    lax.fori_loop(1, n_space, send_p3, 0)

    def wait_p3(k, carry):
        space_wait(buf3, send3, recv3, k)
        return carry

    lax.fori_loop(1, n_space, wait_p3, 0)

    def drain(k, carry):
        space_copy(lambda b: g_ref.at[b], buf1, send1, recv1, k).wait_send()
        space_copy(lambda b: buf3.at[s], buf3, send3, recv3, k).wait_send()
        return carry

    lax.fori_loop(1, n_space, drain, 0)
    out_ref[...] = buf3[...]


def a2a_body(n_tm, src_at, dst_at, x_ref, buf, send, recv, own):
    s = lax.axis_index("space")
    t = lax.axis_index("tm")
    copies = []
    for k in range(1, n_tm):
        a = lax.rem(t + k, n_tm)
        c = pltpu.make_async_remote_copy(
            src_ref=src_at(x_ref, a), dst_ref=dst_at(buf, t), send_sem=send.at[k], recv_sem=recv.at[t],
            device_id=(s, a), device_id_type=MESH,
        )
        c.start()
        copies.append(c)
    mine = pltpu.make_async_copy(src_at(x_ref, t), dst_at(buf, t), own.at[0])
    mine.start()
    mine.wait()
    for k in range(1, n_tm):
        j = lax.rem(t + k, n_tm)
        pltpu.make_async_remote_copy(
            src_ref=src_at(x_ref, j), dst_ref=dst_at(buf, j), send_sem=send.at[k], recv_sem=recv.at[j],
            device_id=(s, j), device_id_type=MESH,
        ).wait_recv()
    for c in copies:
        c.wait_send()


def front_kernel(n_space, n_tm, x_ref, modes_ref, cells, gpart, buf1, buf2, buf3, gfull, part, gathered, *sems):
    send, recv, own = sems[:3]
    greet_all(n_space, n_tm)
    rows, _, cols = x_ref.shape
    width = cols // n_tm
    a2a_body(
        n_tm,
        lambda ref, a: ref.at[:, :, lanes(a, width)],
        lambda ref, j: ref.at[:, pl.ds(j * RANK, RANK), :],
        x_ref, cells, send, recv, own,
    )
    size = cells.shape[1]
    gram = jnp.zeros((size, size), jnp.float32)
    for x in range(rows):
        w = cells[x]
        gram = gram + lax.dot_general(
            w, w, (((1,), (1,)), ((), ())), preferred_element_type=jnp.float32
        )
    gpart[...] = gram.reshape(gpart.shape)
    allreduce_body(n_space, n_tm, gpart, buf1, buf1, buf2, buf3, *sems[3:9])
    gfull[...] = buf3[...].reshape(gfull.shape)
    finish_body(n_tm, gfull, cells, modes_ref, part, gathered, *sems[9:])


def front(vort_x):
    n_space = lax.axis_size("space")
    n_tm = lax.axis_size("tm")
    rows, _, cols = vort_x.shape
    size = n_tm * RANK
    width = cols // n_tm
    cells_shape = (rows, size, width)
    chunks = (n_space, size // n_space, size)
    out_shape = (RANK // n_tm, rows, cols)
    return pl.pallas_call(
        functools.partial(front_kernel, n_space, n_tm),
        out_shape=jax.ShapeDtypeStruct(out_shape, jnp.float32),
        in_specs=[pl.BlockSpec(memory_space=pltpu.VMEM)],
        out_specs=pl.BlockSpec(memory_space=pltpu.VMEM),
        scratch_shapes=[
            pltpu.VMEM(cells_shape, vort_x.dtype),
            pltpu.VMEM(chunks, jnp.float32),
            pltpu.VMEM(chunks, jnp.float32),
            pltpu.VMEM((n_tm,) + chunks[1:], jnp.float32),
            pltpu.VMEM(chunks, jnp.float32),
            pltpu.VMEM((size, size), jnp.float32),
            pltpu.VMEM((RANK, rows, width), jnp.float32),
            pltpu.VMEM(out_shape, jnp.float32),
            pltpu.SemaphoreType.DMA((n_tm,)),
            pltpu.SemaphoreType.DMA((n_tm,)),
            pltpu.SemaphoreType.DMA((1,)),
            pltpu.SemaphoreType.DMA((n_space,)),
            pltpu.SemaphoreType.DMA((n_space,)),
            pltpu.SemaphoreType.DMA((n_tm,)),
            pltpu.SemaphoreType.DMA((n_tm,)),
            pltpu.SemaphoreType.DMA((n_space,)),
            pltpu.SemaphoreType.DMA((n_space,)),
            pltpu.SemaphoreType.DMA((n_tm,)),
            pltpu.SemaphoreType.DMA((n_tm,)),
            pltpu.SemaphoreType.DMA((1,)),
        ],
        compiler_params=pltpu.CompilerParams(collective_id=0, has_side_effects=True),
    )(vort_x)


def lanes(a, width):
    return pl.ds(pl.multiple_of(a * width, width), width)


def bdot(x, y):
    return jnp.einsum("nab,nbc->nac", x, y, precision=HIGH, preferred_element_type=jnp.float32)


def bdot_t(x, y):
    return jnp.einsum("nac,nbc->nab", x, y, precision=HIGH, preferred_element_type=jnp.float32)


def iotas(shape):
    return lax.broadcasted_iota(jnp.int32, shape, 1), lax.broadcasted_iota(jnp.int32, shape, 2)


def merge_coeffs(h):
    n = h.shape[0]
    kt = h[:, :RANK, :] + h[:, RANK:, :]
    row, col = iotas(h.shape)
    dcol = jnp.sum(jnp.where(row == col, h, 0.0), axis=2, keepdims=True)
    scales = jnp.sqrt(dcol[:, :RANK] + dcol[:, RANK:])
    inner = bdot_t(bdot(kt, h), kt)
    row, col = iotas(inner.shape)

    a = inner
    r = kt
    below = row[:, :, :1]
    for j in range(RANK):
        a_row = a[:, j : j + 1, :]
        r_row = r[:, j : j + 1, :]
        factor = jnp.where(below > j, a[:, :, j : j + 1] / a_row[:, :, j : j + 1], 0.0)
        a = a - factor * a_row
        r = r - factor * r_row
    diag_u = jnp.sum(jnp.where(row == col, a, 0.0), axis=2, keepdims=True)
    return r * (scales / jnp.sqrt(diag_u))


def split3(x):
    hi = x.astype(jnp.bfloat16)
    rest = x - hi.astype(jnp.float32)
    mid = rest.astype(jnp.bfloat16)
    lo = (rest - mid.astype(jnp.float32)).astype(jnp.bfloat16)
    return hi, mid, lo


def place(x, offset, width):
    n, r, w = x.shape
    row, col = iotas((n, w, width))
    pick = jnp.where(col == row + offset, 1.0, 0.0).astype(jnp.bfloat16)
    terms = jnp.einsum(
        "nab,nbc->nac", jnp.concatenate(split3(x), axis=1), pick, preferred_element_type=jnp.float32
    )
    return (terms[:, :r] + terms[:, r : 2 * r]) + terms[:, 2 * r :]


def tree_levels(g_ref):
    size = 2 * RANK
    leaves = g_ref.shape[0] // RANK
    picks = []
    for k in range(leaves // 2):
        lane0 = (k * size) // 128 * 128
        block = g_ref[k * size : (k + 1) * size, lane0 : lane0 + 128][None]
        picks.append(place(block, -(k * size - lane0), size))
    basis = merge_coeffs(jnp.concatenate(picks, axis=0))
    while basis.shape[0] > 1:
        n = basis.shape[0] // 2
        w = basis.shape[2]
        pairs = basis.reshape(n, 2, RANK, w)
        bt = jnp.concatenate(
            [place(pairs[:, 0], 0, 2 * w), place(pairs[:, 1], w, 2 * w)], axis=1
        )
        gs = jnp.concatenate(
            [g_ref[k * 2 * w : (k + 1) * 2 * w, k * 2 * w : (k + 1) * 2 * w][None] for k in range(n)],
            axis=0,
        )
        h = bdot_t(bdot(bt, gs), bt)
        basis = bdot(merge_coeffs(h), bt)
    return basis[0]


def finish_body(n_tm, g_ref, w_ref, out_ref, part_ref, buf, send, recv, own):
    s = lax.axis_index("space")
    t = lax.axis_index("tm")
    basis_t = tree_levels(g_ref)
    hi = basis_t.astype(jnp.bfloat16)
    rest = basis_t - hi.astype(jnp.float32)
    mid = rest.astype(jnp.bfloat16)
    lo = (rest - mid.astype(jnp.float32)).astype(jnp.bfloat16)
    pieces = jnp.concatenate([hi, mid, lo], axis=0)
    for x in range(w_ref.shape[0]):
        terms = jnp.dot(pieces, w_ref[x], preferred_element_type=jnp.float32)
        part_ref[:, x, :] = (terms[:RANK] + terms[RANK : 2 * RANK]) + terms[2 * RANK :]
    share = part_ref.shape[0] // n_tm
    width = w_ref.shape[2]
    src_at = lambda a: part_ref.at[pl.ds(a * share, share)]
    dst_at = lambda j: buf.at[:, :, lanes(j, width)]
    copies = []
    for k in range(1, n_tm):
        a = lax.rem(t + k, n_tm)
        c = pltpu.make_async_remote_copy(
            src_ref=src_at(a), dst_ref=dst_at(t), send_sem=send.at[k], recv_sem=recv.at[t],
            device_id=(s, a), device_id_type=MESH,
        )
        c.start()
        copies.append(c)
    mine = pltpu.make_async_copy(src_at(t), dst_at(t), own.at[0])
    mine.start()
    mine.wait()
    for k in range(1, n_tm):
        j = lax.rem(t + k, n_tm)
        pltpu.make_async_remote_copy(
            src_ref=src_at(j), dst_ref=dst_at(j), send_sem=send.at[k], recv_sem=recv.at[j],
            device_id=(s, j), device_id_type=MESH,
        ).wait_recv()
    for c in copies:
        c.wait_send()
    out_ref[...] = buf[...]


def local(velocity):
    rows = velocity.shape[2]
    span_v = halo_rows(velocity[:, 1], 2).astype(jnp.float32)
    stream_u = velocity[:, 0].astype(jnp.float32)
    dv_dx = (
        8.0 * (span_v[:, 3 : rows + 3] - span_v[:, 1 : rows + 1])
        - (span_v[:, 4:] - span_v[:, :rows])
    ) / 12.0
    vorticity = (dv_dx - spanwise(stream_u)).astype(jnp.bfloat16)
    blocks = lax.axis_size("tm")
    cols = vorticity.shape[2]
    width = cols // blocks
    vort_x = jnp.swapaxes(vorticity, 0, 1)
    modes = front(vort_x)
    return (vorticity, modes)


def solution(mesh):
    in_specs = (P("tm", None, "space", None),)
    out_specs = (P("tm", "space", None), P("tm", "space", None))
    return jax.shard_map(local, mesh=mesh, in_specs=in_specs, out_specs=out_specs, check_vma=False)
```

```python
import functools

import jax
import jax.numpy as jnp
from jax import lax
from jax.experimental import pallas as pl
from jax.experimental.pallas import tpu as pltpu
from jax.sharding import PartitionSpec as P

RANK = 32
HIGH = lax.Precision.HIGHEST


def halo_rows(block, width):
    count = lax.axis_size("space")
    forward = [(i, (i + 1) % count) for i in range(count)]
    backward = [(target, source) for source, target in forward]
    rows = block.shape[1]
    low = lax.ppermute(block[:, rows - width :], "space", forward)
    high = lax.ppermute(block[:, :width], "space", backward)
    return jnp.concatenate([low, block, high], axis=1)


def spanwise(field):
    ahead = jnp.roll(field, -1, 2)
    behind = jnp.roll(field, 1, 2)
    ahead_two = jnp.roll(field, -2, 2)
    behind_two = jnp.roll(field, 2, 2)
    return (8.0 * (ahead - behind) - (ahead_two - behind_two)) / 12.0


MESH = pl.DeviceIdType.MESH


def greet_all(n_space, n_tm):
    s = lax.axis_index("space")
    t = lax.axis_index("tm")
    barrier = pltpu.get_barrier_semaphore()

    def greet_space(k, carry):
        b = lax.rem(s + k, n_space)
        pl.semaphore_signal(barrier, inc=1, device_id=(b, t), device_id_type=MESH)
        return carry

    def greet_tm(k, carry):
        a = lax.rem(t + k, n_tm)
        pl.semaphore_signal(barrier, inc=1, device_id=(s, a), device_id_type=MESH)
        return carry

    lax.fori_loop(1, n_space, greet_space, 0)
    lax.fori_loop(1, n_tm, greet_tm, 0)
    pl.semaphore_wait(barrier, (n_space - 1) + (n_tm - 1))


def allreduce_body(n_space, n_tm, g_ref, out_ref, buf1, buf2, buf3, send1, recv1, send2, recv2, send3, recv3):
    s = lax.axis_index("space")
    t = lax.axis_index("tm")

    def space_copy(src, dst_buf, send, recv, k):
        b = lax.rem(s + k, n_space)
        return pltpu.make_async_remote_copy(
            src_ref=src(b), dst_ref=dst_buf.at[s], send_sem=send.at[k], recv_sem=recv.at[s],
            device_id=(b, t), device_id_type=MESH,
        )

    def space_wait(dst_buf, send, recv, k):
        j = lax.rem(s + k, n_space)
        pltpu.make_async_remote_copy(
            src_ref=dst_buf.at[j], dst_ref=dst_buf.at[j], send_sem=send.at[k], recv_sem=recv.at[j],
            device_id=(j, t), device_id_type=MESH,
        ).wait_recv()

    def send_p1(k, carry):
        space_copy(lambda b: g_ref.at[b], buf1, send1, recv1, k).start()
        return carry

    lax.fori_loop(1, n_space, send_p1, 0)
    buf1[s] = g_ref[s]

    def wait_p1(k, carry):
        space_wait(buf1, send1, recv1, k)
        return carry

    lax.fori_loop(1, n_space, wait_p1, 0)
    acc = buf1[0]
    for j in range(1, n_space):
        acc = acc + buf1[j]
    buf2[t] = acc

    copies = []
    for k in range(1, n_tm):
        a = lax.rem(t + k, n_tm)
        c = pltpu.make_async_remote_copy(
            src_ref=buf2.at[t], dst_ref=buf2.at[t], send_sem=send2.at[k], recv_sem=recv2.at[t],
            device_id=(s, a), device_id_type=MESH,
        )
        c.start()
        copies.append(c)
    for k in range(1, n_tm):
        j = lax.rem(t + k, n_tm)
        pltpu.make_async_remote_copy(
            src_ref=buf2.at[j], dst_ref=buf2.at[j], send_sem=send2.at[k], recv_sem=recv2.at[j],
            device_id=(s, j), device_id_type=MESH,
        ).wait_recv()
    for c in copies:
        c.wait_send()
    acc = buf2[0]
    for j in range(1, n_tm):
        acc = acc + buf2[j]
    buf3[s] = acc

    def send_p3(k, carry):
        space_copy(lambda b: buf3.at[s], buf3, send3, recv3, k).start()
        return carry

    lax.fori_loop(1, n_space, send_p3, 0)

    def wait_p3(k, carry):
        space_wait(buf3, send3, recv3, k)
        return carry

    lax.fori_loop(1, n_space, wait_p3, 0)

    def drain(k, carry):
        space_copy(lambda b: g_ref.at[b], buf1, send1, recv1, k).wait_send()
        space_copy(lambda b: buf3.at[s], buf3, send3, recv3, k).wait_send()
        return carry

    lax.fori_loop(1, n_space, drain, 0)
    out_ref[...] = buf3[...]


def a2a_body(n_tm, src_at, dst_at, x_ref, buf, send, recv, own):
    s = lax.axis_index("space")
    t = lax.axis_index("tm")
    copies = []
    for k in range(1, n_tm):
        a = lax.rem(t + k, n_tm)
        c = pltpu.make_async_remote_copy(
            src_ref=src_at(x_ref, a), dst_ref=dst_at(buf, t), send_sem=send.at[k], recv_sem=recv.at[t],
            device_id=(s, a), device_id_type=MESH,
        )
        c.start()
        copies.append(c)
    mine = pltpu.make_async_copy(src_at(x_ref, t), dst_at(buf, t), own.at[0])
    mine.start()
    mine.wait()
    for k in range(1, n_tm):
        j = lax.rem(t + k, n_tm)
        pltpu.make_async_remote_copy(
            src_ref=src_at(x_ref, j), dst_ref=dst_at(buf, j), send_sem=send.at[k], recv_sem=recv.at[j],
            device_id=(s, j), device_id_type=MESH,
        ).wait_recv()
    for c in copies:
        c.wait_send()


def fix_edges(vloc_ref, dudz_ref, halo, fix):
    f = lambda ref, i: ref[i].astype(jnp.float32)
    d = lambda ahead, behind, ahead_two, behind_two: (8.0 * (ahead - behind) - (ahead_two - behind_two)) / 12.0
    v = [f(vloc_ref, i) for i in range(8)]
    lo = [f(halo, 0), f(halo, 1)]
    hi = [f(halo, 2), f(halo, 3)]
    rows_dv = [
        d(v[1], lo[1], v[2], lo[0]),
        d(v[2], v[0], v[3], lo[1]),
        d(v[7], v[5], hi[0], v[4]),
        d(hi[0], v[6], hi[1], v[5]),
    ]
    for i in range(4):
        fix[i] = (rows_dv[i] - dudz_ref[i]).astype(fix.dtype)


def front_kernel(
    n_space, n_tm, x_ref, vloc_ref, dudz_ref, modes_ref, fixed_ref,
    cells, gpart, buf1, buf2, buf3, gfull, part, gathered, halo, fix, *sems,
):
    send, recv, own, esend, hsend, hrecv = sems[:6]
    s = lax.axis_index("space")
    t = lax.axis_index("tm")
    greet_all(n_space, n_tm)
    rows, _, cols = x_ref.shape
    width = cols // n_tm
    left = lax.rem(s + n_space - 1, n_space)
    right = lax.rem(s + 1, n_space)

    def remote(src_ref, dst_ref, ss, rs, dev):
        return pltpu.make_async_remote_copy(
            src_ref=src_ref, dst_ref=dst_ref, send_sem=ss, recv_sem=rs, device_id=dev, device_id_type=MESH
        )

    halo_out = [
        remote(vloc_ref.at[pl.ds(6, 2)], halo.at[pl.ds(0, 2)], hsend.at[0], hrecv.at[0], (right, t)),
        remote(vloc_ref.at[pl.ds(0, 2)], halo.at[pl.ds(2, 2)], hsend.at[1], hrecv.at[1], (left, t)),
    ]
    for c in halo_out:
        c.start()
    src = lambda ref, a, r0, nr: ref.at[pl.ds(r0, nr), :, lanes(a, width)]
    dst = lambda j, r0, nr: cells.at[pl.ds(r0, nr), pl.ds(j * RANK, RANK), :]
    inner = rows - 4
    copies = []
    for k in range(1, n_tm):
        a = lax.rem(t + k, n_tm)
        c = remote(src(x_ref, a, 2, inner), dst(t, 2, inner), send.at[k], recv.at[t], (s, a))
        c.start()
        copies.append(c)
    mine = pltpu.make_async_copy(src(x_ref, t, 2, inner), dst(t, 2, inner), own.at[0])
    mine.start()
    mine.wait()
    remote(vloc_ref.at[pl.ds(6, 2)], halo.at[pl.ds(0, 2)], hsend.at[0], hrecv.at[0], (left, t)).wait_recv()
    remote(vloc_ref.at[pl.ds(0, 2)], halo.at[pl.ds(2, 2)], hsend.at[1], hrecv.at[1], (right, t)).wait_recv()
    fix_edges(vloc_ref, dudz_ref, halo, fix)
    fixed_ref[...] = fix[...]
    for k in range(1, n_tm):
        a = lax.rem(t + k, n_tm)
        for e, (r0, d0) in enumerate(((0, 0), (2, rows - 2))):
            c = remote(src(fix, a, r0, 2), dst(t, d0, 2), esend.at[k, e], recv.at[t], (s, a))
            c.start()
            copies.append(c)
    for r0, d0 in ((0, 0), (2, rows - 2)):
        mine = pltpu.make_async_copy(src(fix, t, r0, 2), dst(t, d0, 2), own.at[0])
        mine.start()
        mine.wait()
    for k in range(1, n_tm):
        j = lax.rem(t + k, n_tm)
        remote(src(x_ref, j, 0, rows), dst(j, 0, rows), send.at[k], recv.at[j], (s, j)).wait_recv()
    for c in copies + halo_out:
        c.wait_send()
    size = cells.shape[1]
    gram = jnp.zeros((size, size), jnp.float32)
    for x in range(rows):
        w = cells[x]
        gram = gram + lax.dot_general(
            w, w, (((1,), (1,)), ((), ())), preferred_element_type=jnp.float32
        )
    gpart[...] = gram.reshape(gpart.shape)
    allreduce_body(n_space, n_tm, gpart, buf1, buf1, buf2, buf3, *sems[6:12])
    gfull[...] = buf3[...].reshape(gfull.shape)
    finish_body(n_tm, gfull, cells, modes_ref, part, gathered, *sems[12:])


def front(vort_x, vloc, dudz):
    n_space = lax.axis_size("space")
    n_tm = lax.axis_size("tm")
    rows, _, cols = vort_x.shape
    size = n_tm * RANK
    width = cols // n_tm
    cells_shape = (rows, size, width)
    chunks = (n_space, size // n_space, size)
    out_shape = (rows, RANK // n_tm, cols)
    edge_shape = (4, RANK, cols)
    return pl.pallas_call(
        functools.partial(front_kernel, n_space, n_tm),
        out_shape=(
            jax.ShapeDtypeStruct(out_shape, jnp.float32),
            jax.ShapeDtypeStruct(edge_shape, vort_x.dtype),
        ),
        in_specs=[pl.BlockSpec(memory_space=pltpu.VMEM)] * 3,
        out_specs=(pl.BlockSpec(memory_space=pltpu.VMEM), pl.BlockSpec(memory_space=pltpu.VMEM)),
        scratch_shapes=[
            pltpu.VMEM(cells_shape, vort_x.dtype),
            pltpu.VMEM(chunks, jnp.float32),
            pltpu.VMEM(chunks, jnp.float32),
            pltpu.VMEM((n_tm,) + chunks[1:], jnp.float32),
            pltpu.VMEM(chunks, jnp.float32),
            pltpu.VMEM((size, size), jnp.float32),
            pltpu.VMEM((rows, RANK, width), jnp.float32),
            pltpu.VMEM(out_shape, jnp.float32),
            pltpu.VMEM(edge_shape, vort_x.dtype),
            pltpu.VMEM(edge_shape, vort_x.dtype),
            pltpu.SemaphoreType.DMA((n_tm,)),
            pltpu.SemaphoreType.DMA((n_tm,)),
            pltpu.SemaphoreType.DMA((1,)),
            pltpu.SemaphoreType.DMA((n_tm, 2)),
            pltpu.SemaphoreType.DMA((2,)),
            pltpu.SemaphoreType.DMA((2,)),
            pltpu.SemaphoreType.DMA((n_space,)),
            pltpu.SemaphoreType.DMA((n_space,)),
            pltpu.SemaphoreType.DMA((n_tm,)),
            pltpu.SemaphoreType.DMA((n_tm,)),
            pltpu.SemaphoreType.DMA((n_space,)),
            pltpu.SemaphoreType.DMA((n_space,)),
            pltpu.SemaphoreType.DMA((n_tm,)),
            pltpu.SemaphoreType.DMA((n_tm,)),
            pltpu.SemaphoreType.DMA((1,)),
        ],
        compiler_params=pltpu.CompilerParams(collective_id=0, has_side_effects=True),
    )(vort_x, vloc, dudz)


def lanes(a, width):
    return pl.ds(pl.multiple_of(a * width, width), width)


def bdot(x, y):
    return jnp.einsum("nab,nbc->nac", x, y, precision=HIGH, preferred_element_type=jnp.float32)


def bdot_t(x, y):
    return jnp.einsum("nac,nbc->nab", x, y, precision=HIGH, preferred_element_type=jnp.float32)


def iotas(shape):
    return lax.broadcasted_iota(jnp.int32, shape, 1), lax.broadcasted_iota(jnp.int32, shape, 2)


def merge_coeffs(h):
    n = h.shape[0]
    kt = h[:, :RANK, :] + h[:, RANK:, :]
    row, col = iotas(h.shape)
    dcol = jnp.sum(jnp.where(row == col, h, 0.0), axis=2, keepdims=True)
    scales = jnp.sqrt(dcol[:, :RANK] + dcol[:, RANK:])
    inner = bdot_t(bdot(kt, h), kt)
    row, col = iotas(inner.shape)

    a = inner
    r = kt
    below = row[:, :, :1]
    for j in range(RANK):
        a_row = a[:, j : j + 1, :]
        r_row = r[:, j : j + 1, :]
        factor = jnp.where(below > j, a[:, :, j : j + 1] / a_row[:, :, j : j + 1], 0.0)
        a = a - factor * a_row
        r = r - factor * r_row
    diag_u = jnp.sum(jnp.where(row == col, a, 0.0), axis=2, keepdims=True)
    return r * (scales / jnp.sqrt(diag_u))


def split3(x):
    hi = x.astype(jnp.bfloat16)
    rest = x - hi.astype(jnp.float32)
    mid = rest.astype(jnp.bfloat16)
    lo = (rest - mid.astype(jnp.float32)).astype(jnp.bfloat16)
    return hi, mid, lo


def place(x, offset, width):
    n, r, w = x.shape
    row, col = iotas((n, w, width))
    pick = jnp.where(col == row + offset, 1.0, 0.0).astype(jnp.bfloat16)
    terms = jnp.einsum(
        "nab,nbc->nac", jnp.concatenate(split3(x), axis=1), pick, preferred_element_type=jnp.float32
    )
    return (terms[:, :r] + terms[:, r : 2 * r]) + terms[:, 2 * r :]


def tree_levels(g_ref):
    size = 2 * RANK
    leaves = g_ref.shape[0] // RANK
    picks = []
    for k in range(leaves // 2):
        lane0 = (k * size) // 128 * 128
        block = g_ref[k * size : (k + 1) * size, lane0 : lane0 + 128][None]
        picks.append(place(block, -(k * size - lane0), size))
    basis = merge_coeffs(jnp.concatenate(picks, axis=0))
    while basis.shape[0] > 1:
        n = basis.shape[0] // 2
        w = basis.shape[2]
        pairs = basis.reshape(n, 2, RANK, w)
        bt = jnp.concatenate(
            [place(pairs[:, 0], 0, 2 * w), place(pairs[:, 1], w, 2 * w)], axis=1
        )
        gs = jnp.concatenate(
            [g_ref[k * 2 * w : (k + 1) * 2 * w, k * 2 * w : (k + 1) * 2 * w][None] for k in range(n)],
            axis=0,
        )
        h = bdot_t(bdot(bt, gs), bt)
        basis = bdot(merge_coeffs(h), bt)
    return basis[0]


def finish_body(n_tm, g_ref, w_ref, out_ref, part_ref, buf, send, recv, own):
    s = lax.axis_index("space")
    t = lax.axis_index("tm")
    basis_t = tree_levels(g_ref)
    hi = basis_t.astype(jnp.bfloat16)
    rest = basis_t - hi.astype(jnp.float32)
    mid = rest.astype(jnp.bfloat16)
    lo = (rest - mid.astype(jnp.float32)).astype(jnp.bfloat16)
    pieces = jnp.concatenate([hi, mid, lo], axis=0)
    for x in range(w_ref.shape[0]):
        terms = jnp.dot(pieces, w_ref[x], preferred_element_type=jnp.float32)
        part_ref[x] = (terms[:RANK] + terms[RANK : 2 * RANK]) + terms[2 * RANK :]
    share = part_ref.shape[1] // n_tm
    width = w_ref.shape[2]
    src_at = lambda a: part_ref.at[:, pl.ds(a * share, share), :]
    dst_at = lambda j: buf.at[:, :, lanes(j, width)]
    copies = []
    for k in range(1, n_tm):
        a = lax.rem(t + k, n_tm)
        c = pltpu.make_async_remote_copy(
            src_ref=src_at(a), dst_ref=dst_at(t), send_sem=send.at[k], recv_sem=recv.at[t],
            device_id=(s, a), device_id_type=MESH,
        )
        c.start()
        copies.append(c)
    mine = pltpu.make_async_copy(src_at(t), dst_at(t), own.at[0])
    mine.start()
    mine.wait()
    for k in range(1, n_tm):
        j = lax.rem(t + k, n_tm)
        pltpu.make_async_remote_copy(
            src_ref=src_at(j), dst_ref=dst_at(j), send_sem=send.at[k], recv_sem=recv.at[j],
            device_id=(s, j), device_id_type=MESH,
        ).wait_recv()
    for c in copies:
        c.wait_send()
    out_ref[...] = buf[...]


def local(velocity):
    rows = velocity.shape[2]
    span_v = velocity[:, 1].astype(jnp.float32)
    stream_u = velocity[:, 0].astype(jnp.float32)
    du_dz = spanwise(stream_u)
    dv_dx = (
        8.0 * (jnp.roll(span_v, -1, 1) - jnp.roll(span_v, 1, 1))
        - (jnp.roll(span_v, -2, 1) - jnp.roll(span_v, 2, 1))
    ) / 12.0
    local_vort = (dv_dx - du_dz).astype(jnp.bfloat16)
    edge = [0, 1, rows - 2, rows - 1]
    vloc = jnp.swapaxes(velocity[:, 1][:, [0, 1, 2, 3, rows - 4, rows - 3, rows - 2, rows - 1]], 0, 1)
    dudz = jnp.swapaxes(du_dz[:, edge], 0, 1)
    modes, fixed = front(jnp.swapaxes(local_vort, 0, 1), vloc, dudz)
    vorticity = local_vort.at[:, edge].set(jnp.swapaxes(fixed, 0, 1))
    return (vorticity, jnp.swapaxes(modes, 0, 1))


def solution(mesh):
    in_specs = (P("tm", None, "space", None),)
    out_specs = (P("tm", "space", None), P("tm", "space", None))
    return jax.shard_map(local, mesh=mesh, in_specs=in_specs, out_specs=out_specs, check_vma=False)
```

```python
import functools

import jax
import jax.numpy as jnp
from jax import lax
from jax.experimental import pallas as pl
from jax.experimental.pallas import tpu as pltpu
from jax.sharding import PartitionSpec as P

RANK = 32
HIGH = lax.Precision.HIGHEST


def halo_rows(block, width):
    count = lax.axis_size("space")
    forward = [(i, (i + 1) % count) for i in range(count)]
    backward = [(target, source) for source, target in forward]
    rows = block.shape[1]
    low = lax.ppermute(block[:, rows - width :], "space", forward)
    high = lax.ppermute(block[:, :width], "space", backward)
    return jnp.concatenate([low, block, high], axis=1)


def spanwise(field):
    ahead = jnp.roll(field, -1, 2)
    behind = jnp.roll(field, 1, 2)
    ahead_two = jnp.roll(field, -2, 2)
    behind_two = jnp.roll(field, 2, 2)
    return (8.0 * (ahead - behind) - (ahead_two - behind_two)) / 12.0


MESH = pl.DeviceIdType.MESH


def greet_all(n_space, n_tm):
    s = lax.axis_index("space")
    t = lax.axis_index("tm")
    barrier = pltpu.get_barrier_semaphore()

    def greet_space(k, carry):
        b = lax.rem(s + k, n_space)
        pl.semaphore_signal(barrier, inc=1, device_id=(b, t), device_id_type=MESH)
        return carry

    def greet_tm(k, carry):
        a = lax.rem(t + k, n_tm)
        pl.semaphore_signal(barrier, inc=1, device_id=(s, a), device_id_type=MESH)
        return carry

    lax.fori_loop(1, n_space, greet_space, 0)
    lax.fori_loop(1, n_tm, greet_tm, 0)
    pl.semaphore_wait(barrier, (n_space - 1) + (n_tm - 1))


def allreduce_body(n_space, n_tm, g_ref, out_ref, buf1, buf2, buf3, send1, recv1, send2, recv2, send3, recv3):
    s = lax.axis_index("space")
    t = lax.axis_index("tm")

    def space_copy(src, dst_buf, send, recv, k):
        b = lax.rem(s + k, n_space)
        return pltpu.make_async_remote_copy(
            src_ref=src(b), dst_ref=dst_buf.at[s], send_sem=send.at[k], recv_sem=recv.at[s],
            device_id=(b, t), device_id_type=MESH,
        )

    def space_wait(dst_buf, send, recv, k):
        j = lax.rem(s + k, n_space)
        pltpu.make_async_remote_copy(
            src_ref=dst_buf.at[j], dst_ref=dst_buf.at[j], send_sem=send.at[k], recv_sem=recv.at[j],
            device_id=(j, t), device_id_type=MESH,
        ).wait_recv()

    def send_p1(k, carry):
        space_copy(lambda b: g_ref.at[b], buf1, send1, recv1, k).start()
        return carry

    lax.fori_loop(1, n_space, send_p1, 0)
    buf1[s] = g_ref[s]

    def wait_p1(k, carry):
        space_wait(buf1, send1, recv1, k)
        return carry

    lax.fori_loop(1, n_space, wait_p1, 0)
    acc = buf1[0]
    for j in range(1, n_space):
        acc = acc + buf1[j]
    buf2[t] = acc

    copies = []
    for k in range(1, n_tm):
        a = lax.rem(t + k, n_tm)
        c = pltpu.make_async_remote_copy(
            src_ref=buf2.at[t], dst_ref=buf2.at[t], send_sem=send2.at[k], recv_sem=recv2.at[t],
            device_id=(s, a), device_id_type=MESH,
        )
        c.start()
        copies.append(c)
    for k in range(1, n_tm):
        j = lax.rem(t + k, n_tm)
        pltpu.make_async_remote_copy(
            src_ref=buf2.at[j], dst_ref=buf2.at[j], send_sem=send2.at[k], recv_sem=recv2.at[j],
            device_id=(s, j), device_id_type=MESH,
        ).wait_recv()
    for c in copies:
        c.wait_send()
    acc = buf2[0]
    for j in range(1, n_tm):
        acc = acc + buf2[j]
    buf3[s] = acc

    def send_p3(k, carry):
        space_copy(lambda b: buf3.at[s], buf3, send3, recv3, k).start()
        return carry

    lax.fori_loop(1, n_space, send_p3, 0)

    def wait_p3(k, carry):
        space_wait(buf3, send3, recv3, k)
        return carry

    lax.fori_loop(1, n_space, wait_p3, 0)

    def drain(k, carry):
        space_copy(lambda b: g_ref.at[b], buf1, send1, recv1, k).wait_send()
        space_copy(lambda b: buf3.at[s], buf3, send3, recv3, k).wait_send()
        return carry

    lax.fori_loop(1, n_space, drain, 0)
    out_ref[...] = buf3[...]


def a2a_body(n_tm, src_at, dst_at, x_ref, buf, send, recv, own):
    s = lax.axis_index("space")
    t = lax.axis_index("tm")
    copies = []
    for k in range(1, n_tm):
        a = lax.rem(t + k, n_tm)
        c = pltpu.make_async_remote_copy(
            src_ref=src_at(x_ref, a), dst_ref=dst_at(buf, t), send_sem=send.at[k], recv_sem=recv.at[t],
            device_id=(s, a), device_id_type=MESH,
        )
        c.start()
        copies.append(c)
    mine = pltpu.make_async_copy(src_at(x_ref, t), dst_at(buf, t), own.at[0])
    mine.start()
    mine.wait()
    for k in range(1, n_tm):
        j = lax.rem(t + k, n_tm)
        pltpu.make_async_remote_copy(
            src_ref=src_at(x_ref, j), dst_ref=dst_at(buf, j), send_sem=send.at[k], recv_sem=recv.at[j],
            device_id=(s, j), device_id_type=MESH,
        ).wait_recv()
    for c in copies:
        c.wait_send()


def fix_edges(vloc_ref, dudz_ref, halo, fix):
    f = lambda ref, i: ref[i].astype(jnp.float32)
    d = lambda ahead, behind, ahead_two, behind_two: (8.0 * (ahead - behind) - (ahead_two - behind_two)) / 12.0
    v = [f(vloc_ref, i) for i in range(8)]
    lo = [f(halo, 0), f(halo, 1)]
    hi = [f(halo, 2), f(halo, 3)]
    rows_dv = [
        d(v[1], lo[1], v[2], lo[0]),
        d(v[2], v[0], v[3], lo[1]),
        d(v[7], v[5], hi[0], v[4]),
        d(hi[0], v[6], hi[1], v[5]),
    ]
    for i in range(4):
        fix[i] = (rows_dv[i] - dudz_ref[i]).astype(fix.dtype)


def front_kernel(
    n_space, n_tm, x_ref, vloc_ref, dudz_ref, modes_ref, fixed_ref,
    cells, gpart, buf1, buf2, buf3, gfull, part, gathered, halo, fix, *sems,
):
    send, recv, own, esend, hsend, hrecv = sems[:6]
    s = lax.axis_index("space")
    t = lax.axis_index("tm")
    greet_all(n_space, n_tm)
    rows, _, cols = x_ref.shape
    width = cols // n_tm
    left = lax.rem(s + n_space - 1, n_space)
    right = lax.rem(s + 1, n_space)

    def remote(src_ref, dst_ref, ss, rs, dev):
        return pltpu.make_async_remote_copy(
            src_ref=src_ref, dst_ref=dst_ref, send_sem=ss, recv_sem=rs, device_id=dev, device_id_type=MESH
        )

    halo_out = [
        remote(vloc_ref.at[pl.ds(6, 2)], halo.at[pl.ds(0, 2)], hsend.at[0], hrecv.at[0], (right, t)),
        remote(vloc_ref.at[pl.ds(0, 2)], halo.at[pl.ds(2, 2)], hsend.at[1], hrecv.at[1], (left, t)),
    ]
    for c in halo_out:
        c.start()
    src = lambda ref, a, r0, nr: ref.at[pl.ds(r0, nr), :, lanes(a, width)]
    dst = lambda j, r0, nr: cells.at[pl.ds(r0, nr), pl.ds(j * RANK, RANK), :]
    inner = rows - 4
    copies = []
    for k in range(1, n_tm):
        a = lax.rem(t + k, n_tm)
        c = remote(src(x_ref, a, 2, inner), dst(t, 2, inner), send.at[k], recv.at[t], (s, a))
        c.start()
        copies.append(c)
    mine = pltpu.make_async_copy(src(x_ref, t, 2, inner), dst(t, 2, inner), own.at[0])
    mine.start()
    mine.wait()
    remote(vloc_ref.at[pl.ds(6, 2)], halo.at[pl.ds(0, 2)], hsend.at[0], hrecv.at[0], (left, t)).wait_recv()
    remote(vloc_ref.at[pl.ds(0, 2)], halo.at[pl.ds(2, 2)], hsend.at[1], hrecv.at[1], (right, t)).wait_recv()
    fix_edges(vloc_ref, dudz_ref, halo, fix)
    fixed_ref[...] = fix[...]
    for k in range(1, n_tm):
        a = lax.rem(t + k, n_tm)
        for e, (r0, d0) in enumerate(((0, 0), (2, rows - 2))):
            c = remote(src(fix, a, r0, 2), dst(t, d0, 2), esend.at[k, e], recv.at[t], (s, a))
            c.start()
            copies.append(c)
    for r0, d0 in ((0, 0), (2, rows - 2)):
        mine = pltpu.make_async_copy(src(fix, t, r0, 2), dst(t, d0, 2), own.at[0])
        mine.start()
        mine.wait()
    for k in range(1, n_tm):
        j = lax.rem(t + k, n_tm)
        remote(src(x_ref, j, 0, rows), dst(j, 0, rows), send.at[k], recv.at[j], (s, j)).wait_recv()
    for c in copies + halo_out:
        c.wait_send()
    size = cells.shape[1]
    gram = jnp.zeros((size, size), jnp.float32)
    for x in range(rows):
        w = cells[x]
        gram = gram + lax.dot_general(
            w, w, (((1,), (1,)), ((), ())), preferred_element_type=jnp.float32
        )
    gpart[...] = gram.reshape(gpart.shape)
    allreduce_body(n_space, n_tm, gpart, buf1, buf1, buf2, buf3, *sems[6:12])
    gfull[...] = buf3[...].reshape(gfull.shape)
    finish_body(n_tm, gfull, cells, modes_ref, part, gathered, *sems[12:])


def front(vort_x, vloc, dudz):
    n_space = lax.axis_size("space")
    n_tm = lax.axis_size("tm")
    rows, _, cols = vort_x.shape
    size = n_tm * RANK
    width = cols // n_tm
    cells_shape = (rows, size, width)
    chunks = (n_space, size // n_space, size)
    out_shape = (rows, RANK // n_tm, cols)
    edge_shape = (4, RANK, cols)
    return pl.pallas_call(
        functools.partial(front_kernel, n_space, n_tm),
        out_shape=(
            jax.ShapeDtypeStruct(out_shape, jnp.float32),
            jax.ShapeDtypeStruct(edge_shape, vort_x.dtype),
        ),
        in_specs=[pl.BlockSpec(memory_space=pltpu.VMEM)] * 3,
        out_specs=(pl.BlockSpec(memory_space=pltpu.VMEM), pl.BlockSpec(memory_space=pltpu.VMEM)),
        scratch_shapes=[
            pltpu.VMEM(cells_shape, vort_x.dtype),
            pltpu.VMEM(chunks, jnp.float32),
            pltpu.VMEM(chunks, jnp.float32),
            pltpu.VMEM((n_tm,) + chunks[1:], jnp.float32),
            pltpu.VMEM(chunks, jnp.float32),
            pltpu.VMEM((size, size), jnp.float32),
            pltpu.VMEM((rows, RANK, width), jnp.float32),
            pltpu.VMEM(out_shape, jnp.float32),
            pltpu.VMEM(edge_shape, vort_x.dtype),
            pltpu.VMEM(edge_shape, vort_x.dtype),
            pltpu.SemaphoreType.DMA((n_tm,)),
            pltpu.SemaphoreType.DMA((n_tm,)),
            pltpu.SemaphoreType.DMA((1,)),
            pltpu.SemaphoreType.DMA((n_tm, 2)),
            pltpu.SemaphoreType.DMA((2,)),
            pltpu.SemaphoreType.DMA((2,)),
            pltpu.SemaphoreType.DMA((n_space,)),
            pltpu.SemaphoreType.DMA((n_space,)),
            pltpu.SemaphoreType.DMA((n_tm,)),
            pltpu.SemaphoreType.DMA((n_tm,)),
            pltpu.SemaphoreType.DMA((n_space,)),
            pltpu.SemaphoreType.DMA((n_space,)),
            pltpu.SemaphoreType.DMA((n_tm,)),
            pltpu.SemaphoreType.DMA((n_tm,)),
            pltpu.SemaphoreType.DMA((1,)),
        ],
        compiler_params=pltpu.CompilerParams(collective_id=0, has_side_effects=True),
    )(vort_x, vloc, dudz)


def lanes(a, width):
    return pl.ds(pl.multiple_of(a * width, width), width)


def bdot(x, y):
    return jnp.einsum("nab,nbc->nac", x, y, precision=HIGH, preferred_element_type=jnp.float32)


def bdot_t(x, y):
    return jnp.einsum("nac,nbc->nab", x, y, precision=HIGH, preferred_element_type=jnp.float32)


def iotas(shape):
    return lax.broadcasted_iota(jnp.int32, shape, 1), lax.broadcasted_iota(jnp.int32, shape, 2)


def merge_coeffs(h):
    n = h.shape[0]
    kt = h[:, :RANK, :] + h[:, RANK:, :]
    row, col = iotas(h.shape)
    dcol = jnp.sum(jnp.where(row == col, h, 0.0), axis=2, keepdims=True)
    scales = jnp.sqrt(dcol[:, :RANK] + dcol[:, RANK:])
    inner = bdot_t(bdot(kt, h), kt)
    row, col = iotas(inner.shape)

    a = inner
    r = kt
    below = row[:, :, :1]
    for j in range(RANK):
        a_row = a[:, j : j + 1, :]
        r_row = r[:, j : j + 1, :]
        factor = jnp.where(below > j, a[:, :, j : j + 1] / a_row[:, :, j : j + 1], 0.0)
        a = a - factor * a_row
        r = r - factor * r_row
    diag_u = jnp.sum(jnp.where(row == col, a, 0.0), axis=2, keepdims=True)
    return r * (scales / jnp.sqrt(diag_u))


def split3(x):
    hi = x.astype(jnp.bfloat16)
    rest = x - hi.astype(jnp.float32)
    mid = rest.astype(jnp.bfloat16)
    lo = (rest - mid.astype(jnp.float32)).astype(jnp.bfloat16)
    return hi, mid, lo


def place(x, offset, width):
    n, r, w = x.shape
    row, col = iotas((n, w, width))
    pick = jnp.where(col == row + offset, 1.0, 0.0).astype(jnp.bfloat16)
    terms = jnp.einsum(
        "nab,nbc->nac", jnp.concatenate(split3(x), axis=1), pick, preferred_element_type=jnp.float32
    )
    return (terms[:, :r] + terms[:, r : 2 * r]) + terms[:, 2 * r :]


def tree_levels(g_ref):
    size = 2 * RANK
    leaves = g_ref.shape[0] // RANK
    picks = []
    for k in range(leaves // 2):
        lane0 = (k * size) // 128 * 128
        block = g_ref[k * size : (k + 1) * size, lane0 : lane0 + 128][None]
        picks.append(place(block, -(k * size - lane0), size))
    basis = merge_coeffs(jnp.concatenate(picks, axis=0))
    while basis.shape[0] > 1:
        n = basis.shape[0] // 2
        w = basis.shape[2]
        pairs = basis.reshape(n, 2, RANK, w)
        bt = jnp.concatenate(
            [place(pairs[:, 0], 0, 2 * w), place(pairs[:, 1], w, 2 * w)], axis=1
        )
        gs = jnp.concatenate(
            [g_ref[k * 2 * w : (k + 1) * 2 * w, k * 2 * w : (k + 1) * 2 * w][None] for k in range(n)],
            axis=0,
        )
        h = bdot_t(bdot(bt, gs), bt)
        basis = bdot(merge_coeffs(h), bt)
    return basis[0]


def finish_body(n_tm, g_ref, w_ref, out_ref, part_ref, buf, send, recv, own):
    s = lax.axis_index("space")
    t = lax.axis_index("tm")
    basis_t = tree_levels(g_ref)
    hi = basis_t.astype(jnp.bfloat16)
    rest = basis_t - hi.astype(jnp.float32)
    mid = rest.astype(jnp.bfloat16)
    lo = (rest - mid.astype(jnp.float32)).astype(jnp.bfloat16)
    pieces = jnp.concatenate([hi, mid, lo], axis=0)
    for x in range(w_ref.shape[0]):
        terms = jnp.dot(pieces, w_ref[x], preferred_element_type=jnp.float32)
        part_ref[x] = (terms[:RANK] + terms[RANK : 2 * RANK]) + terms[2 * RANK :]
    share = part_ref.shape[1] // n_tm
    width = w_ref.shape[2]
    src_at = lambda a: part_ref.at[:, pl.ds(a * share, share), :]
    dst_at = lambda j: buf.at[:, :, lanes(j, width)]
    copies = []
    for k in range(1, n_tm):
        a = lax.rem(t + k, n_tm)
        c = pltpu.make_async_remote_copy(
            src_ref=src_at(a), dst_ref=dst_at(t), send_sem=send.at[k], recv_sem=recv.at[t],
            device_id=(s, a), device_id_type=MESH,
        )
        c.start()
        copies.append(c)
    mine = pltpu.make_async_copy(src_at(t), dst_at(t), own.at[0])
    mine.start()
    mine.wait()
    for k in range(1, n_tm):
        j = lax.rem(t + k, n_tm)
        pltpu.make_async_remote_copy(
            src_ref=src_at(j), dst_ref=dst_at(j), send_sem=send.at[k], recv_sem=recv.at[j],
            device_id=(s, j), device_id_type=MESH,
        ).wait_recv()
    for c in copies:
        c.wait_send()
    out_ref[...] = buf[...]


def local(velocity):
    rows = velocity.shape[2]
    span_v = velocity[:, 1].astype(jnp.float32)
    stream_u = velocity[:, 0].astype(jnp.float32)
    du_dz = spanwise(stream_u)
    dv_dx = (
        8.0 * (jnp.roll(span_v, -1, 1) - jnp.roll(span_v, 1, 1))
        - (jnp.roll(span_v, -2, 1) - jnp.roll(span_v, 2, 1))
    ) / 12.0
    local_vort = (dv_dx - du_dz).astype(jnp.bfloat16)
    v = velocity[:, 1]
    vloc = jnp.swapaxes(jnp.concatenate([v[:, :4], v[:, rows - 4 :]], axis=1), 0, 1)
    dudz = jnp.swapaxes(jnp.concatenate([du_dz[:, :2], du_dz[:, rows - 2 :]], axis=1), 0, 1)
    modes, fixed = front(jnp.swapaxes(local_vort, 0, 1), vloc, dudz)
    fixed = jnp.swapaxes(fixed, 0, 1)
    vorticity = jnp.concatenate([fixed[:, :2], local_vort[:, 2 : rows - 2], fixed[:, 2:]], axis=1)
    return (vorticity, jnp.swapaxes(modes, 0, 1))


def solution(mesh):
    in_specs = (P("tm", None, "space", None),)
    out_specs = (P("tm", "space", None), P("tm", "space", None))
    return jax.shard_map(local, mesh=mesh, in_specs=in_specs, out_specs=out_specs, check_vma=False)
```

```python
import functools

import jax
import jax.numpy as jnp
from jax import lax
from jax.experimental import pallas as pl
from jax.experimental.pallas import tpu as pltpu
from jax.sharding import PartitionSpec as P

RANK = 32
HIGH = lax.Precision.HIGHEST


def halo_rows(block, width):
    count = lax.axis_size("space")
    forward = [(i, (i + 1) % count) for i in range(count)]
    backward = [(target, source) for source, target in forward]
    rows = block.shape[1]
    low = lax.ppermute(block[:, rows - width :], "space", forward)
    high = lax.ppermute(block[:, :width], "space", backward)
    return jnp.concatenate([low, block, high], axis=1)


def spanwise(field):
    ahead = jnp.roll(field, -1, 2)
    behind = jnp.roll(field, 1, 2)
    ahead_two = jnp.roll(field, -2, 2)
    behind_two = jnp.roll(field, 2, 2)
    return (8.0 * (ahead - behind) - (ahead_two - behind_two)) / 12.0


MESH = pl.DeviceIdType.MESH


def greet_all(n_space, n_tm):
    s = lax.axis_index("space")
    t = lax.axis_index("tm")
    barrier = pltpu.get_barrier_semaphore()

    def greet_space(k, carry):
        b = lax.rem(s + k, n_space)
        pl.semaphore_signal(barrier, inc=1, device_id=(b, t), device_id_type=MESH)
        return carry

    def greet_tm(k, carry):
        a = lax.rem(t + k, n_tm)
        pl.semaphore_signal(barrier, inc=1, device_id=(s, a), device_id_type=MESH)
        return carry

    lax.fori_loop(1, n_space, greet_space, 0)
    lax.fori_loop(1, n_tm, greet_tm, 0)
    pl.semaphore_wait(barrier, (n_space - 1) + (n_tm - 1))


def allreduce_body(n_space, n_tm, g_ref, out_ref, buf1, buf2, buf3, send1, recv1, send2, recv2, send3, recv3):
    s = lax.axis_index("space")
    t = lax.axis_index("tm")

    def space_copy(src, dst_buf, send, recv, k):
        b = lax.rem(s + k, n_space)
        return pltpu.make_async_remote_copy(
            src_ref=src(b), dst_ref=dst_buf.at[s], send_sem=send.at[k], recv_sem=recv.at[s],
            device_id=(b, t), device_id_type=MESH,
        )

    def space_wait(dst_buf, send, recv, k):
        j = lax.rem(s + k, n_space)
        pltpu.make_async_remote_copy(
            src_ref=dst_buf.at[j], dst_ref=dst_buf.at[j], send_sem=send.at[k], recv_sem=recv.at[j],
            device_id=(j, t), device_id_type=MESH,
        ).wait_recv()

    def send_p1(k, carry):
        space_copy(lambda b: g_ref.at[b], buf1, send1, recv1, k).start()
        return carry

    lax.fori_loop(1, n_space, send_p1, 0)
    buf1[s] = g_ref[s]

    def wait_p1(k, carry):
        space_wait(buf1, send1, recv1, k)
        return carry

    lax.fori_loop(1, n_space, wait_p1, 0)
    acc = buf1[0]
    for j in range(1, n_space):
        acc = acc + buf1[j]
    buf2[t] = acc

    copies = []
    for k in range(1, n_tm):
        a = lax.rem(t + k, n_tm)
        c = pltpu.make_async_remote_copy(
            src_ref=buf2.at[t], dst_ref=buf2.at[t], send_sem=send2.at[k], recv_sem=recv2.at[t],
            device_id=(s, a), device_id_type=MESH,
        )
        c.start()
        copies.append(c)
    for k in range(1, n_tm):
        j = lax.rem(t + k, n_tm)
        pltpu.make_async_remote_copy(
            src_ref=buf2.at[j], dst_ref=buf2.at[j], send_sem=send2.at[k], recv_sem=recv2.at[j],
            device_id=(s, j), device_id_type=MESH,
        ).wait_recv()
    for c in copies:
        c.wait_send()
    acc = buf2[0]
    for j in range(1, n_tm):
        acc = acc + buf2[j]
    buf3[s] = acc

    def send_p3(k, carry):
        space_copy(lambda b: buf3.at[s], buf3, send3, recv3, k).start()
        return carry

    lax.fori_loop(1, n_space, send_p3, 0)

    def wait_p3(k, carry):
        space_wait(buf3, send3, recv3, k)
        return carry

    lax.fori_loop(1, n_space, wait_p3, 0)

    def drain(k, carry):
        space_copy(lambda b: g_ref.at[b], buf1, send1, recv1, k).wait_send()
        space_copy(lambda b: buf3.at[s], buf3, send3, recv3, k).wait_send()
        return carry

    lax.fori_loop(1, n_space, drain, 0)
    out_ref[...] = buf3[...]


def a2a_body(n_tm, src_at, dst_at, x_ref, buf, send, recv, own):
    s = lax.axis_index("space")
    t = lax.axis_index("tm")
    copies = []
    for k in range(1, n_tm):
        a = lax.rem(t + k, n_tm)
        c = pltpu.make_async_remote_copy(
            src_ref=src_at(x_ref, a), dst_ref=dst_at(buf, t), send_sem=send.at[k], recv_sem=recv.at[t],
            device_id=(s, a), device_id_type=MESH,
        )
        c.start()
        copies.append(c)
    mine = pltpu.make_async_copy(src_at(x_ref, t), dst_at(buf, t), own.at[0])
    mine.start()
    mine.wait()
    for k in range(1, n_tm):
        j = lax.rem(t + k, n_tm)
        pltpu.make_async_remote_copy(
            src_ref=src_at(x_ref, j), dst_ref=dst_at(buf, j), send_sem=send.at[k], recv_sem=recv.at[j],
            device_id=(s, j), device_id_type=MESH,
        ).wait_recv()
    for c in copies:
        c.wait_send()


def fix_edges(vloc_ref, dudz_ref, halo, fix):
    f = lambda ref, i: ref[i].astype(jnp.float32)
    d = lambda ahead, behind, ahead_two, behind_two: (8.0 * (ahead - behind) - (ahead_two - behind_two)) / 12.0
    v = [f(vloc_ref, i) for i in range(8)]
    lo = [f(halo, 0), f(halo, 1)]
    hi = [f(halo, 2), f(halo, 3)]
    rows_dv = [
        d(v[1], lo[1], v[2], lo[0]),
        d(v[2], v[0], v[3], lo[1]),
        d(v[7], v[5], hi[0], v[4]),
        d(hi[0], v[6], hi[1], v[5]),
    ]
    for i in range(4):
        fix[i] = (rows_dv[i] - dudz_ref[i]).astype(fix.dtype)


def front_kernel(
    n_space, n_tm, x_ref, vloc_ref, dudz_ref, modes_ref, fixed_ref,
    cells, gpart, buf1, buf2, buf3, gfull, part, gathered, halo, fix, *sems,
):
    send, recv, own, esend, hsend, hrecv = sems[:6]
    s = lax.axis_index("space")
    t = lax.axis_index("tm")
    greet_all(n_space, n_tm)
    rows, _, cols = x_ref.shape
    width = cols // n_tm
    left = lax.rem(s + n_space - 1, n_space)
    right = lax.rem(s + 1, n_space)

    def remote(src_ref, dst_ref, ss, rs, dev):
        return pltpu.make_async_remote_copy(
            src_ref=src_ref, dst_ref=dst_ref, send_sem=ss, recv_sem=rs, device_id=dev, device_id_type=MESH
        )

    halo_out = [
        remote(vloc_ref.at[pl.ds(6, 2)], halo.at[pl.ds(0, 2)], hsend.at[0], hrecv.at[0], (right, t)),
        remote(vloc_ref.at[pl.ds(0, 2)], halo.at[pl.ds(2, 2)], hsend.at[1], hrecv.at[1], (left, t)),
    ]
    for c in halo_out:
        c.start()
    src = lambda ref, a, r0, nr: ref.at[pl.ds(r0, nr), :, lanes(a, width)]
    dst = lambda j, r0, nr: cells.at[pl.ds(r0, nr), pl.ds(j * RANK, RANK), :]
    inner = rows - 4
    copies = []
    for k in range(1, n_tm):
        a = lax.rem(t + k, n_tm)
        c = remote(src(x_ref, a, 2, inner), dst(t, 2, inner), send.at[k], recv.at[t], (s, a))
        c.start()
        copies.append(c)
    mine = pltpu.make_async_copy(src(x_ref, t, 2, inner), dst(t, 2, inner), own.at[0])
    mine.start()
    mine.wait()
    remote(vloc_ref.at[pl.ds(6, 2)], halo.at[pl.ds(0, 2)], hsend.at[0], hrecv.at[0], (left, t)).wait_recv()
    remote(vloc_ref.at[pl.ds(0, 2)], halo.at[pl.ds(2, 2)], hsend.at[1], hrecv.at[1], (right, t)).wait_recv()
    fix_edges(vloc_ref, dudz_ref, halo, fix)
    fixed_ref[...] = fix[...]
    for k in range(1, n_tm):
        a = lax.rem(t + k, n_tm)
        for e, (r0, d0) in enumerate(((0, 0), (2, rows - 2))):
            c = remote(src(fix, a, r0, 2), dst(t, d0, 2), esend.at[k, e], recv.at[t], (s, a))
            c.start()
            copies.append(c)
    for r0, d0 in ((0, 0), (2, rows - 2)):
        mine = pltpu.make_async_copy(src(fix, t, r0, 2), dst(t, d0, 2), own.at[0])
        mine.start()
        mine.wait()
    for k in range(1, n_tm):
        j = lax.rem(t + k, n_tm)
        remote(src(x_ref, j, 0, rows), dst(j, 0, rows), send.at[k], recv.at[j], (s, j)).wait_recv()
    for c in copies + halo_out:
        c.wait_send()
    size = cells.shape[1]
    gram = jnp.zeros((size, size), jnp.float32)
    for x in range(rows):
        w = cells[x]
        gram = gram + lax.dot_general(
            w, w, (((1,), (1,)), ((), ())), preferred_element_type=jnp.float32
        )
    gpart[...] = gram.reshape(gpart.shape)
    allreduce_body(n_space, n_tm, gpart, buf1, buf1, buf2, buf3, *sems[6:12])
    gfull[...] = buf3[...].reshape(gfull.shape)
    finish_body(n_tm, gfull, cells, modes_ref, part, gathered, *sems[12:])


def front(vort_x, vloc, dudz):
    n_space = lax.axis_size("space")
    n_tm = lax.axis_size("tm")
    rows, _, cols = vort_x.shape
    size = n_tm * RANK
    width = cols // n_tm
    cells_shape = (rows, size, width)
    chunks = (n_space, size // n_space, size)
    out_shape = (rows, RANK // n_tm, cols)
    edge_shape = (4, RANK, cols)
    return pl.pallas_call(
        functools.partial(front_kernel, n_space, n_tm),
        out_shape=(
            jax.ShapeDtypeStruct(out_shape, jnp.float32),
            jax.ShapeDtypeStruct(edge_shape, vort_x.dtype),
        ),
        in_specs=[pl.BlockSpec(memory_space=pltpu.VMEM)] * 3,
        out_specs=(pl.BlockSpec(memory_space=pltpu.VMEM), pl.BlockSpec(memory_space=pltpu.VMEM)),
        scratch_shapes=[
            pltpu.VMEM(cells_shape, vort_x.dtype),
            pltpu.VMEM(chunks, jnp.float32),
            pltpu.VMEM(chunks, jnp.float32),
            pltpu.VMEM((n_tm,) + chunks[1:], jnp.float32),
            pltpu.VMEM(chunks, jnp.float32),
            pltpu.VMEM((size, size), jnp.float32),
            pltpu.VMEM((rows, RANK, width), jnp.float32),
            pltpu.VMEM(out_shape, jnp.float32),
            pltpu.VMEM(edge_shape, vort_x.dtype),
            pltpu.VMEM(edge_shape, vort_x.dtype),
            pltpu.SemaphoreType.DMA((n_tm,)),
            pltpu.SemaphoreType.DMA((n_tm,)),
            pltpu.SemaphoreType.DMA((1,)),
            pltpu.SemaphoreType.DMA((n_tm, 2)),
            pltpu.SemaphoreType.DMA((2,)),
            pltpu.SemaphoreType.DMA((2,)),
            pltpu.SemaphoreType.DMA((n_space,)),
            pltpu.SemaphoreType.DMA((n_space,)),
            pltpu.SemaphoreType.DMA((n_tm,)),
            pltpu.SemaphoreType.DMA((n_tm,)),
            pltpu.SemaphoreType.DMA((n_space,)),
            pltpu.SemaphoreType.DMA((n_space,)),
            pltpu.SemaphoreType.DMA((n_tm,)),
            pltpu.SemaphoreType.DMA((n_tm,)),
            pltpu.SemaphoreType.DMA((1,)),
        ],
        compiler_params=pltpu.CompilerParams(collective_id=0, has_side_effects=True),
    )(vort_x, vloc, dudz)


def lanes(a, width):
    return pl.ds(pl.multiple_of(a * width, width), width)


def bdot(x, y):
    return jnp.einsum("nab,nbc->nac", x, y, precision=HIGH, preferred_element_type=jnp.float32)


def bdot_t(x, y):
    return jnp.einsum("nac,nbc->nab", x, y, precision=HIGH, preferred_element_type=jnp.float32)


def iotas(shape):
    return lax.broadcasted_iota(jnp.int32, shape, 1), lax.broadcasted_iota(jnp.int32, shape, 2)


def merge_coeffs(h):
    n = h.shape[0]
    kt = h[:, :RANK, :] + h[:, RANK:, :]
    row, col = iotas(h.shape)
    dcol = jnp.sum(jnp.where(row == col, h, 0.0), axis=2, keepdims=True)
    scales = jnp.sqrt(dcol[:, :RANK] + dcol[:, RANK:])
    inner = bdot_t(bdot(kt, h), kt)
    row, col = iotas(inner.shape)

    a = inner
    r = kt
    below = row[:, :, :1]
    for j in range(RANK):
        a_row = a[:, j : j + 1, :]
        r_row = r[:, j : j + 1, :]
        factor = jnp.where(below > j, a[:, :, j : j + 1] / a_row[:, :, j : j + 1], 0.0)
        a = a - factor * a_row
        r = r - factor * r_row
    diag_u = jnp.sum(jnp.where(row == col, a, 0.0), axis=2, keepdims=True)
    return r * (scales / jnp.sqrt(diag_u))


def split3(x):
    hi = x.astype(jnp.bfloat16)
    rest = x - hi.astype(jnp.float32)
    mid = rest.astype(jnp.bfloat16)
    lo = (rest - mid.astype(jnp.float32)).astype(jnp.bfloat16)
    return hi, mid, lo


def place(x, offset, width):
    n, r, w = x.shape
    row, col = iotas((n, w, width))
    pick = jnp.where(col == row + offset, 1.0, 0.0).astype(jnp.bfloat16)
    terms = jnp.einsum(
        "nab,nbc->nac", jnp.concatenate(split3(x), axis=1), pick, preferred_element_type=jnp.float32
    )
    return (terms[:, :r] + terms[:, r : 2 * r]) + terms[:, 2 * r :]


def tree_levels(g_ref):
    size = 2 * RANK
    leaves = g_ref.shape[0] // RANK
    picks = []
    for k in range(leaves // 2):
        lane0 = (k * size) // 128 * 128
        block = g_ref[k * size : (k + 1) * size, lane0 : lane0 + 128][None]
        picks.append(place(block, -(k * size - lane0), size))
    basis = merge_coeffs(jnp.concatenate(picks, axis=0))
    while basis.shape[0] > 1:
        n = basis.shape[0] // 2
        w = basis.shape[2]
        pairs = basis.reshape(n, 2, RANK, w)
        bt = jnp.concatenate(
            [place(pairs[:, 0], 0, 2 * w), place(pairs[:, 1], w, 2 * w)], axis=1
        )
        gs = jnp.concatenate(
            [g_ref[k * 2 * w : (k + 1) * 2 * w, k * 2 * w : (k + 1) * 2 * w][None] for k in range(n)],
            axis=0,
        )
        h = bdot_t(bdot(bt, gs), bt)
        basis = bdot(merge_coeffs(h), bt)
    return basis[0]


def finish_body(n_tm, g_ref, w_ref, out_ref, part_ref, buf, send, recv, own):
    s = lax.axis_index("space")
    t = lax.axis_index("tm")
    basis_t = tree_levels(g_ref)
    hi = basis_t.astype(jnp.bfloat16)
    rest = basis_t - hi.astype(jnp.float32)
    mid = rest.astype(jnp.bfloat16)
    lo = (rest - mid.astype(jnp.float32)).astype(jnp.bfloat16)
    pieces = jnp.concatenate([hi, mid, lo], axis=0)
    for x in range(w_ref.shape[0]):
        terms = jnp.dot(pieces, w_ref[x], preferred_element_type=jnp.float32)
        part_ref[x] = (terms[:RANK] + terms[RANK : 2 * RANK]) + terms[2 * RANK :]
    share = part_ref.shape[1] // n_tm
    width = w_ref.shape[2]
    src_at = lambda a: part_ref.at[:, pl.ds(a * share, share), :]
    dst_at = lambda j: buf.at[:, :, lanes(j, width)]
    copies = []
    for k in range(1, n_tm):
        a = lax.rem(t + k, n_tm)
        c = pltpu.make_async_remote_copy(
            src_ref=src_at(a), dst_ref=dst_at(t), send_sem=send.at[k], recv_sem=recv.at[t],
            device_id=(s, a), device_id_type=MESH,
        )
        c.start()
        copies.append(c)
    mine = pltpu.make_async_copy(src_at(t), dst_at(t), own.at[0])
    mine.start()
    mine.wait()
    for k in range(1, n_tm):
        j = lax.rem(t + k, n_tm)
        pltpu.make_async_remote_copy(
            src_ref=src_at(j), dst_ref=dst_at(j), send_sem=send.at[k], recv_sem=recv.at[j],
            device_id=(s, j), device_id_type=MESH,
        ).wait_recv()
    for c in copies:
        c.wait_send()
    out_ref[...] = buf[...]


def local(velocity):
    rows = velocity.shape[2]
    span_v = velocity[:, 1].astype(jnp.float32)
    stream_u = velocity[:, 0].astype(jnp.float32)
    du_dz = spanwise(stream_u)
    dv_dx = (
        8.0 * (jnp.roll(span_v, -1, 1) - jnp.roll(span_v, 1, 1))
        - (jnp.roll(span_v, -2, 1) - jnp.roll(span_v, 2, 1))
    ) / 12.0
    local_vort = (dv_dx - du_dz).astype(jnp.bfloat16)
    v = velocity[:, 1]
    vloc = jnp.swapaxes(jnp.concatenate([v[:, :4], v[:, rows - 4 :]], axis=1), 0, 1)
    dudz = jnp.swapaxes(jnp.concatenate([du_dz[:, :2], du_dz[:, rows - 2 :]], axis=1), 0, 1)
    modes, fixed = front(jnp.swapaxes(local_vort, 0, 1), vloc, dudz)
    fixed = jnp.swapaxes(fixed, 0, 1)
    vorticity = lax.dynamic_update_slice(local_vort, fixed[:, :2], (0, 0, 0))
    vorticity = lax.dynamic_update_slice(vorticity, fixed[:, 2:], (0, rows - 2, 0))
    return (vorticity, jnp.swapaxes(modes, 0, 1))


def solution(mesh):
    in_specs = (P("tm", None, "space", None),)
    out_specs = (P("tm", "space", None), P("tm", "space", None))
    return jax.shard_map(local, mesh=mesh, in_specs=in_specs, out_specs=out_specs, check_vma=False)
```

```python
import functools

import jax
import jax.numpy as jnp
from jax import lax
from jax.experimental import pallas as pl
from jax.experimental.pallas import tpu as pltpu
from jax.sharding import PartitionSpec as P

RANK = 32
HIGH = lax.Precision.HIGHEST


def halo_rows(block, width):
    count = lax.axis_size("space")
    forward = [(i, (i + 1) % count) for i in range(count)]
    backward = [(target, source) for source, target in forward]
    rows = block.shape[1]
    low = lax.ppermute(block[:, rows - width :], "space", forward)
    high = lax.ppermute(block[:, :width], "space", backward)
    return jnp.concatenate([low, block, high], axis=1)


def spanwise(field):
    ahead = jnp.roll(field, -1, 2)
    behind = jnp.roll(field, 1, 2)
    ahead_two = jnp.roll(field, -2, 2)
    behind_two = jnp.roll(field, 2, 2)
    return (8.0 * (ahead - behind) - (ahead_two - behind_two)) / 12.0


MESH = pl.DeviceIdType.MESH


def greet_all(n_space, n_tm):
    s = lax.axis_index("space")
    t = lax.axis_index("tm")
    barrier = pltpu.get_barrier_semaphore()

    def greet_space(k, carry):
        b = lax.rem(s + k, n_space)
        pl.semaphore_signal(barrier, inc=1, device_id=(b, t), device_id_type=MESH)
        return carry

    def greet_tm(k, carry):
        a = lax.rem(t + k, n_tm)
        pl.semaphore_signal(barrier, inc=1, device_id=(s, a), device_id_type=MESH)
        return carry

    lax.fori_loop(1, n_space, greet_space, 0)
    lax.fori_loop(1, n_tm, greet_tm, 0)
    pl.semaphore_wait(barrier, (n_space - 1) + (n_tm - 1))


def allreduce_body(n_space, n_tm, g_ref, out_ref, buf1, buf2, buf3, send1, recv1, send2, recv2, send3, recv3):
    s = lax.axis_index("space")
    t = lax.axis_index("tm")

    def space_copy(src, dst_buf, send, recv, k):
        b = lax.rem(s + k, n_space)
        return pltpu.make_async_remote_copy(
            src_ref=src(b), dst_ref=dst_buf.at[s], send_sem=send.at[k], recv_sem=recv.at[s],
            device_id=(b, t), device_id_type=MESH,
        )

    def space_wait(dst_buf, send, recv, k):
        j = lax.rem(s + k, n_space)
        pltpu.make_async_remote_copy(
            src_ref=dst_buf.at[j], dst_ref=dst_buf.at[j], send_sem=send.at[k], recv_sem=recv.at[j],
            device_id=(j, t), device_id_type=MESH,
        ).wait_recv()

    def send_p1(k, carry):
        space_copy(lambda b: g_ref.at[b], buf1, send1, recv1, k).start()
        return carry

    lax.fori_loop(1, n_space, send_p1, 0)
    buf1[s] = g_ref[s]

    def wait_p1(k, carry):
        space_wait(buf1, send1, recv1, k)
        return carry

    lax.fori_loop(1, n_space, wait_p1, 0)
    acc = buf1[0]
    for j in range(1, n_space):
        acc = acc + buf1[j]
    buf2[t] = acc

    copies = []
    for k in range(1, n_tm):
        a = lax.rem(t + k, n_tm)
        c = pltpu.make_async_remote_copy(
            src_ref=buf2.at[t], dst_ref=buf2.at[t], send_sem=send2.at[k], recv_sem=recv2.at[t],
            device_id=(s, a), device_id_type=MESH,
        )
        c.start()
        copies.append(c)
    for k in range(1, n_tm):
        j = lax.rem(t + k, n_tm)
        pltpu.make_async_remote_copy(
            src_ref=buf2.at[j], dst_ref=buf2.at[j], send_sem=send2.at[k], recv_sem=recv2.at[j],
            device_id=(s, j), device_id_type=MESH,
        ).wait_recv()
    for c in copies:
        c.wait_send()
    acc = buf2[0]
    for j in range(1, n_tm):
        acc = acc + buf2[j]
    buf3[s] = acc

    def send_p3(k, carry):
        space_copy(lambda b: buf3.at[s], buf3, send3, recv3, k).start()
        return carry

    lax.fori_loop(1, n_space, send_p3, 0)

    def wait_p3(k, carry):
        space_wait(buf3, send3, recv3, k)
        return carry

    lax.fori_loop(1, n_space, wait_p3, 0)

    def drain(k, carry):
        space_copy(lambda b: g_ref.at[b], buf1, send1, recv1, k).wait_send()
        space_copy(lambda b: buf3.at[s], buf3, send3, recv3, k).wait_send()
        return carry

    lax.fori_loop(1, n_space, drain, 0)
    out_ref[...] = buf3[...]


def a2a_body(n_tm, src_at, dst_at, x_ref, buf, send, recv, own):
    s = lax.axis_index("space")
    t = lax.axis_index("tm")
    copies = []
    for k in range(1, n_tm):
        a = lax.rem(t + k, n_tm)
        c = pltpu.make_async_remote_copy(
            src_ref=src_at(x_ref, a), dst_ref=dst_at(buf, t), send_sem=send.at[k], recv_sem=recv.at[t],
            device_id=(s, a), device_id_type=MESH,
        )
        c.start()
        copies.append(c)
    mine = pltpu.make_async_copy(src_at(x_ref, t), dst_at(buf, t), own.at[0])
    mine.start()
    mine.wait()
    for k in range(1, n_tm):
        j = lax.rem(t + k, n_tm)
        pltpu.make_async_remote_copy(
            src_ref=src_at(x_ref, j), dst_ref=dst_at(buf, j), send_sem=send.at[k], recv_sem=recv.at[j],
            device_id=(s, j), device_id_type=MESH,
        ).wait_recv()
    for c in copies:
        c.wait_send()


def fix_edges(vloc_ref, dudz_ref, halo, fix):
    f = lambda ref, i: ref[i].astype(jnp.float32)
    d = lambda ahead, behind, ahead_two, behind_two: (8.0 * (ahead - behind) - (ahead_two - behind_two)) / 12.0
    v = [f(vloc_ref, i) for i in range(8)]
    lo = [f(halo, 0), f(halo, 1)]
    hi = [f(halo, 2), f(halo, 3)]
    rows_dv = [
        d(v[1], lo[1], v[2], lo[0]),
        d(v[2], v[0], v[3], lo[1]),
        d(v[7], v[5], hi[0], v[4]),
        d(hi[0], v[6], hi[1], v[5]),
    ]
    for i in range(4):
        fix[i] = (rows_dv[i] - dudz_ref[i]).astype(fix.dtype)


def front_kernel(
    n_space, n_tm, x_ref, vloc_ref, dudz_ref, modes_ref, fixed_ref,
    cells, gpart, buf1, buf2, buf3, gfull, part, gathered, halo, fix, *sems,
):
    send, recv, own, esend, hsend, hrecv = sems[:6]
    s = lax.axis_index("space")
    t = lax.axis_index("tm")
    greet_all(n_space, n_tm)
    inner, _, cols = x_ref.shape
    rows = inner + 4
    width = cols // n_tm
    left = lax.rem(s + n_space - 1, n_space)
    right = lax.rem(s + 1, n_space)

    def remote(src_ref, dst_ref, ss, rs, dev):
        return pltpu.make_async_remote_copy(
            src_ref=src_ref, dst_ref=dst_ref, send_sem=ss, recv_sem=rs, device_id=dev, device_id_type=MESH
        )

    halo_out = [
        remote(vloc_ref.at[pl.ds(6, 2)], halo.at[pl.ds(0, 2)], hsend.at[0], hrecv.at[0], (right, t)),
        remote(vloc_ref.at[pl.ds(0, 2)], halo.at[pl.ds(2, 2)], hsend.at[1], hrecv.at[1], (left, t)),
    ]
    for c in halo_out:
        c.start()
    src = lambda ref, a, r0, nr: ref.at[pl.ds(r0, nr), :, lanes(a, width)]
    dst = lambda j, r0, nr: cells.at[pl.ds(r0, nr), pl.ds(j * RANK, RANK), :]
    copies = []
    for k in range(1, n_tm):
        a = lax.rem(t + k, n_tm)
        c = remote(src(x_ref, a, 0, inner), dst(t, 2, inner), send.at[k], recv.at[t], (s, a))
        c.start()
        copies.append(c)
    mine = pltpu.make_async_copy(src(x_ref, t, 0, inner), dst(t, 2, inner), own.at[0])
    mine.start()
    mine.wait()
    remote(vloc_ref.at[pl.ds(6, 2)], halo.at[pl.ds(0, 2)], hsend.at[0], hrecv.at[0], (left, t)).wait_recv()
    remote(vloc_ref.at[pl.ds(0, 2)], halo.at[pl.ds(2, 2)], hsend.at[1], hrecv.at[1], (right, t)).wait_recv()
    fix_edges(vloc_ref, dudz_ref, halo, fix)
    fixed_ref[...] = fix[...]
    for k in range(1, n_tm):
        a = lax.rem(t + k, n_tm)
        for e, (r0, d0) in enumerate(((0, 0), (2, rows - 2))):
            c = remote(src(fix, a, r0, 2), dst(t, d0, 2), esend.at[k, e], recv.at[t], (s, a))
            c.start()
            copies.append(c)
    for r0, d0 in ((0, 0), (2, rows - 2)):
        mine = pltpu.make_async_copy(src(fix, t, r0, 2), dst(t, d0, 2), own.at[0])
        mine.start()
        mine.wait()
    for k in range(1, n_tm):
        j = lax.rem(t + k, n_tm)
        remote(dst(j, 0, rows), dst(j, 0, rows), send.at[k], recv.at[j], (s, j)).wait_recv()
    for c in copies + halo_out:
        c.wait_send()
    size = cells.shape[1]
    gram = jnp.zeros((size, size), jnp.float32)
    for x in range(rows):
        w = cells[x]
        gram = gram + lax.dot_general(
            w, w, (((1,), (1,)), ((), ())), preferred_element_type=jnp.float32
        )
    gpart[...] = gram.reshape(gpart.shape)
    allreduce_body(n_space, n_tm, gpart, buf1, buf1, buf2, buf3, *sems[6:12])
    gfull[...] = buf3[...].reshape(gfull.shape)
    finish_body(n_tm, gfull, cells, modes_ref, part, gathered, *sems[12:])


def front(vort_x, vloc, dudz):
    n_space = lax.axis_size("space")
    n_tm = lax.axis_size("tm")
    inner, _, cols = vort_x.shape
    rows = inner + 4
    size = n_tm * RANK
    width = cols // n_tm
    cells_shape = (rows, size, width)
    chunks = (n_space, size // n_space, size)
    out_shape = (rows, RANK // n_tm, cols)
    edge_shape = (4, RANK, cols)
    return pl.pallas_call(
        functools.partial(front_kernel, n_space, n_tm),
        out_shape=(
            jax.ShapeDtypeStruct(out_shape, jnp.float32),
            jax.ShapeDtypeStruct(edge_shape, vort_x.dtype),
        ),
        in_specs=[pl.BlockSpec(memory_space=pltpu.VMEM)] * 3,
        out_specs=(pl.BlockSpec(memory_space=pltpu.VMEM), pl.BlockSpec(memory_space=pltpu.VMEM)),
        scratch_shapes=[
            pltpu.VMEM(cells_shape, vort_x.dtype),
            pltpu.VMEM(chunks, jnp.float32),
            pltpu.VMEM(chunks, jnp.float32),
            pltpu.VMEM((n_tm,) + chunks[1:], jnp.float32),
            pltpu.VMEM(chunks, jnp.float32),
            pltpu.VMEM((size, size), jnp.float32),
            pltpu.VMEM((rows, RANK, width), jnp.float32),
            pltpu.VMEM(out_shape, jnp.float32),
            pltpu.VMEM(edge_shape, vort_x.dtype),
            pltpu.VMEM(edge_shape, vort_x.dtype),
            pltpu.SemaphoreType.DMA((n_tm,)),
            pltpu.SemaphoreType.DMA((n_tm,)),
            pltpu.SemaphoreType.DMA((1,)),
            pltpu.SemaphoreType.DMA((n_tm, 2)),
            pltpu.SemaphoreType.DMA((2,)),
            pltpu.SemaphoreType.DMA((2,)),
            pltpu.SemaphoreType.DMA((n_space,)),
            pltpu.SemaphoreType.DMA((n_space,)),
            pltpu.SemaphoreType.DMA((n_tm,)),
            pltpu.SemaphoreType.DMA((n_tm,)),
            pltpu.SemaphoreType.DMA((n_space,)),
            pltpu.SemaphoreType.DMA((n_space,)),
            pltpu.SemaphoreType.DMA((n_tm,)),
            pltpu.SemaphoreType.DMA((n_tm,)),
            pltpu.SemaphoreType.DMA((1,)),
        ],
        compiler_params=pltpu.CompilerParams(collective_id=0, has_side_effects=True),
    )(vort_x, vloc, dudz)


def lanes(a, width):
    return pl.ds(pl.multiple_of(a * width, width), width)


def bdot(x, y):
    return jnp.einsum("nab,nbc->nac", x, y, precision=HIGH, preferred_element_type=jnp.float32)


def bdot_t(x, y):
    return jnp.einsum("nac,nbc->nab", x, y, precision=HIGH, preferred_element_type=jnp.float32)


def iotas(shape):
    return lax.broadcasted_iota(jnp.int32, shape, 1), lax.broadcasted_iota(jnp.int32, shape, 2)


def merge_coeffs(h):
    n = h.shape[0]
    kt = h[:, :RANK, :] + h[:, RANK:, :]
    row, col = iotas(h.shape)
    dcol = jnp.sum(jnp.where(row == col, h, 0.0), axis=2, keepdims=True)
    scales = jnp.sqrt(dcol[:, :RANK] + dcol[:, RANK:])
    inner = bdot_t(bdot(kt, h), kt)
    row, col = iotas(inner.shape)

    a = inner
    r = kt
    below = row[:, :, :1]
    for j in range(RANK):
        a_row = a[:, j : j + 1, :]
        r_row = r[:, j : j + 1, :]
        factor = jnp.where(below > j, a[:, :, j : j + 1] / a_row[:, :, j : j + 1], 0.0)
        a = a - factor * a_row
        r = r - factor * r_row
    diag_u = jnp.sum(jnp.where(row == col, a, 0.0), axis=2, keepdims=True)
    return r * (scales / jnp.sqrt(diag_u))


def split3(x):
    hi = x.astype(jnp.bfloat16)
    rest = x - hi.astype(jnp.float32)
    mid = rest.astype(jnp.bfloat16)
    lo = (rest - mid.astype(jnp.float32)).astype(jnp.bfloat16)
    return hi, mid, lo


def place(x, offset, width):
    n, r, w = x.shape
    row, col = iotas((n, w, width))
    pick = jnp.where(col == row + offset, 1.0, 0.0).astype(jnp.bfloat16)
    terms = jnp.einsum(
        "nab,nbc->nac", jnp.concatenate(split3(x), axis=1), pick, preferred_element_type=jnp.float32
    )
    return (terms[:, :r] + terms[:, r : 2 * r]) + terms[:, 2 * r :]


def tree_levels(g_ref):
    size = 2 * RANK
    leaves = g_ref.shape[0] // RANK
    picks = []
    for k in range(leaves // 2):
        lane0 = (k * size) // 128 * 128
        block = g_ref[k * size : (k + 1) * size, lane0 : lane0 + 128][None]
        picks.append(place(block, -(k * size - lane0), size))
    basis = merge_coeffs(jnp.concatenate(picks, axis=0))
    while basis.shape[0] > 1:
        n = basis.shape[0] // 2
        w = basis.shape[2]
        pairs = basis.reshape(n, 2, RANK, w)
        bt = jnp.concatenate(
            [place(pairs[:, 0], 0, 2 * w), place(pairs[:, 1], w, 2 * w)], axis=1
        )
        gs = jnp.concatenate(
            [g_ref[k * 2 * w : (k + 1) * 2 * w, k * 2 * w : (k + 1) * 2 * w][None] for k in range(n)],
            axis=0,
        )
        h = bdot_t(bdot(bt, gs), bt)
        basis = bdot(merge_coeffs(h), bt)
    return basis[0]


def finish_body(n_tm, g_ref, w_ref, out_ref, part_ref, buf, send, recv, own):
    s = lax.axis_index("space")
    t = lax.axis_index("tm")
    basis_t = tree_levels(g_ref)
    hi = basis_t.astype(jnp.bfloat16)
    rest = basis_t - hi.astype(jnp.float32)
    mid = rest.astype(jnp.bfloat16)
    lo = (rest - mid.astype(jnp.float32)).astype(jnp.bfloat16)
    pieces = jnp.concatenate([hi, mid, lo], axis=0)
    for x in range(w_ref.shape[0]):
        terms = jnp.dot(pieces, w_ref[x], preferred_element_type=jnp.float32)
        part_ref[x] = (terms[:RANK] + terms[RANK : 2 * RANK]) + terms[2 * RANK :]
    share = part_ref.shape[1] // n_tm
    width = w_ref.shape[2]
    src_at = lambda a: part_ref.at[:, pl.ds(a * share, share), :]
    dst_at = lambda j: buf.at[:, :, lanes(j, width)]
    copies = []
    for k in range(1, n_tm):
        a = lax.rem(t + k, n_tm)
        c = pltpu.make_async_remote_copy(
            src_ref=src_at(a), dst_ref=dst_at(t), send_sem=send.at[k], recv_sem=recv.at[t],
            device_id=(s, a), device_id_type=MESH,
        )
        c.start()
        copies.append(c)
    mine = pltpu.make_async_copy(src_at(t), dst_at(t), own.at[0])
    mine.start()
    mine.wait()
    for k in range(1, n_tm):
        j = lax.rem(t + k, n_tm)
        pltpu.make_async_remote_copy(
            src_ref=src_at(j), dst_ref=dst_at(j), send_sem=send.at[k], recv_sem=recv.at[j],
            device_id=(s, j), device_id_type=MESH,
        ).wait_recv()
    for c in copies:
        c.wait_send()
    out_ref[...] = buf[...]


def local(velocity):
    rows = velocity.shape[2]
    span_v = velocity[:, 1].astype(jnp.float32)
    stream_u = velocity[:, 0].astype(jnp.float32)
    du_dz = spanwise(stream_u)
    dv_dx = (
        8.0 * (span_v[:, 3 : rows - 1] - span_v[:, 1 : rows - 3])
        - (span_v[:, 4:rows] - span_v[:, : rows - 4])
    ) / 12.0
    interior = (dv_dx - du_dz[:, 2 : rows - 2]).astype(jnp.bfloat16)
    v = velocity[:, 1]
    vloc = jnp.swapaxes(jnp.concatenate([v[:, :4], v[:, rows - 4 :]], axis=1), 0, 1)
    dudz = jnp.swapaxes(jnp.concatenate([du_dz[:, :2], du_dz[:, rows - 2 :]], axis=1), 0, 1)
    modes, fixed = front(jnp.swapaxes(interior, 0, 1), vloc, dudz)
    fixed = jnp.swapaxes(fixed, 0, 1)
    vorticity = jnp.concatenate([fixed[:, :2], interior, fixed[:, 2:]], axis=1)
    return (vorticity, jnp.swapaxes(modes, 0, 1))


def solution(mesh):
    in_specs = (P("tm", None, "space", None),)
    out_specs = (P("tm", "space", None), P("tm", "space", None))
    return jax.shard_map(local, mesh=mesh, in_specs=in_specs, out_specs=out_specs, check_vma=False)
```

```python
import functools

import jax
import jax.numpy as jnp
from jax import lax
from jax.experimental import pallas as pl
from jax.experimental.pallas import tpu as pltpu
from jax.sharding import PartitionSpec as P

RANK = 32
HIGH = lax.Precision.HIGHEST


def halo_rows(block, width):
    count = lax.axis_size("space")
    forward = [(i, (i + 1) % count) for i in range(count)]
    backward = [(target, source) for source, target in forward]
    rows = block.shape[1]
    low = lax.ppermute(block[:, rows - width :], "space", forward)
    high = lax.ppermute(block[:, :width], "space", backward)
    return jnp.concatenate([low, block, high], axis=1)


def spanwise(field):
    ahead = jnp.roll(field, -1, 2)
    behind = jnp.roll(field, 1, 2)
    ahead_two = jnp.roll(field, -2, 2)
    behind_two = jnp.roll(field, 2, 2)
    return (8.0 * (ahead - behind) - (ahead_two - behind_two)) / 12.0


MESH = pl.DeviceIdType.MESH


def greet_all(n_space, n_tm):
    s = lax.axis_index("space")
    t = lax.axis_index("tm")
    barrier = pltpu.get_barrier_semaphore()

    def greet_space(k, carry):
        b = lax.rem(s + k, n_space)
        pl.semaphore_signal(barrier, inc=1, device_id=(b, t), device_id_type=MESH)
        return carry

    def greet_tm(k, carry):
        a = lax.rem(t + k, n_tm)
        pl.semaphore_signal(barrier, inc=1, device_id=(s, a), device_id_type=MESH)
        return carry

    lax.fori_loop(1, n_space, greet_space, 0)
    lax.fori_loop(1, n_tm, greet_tm, 0)
    pl.semaphore_wait(barrier, (n_space - 1) + (n_tm - 1))


def allreduce_body(n_space, n_tm, g_ref, out_ref, buf1, buf2, buf3, send1, recv1, send2, recv2, send3, recv3):
    s = lax.axis_index("space")
    t = lax.axis_index("tm")

    def space_copy(src, dst_buf, send, recv, k):
        b = lax.rem(s + k, n_space)
        return pltpu.make_async_remote_copy(
            src_ref=src(b), dst_ref=dst_buf.at[s], send_sem=send.at[k], recv_sem=recv.at[s],
            device_id=(b, t), device_id_type=MESH,
        )

    def space_wait(dst_buf, send, recv, k):
        j = lax.rem(s + k, n_space)
        pltpu.make_async_remote_copy(
            src_ref=dst_buf.at[j], dst_ref=dst_buf.at[j], send_sem=send.at[k], recv_sem=recv.at[j],
            device_id=(j, t), device_id_type=MESH,
        ).wait_recv()

    def send_p1(k, carry):
        space_copy(lambda b: g_ref.at[b], buf1, send1, recv1, k).start()
        return carry

    lax.fori_loop(1, n_space, send_p1, 0)
    buf1[s] = g_ref[s]

    def wait_p1(k, carry):
        space_wait(buf1, send1, recv1, k)
        return carry

    lax.fori_loop(1, n_space, wait_p1, 0)
    acc = buf1[0]
    for j in range(1, n_space):
        acc = acc + buf1[j]
    buf2[t] = acc

    copies = []
    for k in range(1, n_tm):
        a = lax.rem(t + k, n_tm)
        c = pltpu.make_async_remote_copy(
            src_ref=buf2.at[t], dst_ref=buf2.at[t], send_sem=send2.at[k], recv_sem=recv2.at[t],
            device_id=(s, a), device_id_type=MESH,
        )
        c.start()
        copies.append(c)
    for k in range(1, n_tm):
        j = lax.rem(t + k, n_tm)
        pltpu.make_async_remote_copy(
            src_ref=buf2.at[j], dst_ref=buf2.at[j], send_sem=send2.at[k], recv_sem=recv2.at[j],
            device_id=(s, j), device_id_type=MESH,
        ).wait_recv()
    for c in copies:
        c.wait_send()
    acc = buf2[0]
    for j in range(1, n_tm):
        acc = acc + buf2[j]
    buf3[s] = acc

    def send_p3(k, carry):
        space_copy(lambda b: buf3.at[s], buf3, send3, recv3, k).start()
        return carry

    lax.fori_loop(1, n_space, send_p3, 0)

    def wait_p3(k, carry):
        space_wait(buf3, send3, recv3, k)
        return carry

    lax.fori_loop(1, n_space, wait_p3, 0)

    def drain(k, carry):
        space_copy(lambda b: g_ref.at[b], buf1, send1, recv1, k).wait_send()
        space_copy(lambda b: buf3.at[s], buf3, send3, recv3, k).wait_send()
        return carry

    lax.fori_loop(1, n_space, drain, 0)
    out_ref[...] = buf3[...]


def a2a_body(n_tm, src_at, dst_at, x_ref, buf, send, recv, own):
    s = lax.axis_index("space")
    t = lax.axis_index("tm")
    copies = []
    for k in range(1, n_tm):
        a = lax.rem(t + k, n_tm)
        c = pltpu.make_async_remote_copy(
            src_ref=src_at(x_ref, a), dst_ref=dst_at(buf, t), send_sem=send.at[k], recv_sem=recv.at[t],
            device_id=(s, a), device_id_type=MESH,
        )
        c.start()
        copies.append(c)
    mine = pltpu.make_async_copy(src_at(x_ref, t), dst_at(buf, t), own.at[0])
    mine.start()
    mine.wait()
    for k in range(1, n_tm):
        j = lax.rem(t + k, n_tm)
        pltpu.make_async_remote_copy(
            src_ref=src_at(x_ref, j), dst_ref=dst_at(buf, j), send_sem=send.at[k], recv_sem=recv.at[j],
            device_id=(s, j), device_id_type=MESH,
        ).wait_recv()
    for c in copies:
        c.wait_send()


def fix_edges(vloc_ref, dudz_ref, halo, fix):
    f = lambda ref, i: ref[i].astype(jnp.float32)
    d = lambda ahead, behind, ahead_two, behind_two: (8.0 * (ahead - behind) - (ahead_two - behind_two)) / 12.0
    v = [f(vloc_ref, i) for i in range(8)]
    lo = [f(halo, 0), f(halo, 1)]
    hi = [f(halo, 2), f(halo, 3)]
    rows_dv = [
        d(v[1], lo[1], v[2], lo[0]),
        d(v[2], v[0], v[3], lo[1]),
        d(v[7], v[5], hi[0], v[4]),
        d(hi[0], v[6], hi[1], v[5]),
    ]
    for i in range(4):
        fix[i] = (rows_dv[i] - dudz_ref[i]).astype(fix.dtype)


def front_kernel(
    n_space, n_tm, x_ref, vloc_ref, dudz_ref, modes_ref, fixed_ref,
    cells, gpart, buf1, buf2, buf3, gfull, part, gathered, halo, fix, *sems,
):
    send, recv, own, esend, hsend, hrecv = sems[:6]
    s = lax.axis_index("space")
    t = lax.axis_index("tm")
    greet_all(n_space, n_tm)
    inner, _, cols = x_ref.shape
    rows = inner + 4
    width = cols // n_tm
    left = lax.rem(s + n_space - 1, n_space)
    right = lax.rem(s + 1, n_space)

    def remote(src_ref, dst_ref, ss, rs, dev):
        return pltpu.make_async_remote_copy(
            src_ref=src_ref, dst_ref=dst_ref, send_sem=ss, recv_sem=rs, device_id=dev, device_id_type=MESH
        )

    halo_out = [
        remote(vloc_ref.at[pl.ds(6, 2)], halo.at[pl.ds(0, 2)], hsend.at[0], hrecv.at[0], (right, t)),
        remote(vloc_ref.at[pl.ds(0, 2)], halo.at[pl.ds(2, 2)], hsend.at[1], hrecv.at[1], (left, t)),
    ]
    for c in halo_out:
        c.start()
    src = lambda ref, a, r0, nr: ref.at[pl.ds(r0, nr), :, lanes(a, width)]
    dst = lambda j, r0, nr: cells.at[pl.ds(r0, nr), pl.ds(j * RANK, RANK), :]
    copies = []
    for k in range(1, n_tm):
        a = lax.rem(t + k, n_tm)
        c = remote(src(x_ref, a, 0, inner), dst(t, 2, inner), send.at[k], recv.at[t], (s, a))
        c.start()
        copies.append(c)
    mine = pltpu.make_async_copy(src(x_ref, t, 0, inner), dst(t, 2, inner), own.at[0])
    mine.start()
    mine.wait()
    remote(vloc_ref.at[pl.ds(6, 2)], halo.at[pl.ds(0, 2)], hsend.at[0], hrecv.at[0], (left, t)).wait_recv()
    remote(vloc_ref.at[pl.ds(0, 2)], halo.at[pl.ds(2, 2)], hsend.at[1], hrecv.at[1], (right, t)).wait_recv()
    fix_edges(vloc_ref, dudz_ref, halo, fix)
    fixed_ref[...] = fix[...]
    for k in range(1, n_tm):
        a = lax.rem(t + k, n_tm)
        for e, (r0, d0) in enumerate(((0, 0), (2, rows - 2))):
            c = remote(src(fix, a, r0, 2), dst(t, d0, 2), esend.at[k, e], recv.at[t], (s, a))
            c.start()
            copies.append(c)
    for r0, d0 in ((0, 0), (2, rows - 2)):
        mine = pltpu.make_async_copy(src(fix, t, r0, 2), dst(t, d0, 2), own.at[0])
        mine.start()
        mine.wait()
    for k in range(1, n_tm):
        j = lax.rem(t + k, n_tm)
        remote(dst(j, 0, rows), dst(j, 0, rows), send.at[k], recv.at[j], (s, j)).wait_recv()
    for c in copies + halo_out:
        c.wait_send()
    size = cells.shape[1]
    gram = jnp.zeros((size, size), jnp.float32)
    for x in range(rows):
        w = cells[x]
        gram = gram + lax.dot_general(
            w, w, (((1,), (1,)), ((), ())), preferred_element_type=jnp.float32
        )
    gpart[...] = gram.reshape(gpart.shape)
    allreduce_body(n_space, n_tm, gpart, buf1, buf1, buf2, buf3, *sems[6:12])
    gfull[...] = buf3[...].reshape(gfull.shape)
    finish_body(n_tm, gfull, cells, modes_ref, part, gathered, *sems[12:])


def front(vort_x, vloc, dudz):
    n_space = lax.axis_size("space")
    n_tm = lax.axis_size("tm")
    inner, _, cols = vort_x.shape
    rows = inner + 4
    size = n_tm * RANK
    width = cols // n_tm
    cells_shape = (rows, size, width)
    chunks = (n_space, size // n_space, size)
    out_shape = (rows, RANK // n_tm, cols)
    edge_shape = (4, RANK, cols)
    return pl.pallas_call(
        functools.partial(front_kernel, n_space, n_tm),
        out_shape=(
            jax.ShapeDtypeStruct(out_shape, jnp.float32),
            jax.ShapeDtypeStruct(edge_shape, vort_x.dtype),
        ),
        in_specs=[pl.BlockSpec(memory_space=pltpu.VMEM)] * 3,
        out_specs=(pl.BlockSpec(memory_space=pltpu.VMEM), pl.BlockSpec(memory_space=pltpu.VMEM)),
        scratch_shapes=[
            pltpu.VMEM(cells_shape, vort_x.dtype),
            pltpu.VMEM(chunks, jnp.float32),
            pltpu.VMEM(chunks, jnp.float32),
            pltpu.VMEM((n_tm,) + chunks[1:], jnp.float32),
            pltpu.VMEM(chunks, jnp.float32),
            pltpu.VMEM((size, size), jnp.float32),
            pltpu.VMEM((rows, RANK, width), jnp.float32),
            pltpu.VMEM(out_shape, jnp.float32),
            pltpu.VMEM(edge_shape, vort_x.dtype),
            pltpu.VMEM(edge_shape, vort_x.dtype),
            pltpu.SemaphoreType.DMA((n_tm,)),
            pltpu.SemaphoreType.DMA((n_tm,)),
            pltpu.SemaphoreType.DMA((1,)),
            pltpu.SemaphoreType.DMA((n_tm, 2)),
            pltpu.SemaphoreType.DMA((2,)),
            pltpu.SemaphoreType.DMA((2,)),
            pltpu.SemaphoreType.DMA((n_space,)),
            pltpu.SemaphoreType.DMA((n_space,)),
            pltpu.SemaphoreType.DMA((n_tm,)),
            pltpu.SemaphoreType.DMA((n_tm,)),
            pltpu.SemaphoreType.DMA((n_space,)),
            pltpu.SemaphoreType.DMA((n_space,)),
            pltpu.SemaphoreType.DMA((n_tm,)),
            pltpu.SemaphoreType.DMA((n_tm,)),
            pltpu.SemaphoreType.DMA((1,)),
        ],
        compiler_params=pltpu.CompilerParams(collective_id=0, has_side_effects=True),
    )(vort_x, vloc, dudz)


def lanes(a, width):
    return pl.ds(pl.multiple_of(a * width, width), width)


def bdot(x, y):
    return jnp.einsum("nab,nbc->nac", x, y, precision=HIGH, preferred_element_type=jnp.float32)


def bdot_t(x, y):
    return jnp.einsum("nac,nbc->nab", x, y, precision=HIGH, preferred_element_type=jnp.float32)


def iotas(shape):
    return lax.broadcasted_iota(jnp.int32, shape, 1), lax.broadcasted_iota(jnp.int32, shape, 2)


def merge_coeffs(h):
    n = h.shape[0]
    kt = h[:, :RANK, :] + h[:, RANK:, :]
    row, col = iotas(h.shape)
    dcol = jnp.sum(jnp.where(row == col, h, 0.0), axis=2, keepdims=True)
    scales = jnp.sqrt(dcol[:, :RANK] + dcol[:, RANK:])
    inner = bdot_t(bdot(kt, h), kt)
    row, col = iotas(inner.shape)

    a = inner
    r = kt
    below = row[:, :, :1]
    for j in range(RANK):
        a_row = a[:, j : j + 1, :]
        r_row = r[:, j : j + 1, :]
        factor = jnp.where(below > j, a[:, :, j : j + 1] / a_row[:, :, j : j + 1], 0.0)
        a = a - factor * a_row
        r = r - factor * r_row
    diag_u = jnp.sum(jnp.where(row == col, a, 0.0), axis=2, keepdims=True)
    return r * (scales / jnp.sqrt(diag_u))


def split3(x):
    hi = x.astype(jnp.bfloat16)
    rest = x - hi.astype(jnp.float32)
    mid = rest.astype(jnp.bfloat16)
    lo = (rest - mid.astype(jnp.float32)).astype(jnp.bfloat16)
    return hi, mid, lo


def place(x, offset, width):
    n, r, w = x.shape
    row, col = iotas((n, w, width))
    pick = jnp.where(col == row + offset, 1.0, 0.0).astype(jnp.bfloat16)
    terms = jnp.einsum(
        "nab,nbc->nac", jnp.concatenate(split3(x), axis=1), pick, preferred_element_type=jnp.float32
    )
    return (terms[:, :r] + terms[:, r : 2 * r]) + terms[:, 2 * r :]


def tree_levels(g_ref):
    size = 2 * RANK
    leaves = g_ref.shape[0] // RANK
    picks = []
    for k in range(leaves // 2):
        lane0 = (k * size) // 128 * 128
        block = g_ref[k * size : (k + 1) * size, lane0 : lane0 + 128][None]
        picks.append(place(block, -(k * size - lane0), size))
    basis = merge_coeffs(jnp.concatenate(picks, axis=0))
    while basis.shape[0] > 1:
        n = basis.shape[0] // 2
        w = basis.shape[2]
        pairs = basis.reshape(n, 2, RANK, w)
        bt = jnp.concatenate(
            [place(pairs[:, 0], 0, 2 * w), place(pairs[:, 1], w, 2 * w)], axis=1
        )
        gs = jnp.concatenate(
            [g_ref[k * 2 * w : (k + 1) * 2 * w, k * 2 * w : (k + 1) * 2 * w][None] for k in range(n)],
            axis=0,
        )
        h = bdot_t(bdot(bt, gs), bt)
        basis = bdot(merge_coeffs(h), bt)
    return basis[0]


def finish_body(n_tm, g_ref, w_ref, out_ref, part_ref, buf, send, recv, own):
    s = lax.axis_index("space")
    t = lax.axis_index("tm")
    basis_t = tree_levels(g_ref)
    hi = basis_t.astype(jnp.bfloat16)
    rest = basis_t - hi.astype(jnp.float32)
    mid = rest.astype(jnp.bfloat16)
    lo = (rest - mid.astype(jnp.float32)).astype(jnp.bfloat16)
    pieces = jnp.concatenate([hi, mid, lo], axis=0)
    for x in range(w_ref.shape[0]):
        terms = jnp.dot(pieces, w_ref[x], preferred_element_type=jnp.float32)
        part_ref[x] = (terms[:RANK] + terms[RANK : 2 * RANK]) + terms[2 * RANK :]
    share = part_ref.shape[1] // n_tm
    width = w_ref.shape[2]
    src_at = lambda a: part_ref.at[:, pl.ds(a * share, share), :]
    dst_at = lambda j: buf.at[:, :, lanes(j, width)]
    copies = []
    for k in range(1, n_tm):
        a = lax.rem(t + k, n_tm)
        c = pltpu.make_async_remote_copy(
            src_ref=src_at(a), dst_ref=dst_at(t), send_sem=send.at[k], recv_sem=recv.at[t],
            device_id=(s, a), device_id_type=MESH,
        )
        c.start()
        copies.append(c)
    mine = pltpu.make_async_copy(src_at(t), dst_at(t), own.at[0])
    mine.start()
    mine.wait()
    for k in range(1, n_tm):
        j = lax.rem(t + k, n_tm)
        pltpu.make_async_remote_copy(
            src_ref=src_at(j), dst_ref=dst_at(j), send_sem=send.at[k], recv_sem=recv.at[j],
            device_id=(s, j), device_id_type=MESH,
        ).wait_recv()
    for c in copies:
        c.wait_send()
    out_ref[...] = buf[...]


def local(velocity):
    rows = velocity.shape[2]
    span_v = velocity[:, 1].astype(jnp.float32)
    u = velocity[:, 0]
    cols = u.shape[2]
    wrapped = jnp.concatenate([u[:, :, cols - 2 :], u, u[:, :, :2]], axis=2)
    f32 = lambda lo: wrapped[:, :, lo : lo + cols].astype(jnp.float32)
    du_dz = (8.0 * (f32(3) - f32(1)) - (f32(4) - f32(0))) / 12.0
    dv_dx = (
        8.0 * (span_v[:, 3 : rows - 1] - span_v[:, 1 : rows - 3])
        - (span_v[:, 4:rows] - span_v[:, : rows - 4])
    ) / 12.0
    interior = (dv_dx - du_dz[:, 2 : rows - 2]).astype(jnp.bfloat16)
    v = velocity[:, 1]
    vloc = jnp.swapaxes(jnp.concatenate([v[:, :4], v[:, rows - 4 :]], axis=1), 0, 1)
    dudz = jnp.swapaxes(jnp.concatenate([du_dz[:, :2], du_dz[:, rows - 2 :]], axis=1), 0, 1)
    modes, fixed = front(jnp.swapaxes(interior, 0, 1), vloc, dudz)
    fixed = jnp.swapaxes(fixed, 0, 1)
    vorticity = jnp.concatenate([fixed[:, :2], interior, fixed[:, 2:]], axis=1)
    return (vorticity, jnp.swapaxes(modes, 0, 1))


def solution(mesh):
    in_specs = (P("tm", None, "space", None),)
    out_specs = (P("tm", "space", None), P("tm", "space", None))
    return jax.shard_map(local, mesh=mesh, in_specs=in_specs, out_specs=out_specs, check_vma=False)
```

```python
import functools

import jax
import jax.numpy as jnp
from jax import lax
from jax.experimental import pallas as pl
from jax.experimental.pallas import tpu as pltpu
from jax.sharding import PartitionSpec as P

RANK = 32
HIGH = lax.Precision.HIGHEST


def halo_rows(block, width):
    count = lax.axis_size("space")
    forward = [(i, (i + 1) % count) for i in range(count)]
    backward = [(target, source) for source, target in forward]
    rows = block.shape[1]
    low = lax.ppermute(block[:, rows - width :], "space", forward)
    high = lax.ppermute(block[:, :width], "space", backward)
    return jnp.concatenate([low, block, high], axis=1)


def spanwise(field):
    ahead = jnp.roll(field, -1, 2)
    behind = jnp.roll(field, 1, 2)
    ahead_two = jnp.roll(field, -2, 2)
    behind_two = jnp.roll(field, 2, 2)
    return (8.0 * (ahead - behind) - (ahead_two - behind_two)) / 12.0


MESH = pl.DeviceIdType.MESH


def greet_all(n_space, n_tm):
    s = lax.axis_index("space")
    t = lax.axis_index("tm")
    barrier = pltpu.get_barrier_semaphore()

    def greet_space(k, carry):
        b = lax.rem(s + k, n_space)
        pl.semaphore_signal(barrier, inc=1, device_id=(b, t), device_id_type=MESH)
        return carry

    def greet_tm(k, carry):
        a = lax.rem(t + k, n_tm)
        pl.semaphore_signal(barrier, inc=1, device_id=(s, a), device_id_type=MESH)
        return carry

    lax.fori_loop(1, n_space, greet_space, 0)
    lax.fori_loop(1, n_tm, greet_tm, 0)
    pl.semaphore_wait(barrier, (n_space - 1) + (n_tm - 1))


def allreduce_body(n_space, n_tm, g_ref, out_ref, buf1, buf2, buf3, send1, recv1, send2, recv2, send3, recv3):
    s = lax.axis_index("space")
    t = lax.axis_index("tm")

    def space_copy(src, dst_buf, send, recv, k):
        b = lax.rem(s + k, n_space)
        return pltpu.make_async_remote_copy(
            src_ref=src(b), dst_ref=dst_buf.at[s], send_sem=send.at[k], recv_sem=recv.at[s],
            device_id=(b, t), device_id_type=MESH,
        )

    def space_wait(dst_buf, send, recv, k):
        j = lax.rem(s + k, n_space)
        pltpu.make_async_remote_copy(
            src_ref=dst_buf.at[j], dst_ref=dst_buf.at[j], send_sem=send.at[k], recv_sem=recv.at[j],
            device_id=(j, t), device_id_type=MESH,
        ).wait_recv()

    def send_p1(k, carry):
        space_copy(lambda b: g_ref.at[b], buf1, send1, recv1, k).start()
        return carry

    lax.fori_loop(1, n_space, send_p1, 0)
    buf1[s] = g_ref[s]

    def wait_p1(k, carry):
        space_wait(buf1, send1, recv1, k)
        return carry

    lax.fori_loop(1, n_space, wait_p1, 0)
    acc = buf1[0]
    for j in range(1, n_space):
        acc = acc + buf1[j]
    buf2[t] = acc

    copies = []
    for k in range(1, n_tm):
        a = lax.rem(t + k, n_tm)
        c = pltpu.make_async_remote_copy(
            src_ref=buf2.at[t], dst_ref=buf2.at[t], send_sem=send2.at[k], recv_sem=recv2.at[t],
            device_id=(s, a), device_id_type=MESH,
        )
        c.start()
        copies.append(c)
    for k in range(1, n_tm):
        j = lax.rem(t + k, n_tm)
        pltpu.make_async_remote_copy(
            src_ref=buf2.at[j], dst_ref=buf2.at[j], send_sem=send2.at[k], recv_sem=recv2.at[j],
            device_id=(s, j), device_id_type=MESH,
        ).wait_recv()
    for c in copies:
        c.wait_send()
    acc = buf2[0]
    for j in range(1, n_tm):
        acc = acc + buf2[j]
    buf3[s] = acc

    def send_p3(k, carry):
        space_copy(lambda b: buf3.at[s], buf3, send3, recv3, k).start()
        return carry

    lax.fori_loop(1, n_space, send_p3, 0)

    def wait_p3(k, carry):
        space_wait(buf3, send3, recv3, k)
        return carry

    lax.fori_loop(1, n_space, wait_p3, 0)

    def drain(k, carry):
        space_copy(lambda b: g_ref.at[b], buf1, send1, recv1, k).wait_send()
        space_copy(lambda b: buf3.at[s], buf3, send3, recv3, k).wait_send()
        return carry

    lax.fori_loop(1, n_space, drain, 0)
    out_ref[...] = buf3[...]


def a2a_body(n_tm, src_at, dst_at, x_ref, buf, send, recv, own):
    s = lax.axis_index("space")
    t = lax.axis_index("tm")
    copies = []
    for k in range(1, n_tm):
        a = lax.rem(t + k, n_tm)
        c = pltpu.make_async_remote_copy(
            src_ref=src_at(x_ref, a), dst_ref=dst_at(buf, t), send_sem=send.at[k], recv_sem=recv.at[t],
            device_id=(s, a), device_id_type=MESH,
        )
        c.start()
        copies.append(c)
    mine = pltpu.make_async_copy(src_at(x_ref, t), dst_at(buf, t), own.at[0])
    mine.start()
    mine.wait()
    for k in range(1, n_tm):
        j = lax.rem(t + k, n_tm)
        pltpu.make_async_remote_copy(
            src_ref=src_at(x_ref, j), dst_ref=dst_at(buf, j), send_sem=send.at[k], recv_sem=recv.at[j],
            device_id=(s, j), device_id_type=MESH,
        ).wait_recv()
    for c in copies:
        c.wait_send()


def fix_edges(vloc_ref, dudz_ref, halo, fix):
    f = lambda ref, i: ref[i].astype(jnp.float32)
    d = lambda ahead, behind, ahead_two, behind_two: (8.0 * (ahead - behind) - (ahead_two - behind_two)) / 12.0
    v = [f(vloc_ref, i) for i in range(8)]
    lo = [f(halo, 0), f(halo, 1)]
    hi = [f(halo, 2), f(halo, 3)]
    rows_dv = [
        d(v[1], lo[1], v[2], lo[0]),
        d(v[2], v[0], v[3], lo[1]),
        d(v[7], v[5], hi[0], v[4]),
        d(hi[0], v[6], hi[1], v[5]),
    ]
    for i in range(4):
        fix[i] = (rows_dv[i] - dudz_ref[i]).astype(fix.dtype)


def front_kernel(
    n_space, n_tm, x_ref, vloc_ref, dudz_ref, modes_ref, fixed_ref,
    cells, gpart, buf1, buf2, buf3, gfull, part, gathered, halo, fix, *sems,
):
    send, recv, own, esend, hsend, hrecv = sems[:6]
    s = lax.axis_index("space")
    t = lax.axis_index("tm")
    greet_all(n_space, n_tm)
    inner, _, cols = x_ref.shape
    rows = inner + 4
    width = cols // n_tm
    left = lax.rem(s + n_space - 1, n_space)
    right = lax.rem(s + 1, n_space)

    def remote(src_ref, dst_ref, ss, rs, dev):
        return pltpu.make_async_remote_copy(
            src_ref=src_ref, dst_ref=dst_ref, send_sem=ss, recv_sem=rs, device_id=dev, device_id_type=MESH
        )

    halo_out = [
        remote(vloc_ref.at[pl.ds(6, 2)], halo.at[pl.ds(0, 2)], hsend.at[0], hrecv.at[0], (right, t)),
        remote(vloc_ref.at[pl.ds(0, 2)], halo.at[pl.ds(2, 2)], hsend.at[1], hrecv.at[1], (left, t)),
    ]
    for c in halo_out:
        c.start()
    src = lambda ref, a, r0, nr: ref.at[pl.ds(r0, nr), :, lanes(a, width)]
    dst = lambda j, r0, nr: cells.at[pl.ds(r0, nr), pl.ds(j * RANK, RANK), :]
    copies = []
    for k in range(1, n_tm):
        a = lax.rem(t + k, n_tm)
        c = remote(src(x_ref, a, 0, inner), dst(t, 2, inner), send.at[k], recv.at[t], (s, a))
        c.start()
        copies.append(c)
    mine = pltpu.make_async_copy(src(x_ref, t, 0, inner), dst(t, 2, inner), own.at[0])
    mine.start()
    mine.wait()
    remote(vloc_ref.at[pl.ds(6, 2)], halo.at[pl.ds(0, 2)], hsend.at[0], hrecv.at[0], (left, t)).wait_recv()
    remote(vloc_ref.at[pl.ds(0, 2)], halo.at[pl.ds(2, 2)], hsend.at[1], hrecv.at[1], (right, t)).wait_recv()
    fix_edges(vloc_ref, dudz_ref, halo, fix)
    fixed_ref[...] = fix[...]
    for k in range(1, n_tm):
        a = lax.rem(t + k, n_tm)
        for e, (r0, d0) in enumerate(((0, 0), (2, rows - 2))):
            c = remote(src(fix, a, r0, 2), dst(t, d0, 2), esend.at[k, e], recv.at[t], (s, a))
            c.start()
            copies.append(c)
    for r0, d0 in ((0, 0), (2, rows - 2)):
        mine = pltpu.make_async_copy(src(fix, t, r0, 2), dst(t, d0, 2), own.at[0])
        mine.start()
        mine.wait()
    for k in range(1, n_tm):
        j = lax.rem(t + k, n_tm)
        remote(dst(j, 0, rows), dst(j, 0, rows), send.at[k], recv.at[j], (s, j)).wait_recv()
    for c in copies + halo_out:
        c.wait_send()
    size = cells.shape[1]
    gram = jnp.zeros((size, size), jnp.float32)
    for x in range(rows):
        w = cells[x]
        gram = gram + lax.dot_general(
            w, w, (((1,), (1,)), ((), ())), preferred_element_type=jnp.float32
        )
    gpart[...] = gram.reshape(gpart.shape)
    allreduce_body(n_space, n_tm, gpart, buf1, buf1, buf2, buf3, *sems[6:12])
    gfull[...] = buf3[...].reshape(gfull.shape)
    finish_body(n_tm, gfull, cells, modes_ref, part, gathered, *sems[12:])


def front(vort_x, vloc, dudz):
    n_space = lax.axis_size("space")
    n_tm = lax.axis_size("tm")
    inner, _, cols = vort_x.shape
    rows = inner + 4
    size = n_tm * RANK
    width = cols // n_tm
    cells_shape = (rows, size, width)
    chunks = (n_space, size // n_space, size)
    out_shape = (rows, RANK // n_tm, cols)
    edge_shape = (4, RANK, cols)
    return pl.pallas_call(
        functools.partial(front_kernel, n_space, n_tm),
        out_shape=(
            jax.ShapeDtypeStruct(out_shape, jnp.float32),
            jax.ShapeDtypeStruct(edge_shape, vort_x.dtype),
        ),
        in_specs=[pl.BlockSpec(memory_space=pltpu.VMEM)] * 3,
        out_specs=(pl.BlockSpec(memory_space=pltpu.VMEM), pl.BlockSpec(memory_space=pltpu.VMEM)),
        scratch_shapes=[
            pltpu.VMEM(cells_shape, vort_x.dtype),
            pltpu.VMEM(chunks, jnp.float32),
            pltpu.VMEM(chunks, jnp.float32),
            pltpu.VMEM((n_tm,) + chunks[1:], jnp.float32),
            pltpu.VMEM(chunks, jnp.float32),
            pltpu.VMEM((size, size), jnp.float32),
            pltpu.VMEM((rows, RANK, width), jnp.float32),
            pltpu.VMEM(out_shape, jnp.float32),
            pltpu.VMEM(edge_shape, vort_x.dtype),
            pltpu.VMEM(edge_shape, vort_x.dtype),
            pltpu.SemaphoreType.DMA((n_tm,)),
            pltpu.SemaphoreType.DMA((n_tm,)),
            pltpu.SemaphoreType.DMA((1,)),
            pltpu.SemaphoreType.DMA((n_tm, 2)),
            pltpu.SemaphoreType.DMA((2,)),
            pltpu.SemaphoreType.DMA((2,)),
            pltpu.SemaphoreType.DMA((n_space,)),
            pltpu.SemaphoreType.DMA((n_space,)),
            pltpu.SemaphoreType.DMA((n_tm,)),
            pltpu.SemaphoreType.DMA((n_tm,)),
            pltpu.SemaphoreType.DMA((n_space,)),
            pltpu.SemaphoreType.DMA((n_space,)),
            pltpu.SemaphoreType.DMA((n_tm,)),
            pltpu.SemaphoreType.DMA((n_tm,)),
            pltpu.SemaphoreType.DMA((1,)),
        ],
        compiler_params=pltpu.CompilerParams(collective_id=0, has_side_effects=True),
    )(vort_x, vloc, dudz)


def lanes(a, width):
    return pl.ds(pl.multiple_of(a * width, width), width)


def bdot(x, y):
    return jnp.einsum("nab,nbc->nac", x, y, precision=HIGH, preferred_element_type=jnp.float32)


def bdot_t(x, y):
    return jnp.einsum("nac,nbc->nab", x, y, precision=HIGH, preferred_element_type=jnp.float32)


def iotas(shape):
    return lax.broadcasted_iota(jnp.int32, shape, 1), lax.broadcasted_iota(jnp.int32, shape, 2)


def merge_coeffs(h):
    n = h.shape[0]
    kt = h[:, :RANK, :] + h[:, RANK:, :]
    row, col = iotas(h.shape)
    dcol = jnp.sum(jnp.where(row == col, h, 0.0), axis=2, keepdims=True)
    scales = jnp.sqrt(dcol[:, :RANK] + dcol[:, RANK:])
    inner = bdot_t(bdot(kt, h), kt)
    row, col = iotas(inner.shape)

    a = inner
    r = kt
    below = row[:, :, :1]
    for j in range(RANK):
        a_row = a[:, j : j + 1, :]
        r_row = r[:, j : j + 1, :]
        inv = 1.0 / a_row[:, :, j : j + 1]
        factor = jnp.where(below > j, a[:, :, j : j + 1] * inv, 0.0)
        a = a - factor * a_row
        r = r - factor * r_row
    diag_u = jnp.sum(jnp.where(row == col, a, 0.0), axis=2, keepdims=True)
    return r * (scales / jnp.sqrt(diag_u))


def split3(x):
    hi = x.astype(jnp.bfloat16)
    rest = x - hi.astype(jnp.float32)
    mid = rest.astype(jnp.bfloat16)
    lo = (rest - mid.astype(jnp.float32)).astype(jnp.bfloat16)
    return hi, mid, lo


def place(x, offset, width):
    n, r, w = x.shape
    row, col = iotas((n, w, width))
    pick = jnp.where(col == row + offset, 1.0, 0.0).astype(jnp.bfloat16)
    terms = jnp.einsum(
        "nab,nbc->nac", jnp.concatenate(split3(x), axis=1), pick, preferred_element_type=jnp.float32
    )
    return (terms[:, :r] + terms[:, r : 2 * r]) + terms[:, 2 * r :]


def tree_levels(g_ref):
    size = 2 * RANK
    leaves = g_ref.shape[0] // RANK
    picks = []
    for k in range(leaves // 2):
        lane0 = (k * size) // 128 * 128
        block = g_ref[k * size : (k + 1) * size, lane0 : lane0 + 128][None]
        picks.append(place(block, -(k * size - lane0), size))
    basis = merge_coeffs(jnp.concatenate(picks, axis=0))
    while basis.shape[0] > 1:
        n = basis.shape[0] // 2
        w = basis.shape[2]
        pairs = basis.reshape(n, 2, RANK, w)
        bt = jnp.concatenate(
            [place(pairs[:, 0], 0, 2 * w), place(pairs[:, 1], w, 2 * w)], axis=1
        )
        gs = jnp.concatenate(
            [g_ref[k * 2 * w : (k + 1) * 2 * w, k * 2 * w : (k + 1) * 2 * w][None] for k in range(n)],
            axis=0,
        )
        h = bdot_t(bdot(bt, gs), bt)
        basis = bdot(merge_coeffs(h), bt)
    return basis[0]


def finish_body(n_tm, g_ref, w_ref, out_ref, part_ref, buf, send, recv, own):
    s = lax.axis_index("space")
    t = lax.axis_index("tm")
    basis_t = tree_levels(g_ref)
    hi = basis_t.astype(jnp.bfloat16)
    rest = basis_t - hi.astype(jnp.float32)
    mid = rest.astype(jnp.bfloat16)
    lo = (rest - mid.astype(jnp.float32)).astype(jnp.bfloat16)
    pieces = jnp.concatenate([hi, mid, lo], axis=0)
    for x in range(w_ref.shape[0]):
        terms = jnp.dot(pieces, w_ref[x], preferred_element_type=jnp.float32)
        part_ref[x] = (terms[:RANK] + terms[RANK : 2 * RANK]) + terms[2 * RANK :]
    share = part_ref.shape[1] // n_tm
    width = w_ref.shape[2]
    src_at = lambda a: part_ref.at[:, pl.ds(a * share, share), :]
    dst_at = lambda j: buf.at[:, :, lanes(j, width)]
    copies = []
    for k in range(1, n_tm):
        a = lax.rem(t + k, n_tm)
        c = pltpu.make_async_remote_copy(
            src_ref=src_at(a), dst_ref=dst_at(t), send_sem=send.at[k], recv_sem=recv.at[t],
            device_id=(s, a), device_id_type=MESH,
        )
        c.start()
        copies.append(c)
    mine = pltpu.make_async_copy(src_at(t), dst_at(t), own.at[0])
    mine.start()
    mine.wait()
    for k in range(1, n_tm):
        j = lax.rem(t + k, n_tm)
        pltpu.make_async_remote_copy(
            src_ref=src_at(j), dst_ref=dst_at(j), send_sem=send.at[k], recv_sem=recv.at[j],
            device_id=(s, j), device_id_type=MESH,
        ).wait_recv()
    for c in copies:
        c.wait_send()
    out_ref[...] = buf[...]


def local(velocity):
    rows = velocity.shape[2]
    span_v = velocity[:, 1].astype(jnp.float32)
    u = velocity[:, 0]
    cols = u.shape[2]
    wrapped = jnp.concatenate([u[:, :, cols - 2 :], u, u[:, :, :2]], axis=2)
    f32 = lambda lo: wrapped[:, :, lo : lo + cols].astype(jnp.float32)
    du_dz = (8.0 * (f32(3) - f32(1)) - (f32(4) - f32(0))) / 12.0
    dv_dx = (
        8.0 * (span_v[:, 3 : rows - 1] - span_v[:, 1 : rows - 3])
        - (span_v[:, 4:rows] - span_v[:, : rows - 4])
    ) / 12.0
    interior = (dv_dx - du_dz[:, 2 : rows - 2]).astype(jnp.bfloat16)
    v = velocity[:, 1]
    vloc = jnp.swapaxes(jnp.concatenate([v[:, :4], v[:, rows - 4 :]], axis=1), 0, 1)
    dudz = jnp.swapaxes(jnp.concatenate([du_dz[:, :2], du_dz[:, rows - 2 :]], axis=1), 0, 1)
    modes, fixed = front(jnp.swapaxes(interior, 0, 1), vloc, dudz)
    fixed = jnp.swapaxes(fixed, 0, 1)
    vorticity = jnp.concatenate([fixed[:, :2], interior, fixed[:, 2:]], axis=1)
    return (vorticity, jnp.swapaxes(modes, 0, 1))


def solution(mesh):
    in_specs = (P("tm", None, "space", None),)
    out_specs = (P("tm", "space", None), P("tm", "space", None))
    return jax.shard_map(local, mesh=mesh, in_specs=in_specs, out_specs=out_specs, check_vma=False)
```

```python
import functools

import jax
import jax.numpy as jnp
from jax import lax
from jax.experimental import pallas as pl
from jax.experimental.pallas import tpu as pltpu
from jax.sharding import PartitionSpec as P

RANK = 32
HIGH = lax.Precision.HIGHEST


def halo_rows(block, width):
    count = lax.axis_size("space")
    forward = [(i, (i + 1) % count) for i in range(count)]
    backward = [(target, source) for source, target in forward]
    rows = block.shape[1]
    low = lax.ppermute(block[:, rows - width :], "space", forward)
    high = lax.ppermute(block[:, :width], "space", backward)
    return jnp.concatenate([low, block, high], axis=1)


def spanwise(field):
    ahead = jnp.roll(field, -1, 2)
    behind = jnp.roll(field, 1, 2)
    ahead_two = jnp.roll(field, -2, 2)
    behind_two = jnp.roll(field, 2, 2)
    return (8.0 * (ahead - behind) - (ahead_two - behind_two)) / 12.0


MESH = pl.DeviceIdType.MESH


def greet_all(n_space, n_tm):
    s = lax.axis_index("space")
    t = lax.axis_index("tm")
    barrier = pltpu.get_barrier_semaphore()

    def greet_space(k, carry):
        b = lax.rem(s + k, n_space)
        pl.semaphore_signal(barrier, inc=1, device_id=(b, t), device_id_type=MESH)
        return carry

    def greet_tm(k, carry):
        a = lax.rem(t + k, n_tm)
        pl.semaphore_signal(barrier, inc=1, device_id=(s, a), device_id_type=MESH)
        return carry

    lax.fori_loop(1, n_space, greet_space, 0)
    lax.fori_loop(1, n_tm, greet_tm, 0)
    pl.semaphore_wait(barrier, (n_space - 1) + (n_tm - 1))


def allreduce_body(n_space, n_tm, g_ref, out_ref, buf1, buf2, buf3, send1, recv1, send2, recv2, send3, recv3):
    s = lax.axis_index("space")
    t = lax.axis_index("tm")

    def space_copy(src, dst_buf, send, recv, k):
        b = lax.rem(s + k, n_space)
        return pltpu.make_async_remote_copy(
            src_ref=src(b), dst_ref=dst_buf.at[s], send_sem=send.at[k], recv_sem=recv.at[s],
            device_id=(b, t), device_id_type=MESH,
        )

    def space_wait(dst_buf, send, recv, k):
        j = lax.rem(s + k, n_space)
        pltpu.make_async_remote_copy(
            src_ref=dst_buf.at[j], dst_ref=dst_buf.at[j], send_sem=send.at[k], recv_sem=recv.at[j],
            device_id=(j, t), device_id_type=MESH,
        ).wait_recv()

    def send_p1(k, carry):
        space_copy(lambda b: g_ref.at[b], buf1, send1, recv1, k).start()
        return carry

    lax.fori_loop(1, n_space, send_p1, 0)
    buf1[s] = g_ref[s]

    def wait_p1(k, carry):
        space_wait(buf1, send1, recv1, k)
        return carry

    lax.fori_loop(1, n_space, wait_p1, 0)
    acc = buf1[0]
    for j in range(1, n_space):
        acc = acc + buf1[j]
    buf2[t] = acc

    copies = []
    for k in range(1, n_tm):
        a = lax.rem(t + k, n_tm)
        c = pltpu.make_async_remote_copy(
            src_ref=buf2.at[t], dst_ref=buf2.at[t], send_sem=send2.at[k], recv_sem=recv2.at[t],
            device_id=(s, a), device_id_type=MESH,
        )
        c.start()
        copies.append(c)
    for k in range(1, n_tm):
        j = lax.rem(t + k, n_tm)
        pltpu.make_async_remote_copy(
            src_ref=buf2.at[j], dst_ref=buf2.at[j], send_sem=send2.at[k], recv_sem=recv2.at[j],
            device_id=(s, j), device_id_type=MESH,
        ).wait_recv()
    for c in copies:
        c.wait_send()
    acc = buf2[0]
    for j in range(1, n_tm):
        acc = acc + buf2[j]
    buf3[s] = acc

    def send_p3(k, carry):
        space_copy(lambda b: buf3.at[s], buf3, send3, recv3, k).start()
        return carry

    lax.fori_loop(1, n_space, send_p3, 0)

    def wait_p3(k, carry):
        space_wait(buf3, send3, recv3, k)
        return carry

    lax.fori_loop(1, n_space, wait_p3, 0)

    def drain(k, carry):
        space_copy(lambda b: g_ref.at[b], buf1, send1, recv1, k).wait_send()
        space_copy(lambda b: buf3.at[s], buf3, send3, recv3, k).wait_send()
        return carry

    lax.fori_loop(1, n_space, drain, 0)
    out_ref[...] = buf3[...]


def a2a_body(n_tm, src_at, dst_at, x_ref, buf, send, recv, own):
    s = lax.axis_index("space")
    t = lax.axis_index("tm")
    copies = []
    for k in range(1, n_tm):
        a = lax.rem(t + k, n_tm)
        c = pltpu.make_async_remote_copy(
            src_ref=src_at(x_ref, a), dst_ref=dst_at(buf, t), send_sem=send.at[k], recv_sem=recv.at[t],
            device_id=(s, a), device_id_type=MESH,
        )
        c.start()
        copies.append(c)
    mine = pltpu.make_async_copy(src_at(x_ref, t), dst_at(buf, t), own.at[0])
    mine.start()
    mine.wait()
    for k in range(1, n_tm):
        j = lax.rem(t + k, n_tm)
        pltpu.make_async_remote_copy(
            src_ref=src_at(x_ref, j), dst_ref=dst_at(buf, j), send_sem=send.at[k], recv_sem=recv.at[j],
            device_id=(s, j), device_id_type=MESH,
        ).wait_recv()
    for c in copies:
        c.wait_send()


def fix_edges(vloc_ref, dudz_ref, halo, fix):
    f = lambda ref, i: ref[i].astype(jnp.float32)
    d = lambda ahead, behind, ahead_two, behind_two: (8.0 * (ahead - behind) - (ahead_two - behind_two)) / 12.0
    v = [f(vloc_ref, i) for i in range(8)]
    lo = [f(halo, 0), f(halo, 1)]
    hi = [f(halo, 2), f(halo, 3)]
    rows_dv = [
        d(v[1], lo[1], v[2], lo[0]),
        d(v[2], v[0], v[3], lo[1]),
        d(v[7], v[5], hi[0], v[4]),
        d(hi[0], v[6], hi[1], v[5]),
    ]
    for i in range(4):
        fix[i] = (rows_dv[i] - dudz_ref[i]).astype(fix.dtype)


def front_kernel(
    n_space, n_tm, x_ref, vloc_ref, dudz_ref, modes_ref, fixed_ref,
    cells, gpart, buf1, buf2, buf3, gfull, part, gathered, halo, fix, *sems,
):
    send, recv, own, esend, hsend, hrecv = sems[:6]
    s = lax.axis_index("space")
    t = lax.axis_index("tm")
    greet_all(n_space, n_tm)
    inner, _, cols = x_ref.shape
    rows = inner + 4
    width = cols // n_tm
    left = lax.rem(s + n_space - 1, n_space)
    right = lax.rem(s + 1, n_space)

    def remote(src_ref, dst_ref, ss, rs, dev):
        return pltpu.make_async_remote_copy(
            src_ref=src_ref, dst_ref=dst_ref, send_sem=ss, recv_sem=rs, device_id=dev, device_id_type=MESH
        )

    halo_out = [
        remote(vloc_ref.at[pl.ds(6, 2)], halo.at[pl.ds(0, 2)], hsend.at[0], hrecv.at[0], (right, t)),
        remote(vloc_ref.at[pl.ds(0, 2)], halo.at[pl.ds(2, 2)], hsend.at[1], hrecv.at[1], (left, t)),
    ]
    for c in halo_out:
        c.start()
    src = lambda ref, a, r0, nr: ref.at[pl.ds(r0, nr), :, lanes(a, width)]
    dst = lambda j, r0, nr: cells.at[pl.ds(r0, nr), pl.ds(j * RANK, RANK), :]
    copies = []
    for k in range(1, n_tm):
        a = lax.rem(t + k, n_tm)
        c = remote(src(x_ref, a, 0, inner), dst(t, 2, inner), send.at[k], recv.at[t], (s, a))
        c.start()
        copies.append(c)
    mine = pltpu.make_async_copy(src(x_ref, t, 0, inner), dst(t, 2, inner), own.at[0])
    mine.start()
    mine.wait()
    remote(vloc_ref.at[pl.ds(6, 2)], halo.at[pl.ds(0, 2)], hsend.at[0], hrecv.at[0], (left, t)).wait_recv()
    remote(vloc_ref.at[pl.ds(0, 2)], halo.at[pl.ds(2, 2)], hsend.at[1], hrecv.at[1], (right, t)).wait_recv()
    fix_edges(vloc_ref, dudz_ref, halo, fix)
    fixed_ref[...] = fix[...]
    for k in range(1, n_tm):
        a = lax.rem(t + k, n_tm)
        for e, (r0, d0) in enumerate(((0, 0), (2, rows - 2))):
            c = remote(src(fix, a, r0, 2), dst(t, d0, 2), esend.at[k, e], recv.at[t], (s, a))
            c.start()
            copies.append(c)
    for r0, d0 in ((0, 0), (2, rows - 2)):
        mine = pltpu.make_async_copy(src(fix, t, r0, 2), dst(t, d0, 2), own.at[0])
        mine.start()
        mine.wait()
    for k in range(1, n_tm):
        j = lax.rem(t + k, n_tm)
        remote(dst(j, 0, rows), dst(j, 0, rows), send.at[k], recv.at[j], (s, j)).wait_recv()
    for c in copies + halo_out:
        c.wait_send()
    size = cells.shape[1]
    gram = jnp.zeros((size, size), jnp.float32)
    for x in range(rows):
        w = cells[x]
        gram = gram + lax.dot_general(
            w, w, (((1,), (1,)), ((), ())), preferred_element_type=jnp.float32
        )
    gpart[...] = gram.reshape(gpart.shape)
    allreduce_body(n_space, n_tm, gpart, buf1, buf1, buf2, buf3, *sems[6:12])
    gfull[...] = buf3[...].reshape(gfull.shape)
    finish_body(n_tm, gfull, cells, modes_ref, part, gathered, *sems[12:])


def front(vort_x, vloc, dudz):
    n_space = lax.axis_size("space")
    n_tm = lax.axis_size("tm")
    inner, _, cols = vort_x.shape
    rows = inner + 4
    size = n_tm * RANK
    width = cols // n_tm
    cells_shape = (rows, size, width)
    chunks = (n_space, size // n_space, size)
    out_shape = (RANK // n_tm, rows, cols)
    edge_shape = (4, RANK, cols)
    return pl.pallas_call(
        functools.partial(front_kernel, n_space, n_tm),
        out_shape=(
            jax.ShapeDtypeStruct(out_shape, jnp.float32),
            jax.ShapeDtypeStruct(edge_shape, vort_x.dtype),
        ),
        in_specs=[pl.BlockSpec(memory_space=pltpu.VMEM)] * 3,
        out_specs=(pl.BlockSpec(memory_space=pltpu.VMEM), pl.BlockSpec(memory_space=pltpu.VMEM)),
        scratch_shapes=[
            pltpu.VMEM(cells_shape, vort_x.dtype),
            pltpu.VMEM(chunks, jnp.float32),
            pltpu.VMEM(chunks, jnp.float32),
            pltpu.VMEM((n_tm,) + chunks[1:], jnp.float32),
            pltpu.VMEM(chunks, jnp.float32),
            pltpu.VMEM((size, size), jnp.float32),
            pltpu.VMEM((RANK, rows, width), jnp.float32),
            pltpu.VMEM(out_shape, jnp.float32),
            pltpu.VMEM(edge_shape, vort_x.dtype),
            pltpu.VMEM(edge_shape, vort_x.dtype),
            pltpu.SemaphoreType.DMA((n_tm,)),
            pltpu.SemaphoreType.DMA((n_tm,)),
            pltpu.SemaphoreType.DMA((1,)),
            pltpu.SemaphoreType.DMA((n_tm, 2)),
            pltpu.SemaphoreType.DMA((2,)),
            pltpu.SemaphoreType.DMA((2,)),
            pltpu.SemaphoreType.DMA((n_space,)),
            pltpu.SemaphoreType.DMA((n_space,)),
            pltpu.SemaphoreType.DMA((n_tm,)),
            pltpu.SemaphoreType.DMA((n_tm,)),
            pltpu.SemaphoreType.DMA((n_space,)),
            pltpu.SemaphoreType.DMA((n_space,)),
            pltpu.SemaphoreType.DMA((n_tm,)),
            pltpu.SemaphoreType.DMA((n_tm,)),
            pltpu.SemaphoreType.DMA((1,)),
        ],
        compiler_params=pltpu.CompilerParams(collective_id=0, has_side_effects=True),
    )(vort_x, vloc, dudz)


def lanes(a, width):
    return pl.ds(pl.multiple_of(a * width, width), width)


def bdot(x, y):
    return jnp.einsum("nab,nbc->nac", x, y, precision=HIGH, preferred_element_type=jnp.float32)


def bdot_t(x, y):
    return jnp.einsum("nac,nbc->nab", x, y, precision=HIGH, preferred_element_type=jnp.float32)


def iotas(shape):
    return lax.broadcasted_iota(jnp.int32, shape, 1), lax.broadcasted_iota(jnp.int32, shape, 2)


def merge_coeffs(h):
    n = h.shape[0]
    kt = h[:, :RANK, :] + h[:, RANK:, :]
    row, col = iotas(h.shape)
    dcol = jnp.sum(jnp.where(row == col, h, 0.0), axis=2, keepdims=True)
    scales = jnp.sqrt(dcol[:, :RANK] + dcol[:, RANK:])
    inner = bdot_t(bdot(kt, h), kt)
    row, col = iotas(inner.shape)

    a = inner
    r = kt
    below = row[:, :, :1]
    for j in range(RANK):
        a_row = a[:, j : j + 1, :]
        r_row = r[:, j : j + 1, :]
        factor = jnp.where(below > j, a[:, :, j : j + 1] / a_row[:, :, j : j + 1], 0.0)
        a = a - factor * a_row
        r = r - factor * r_row
    diag_u = jnp.sum(jnp.where(row == col, a, 0.0), axis=2, keepdims=True)
    return r * (scales / jnp.sqrt(diag_u))


def split3(x):
    hi = x.astype(jnp.bfloat16)
    rest = x - hi.astype(jnp.float32)
    mid = rest.astype(jnp.bfloat16)
    lo = (rest - mid.astype(jnp.float32)).astype(jnp.bfloat16)
    return hi, mid, lo


def place(x, offset, width):
    n, r, w = x.shape
    row, col = iotas((n, w, width))
    pick = jnp.where(col == row + offset, 1.0, 0.0).astype(jnp.bfloat16)
    terms = jnp.einsum(
        "nab,nbc->nac", jnp.concatenate(split3(x), axis=1), pick, preferred_element_type=jnp.float32
    )
    return (terms[:, :r] + terms[:, r : 2 * r]) + terms[:, 2 * r :]


def tree_levels(g_ref):
    size = 2 * RANK
    leaves = g_ref.shape[0] // RANK
    picks = []
    for k in range(leaves // 2):
        lane0 = (k * size) // 128 * 128
        block = g_ref[k * size : (k + 1) * size, lane0 : lane0 + 128][None]
        picks.append(place(block, -(k * size - lane0), size))
    basis = merge_coeffs(jnp.concatenate(picks, axis=0))
    while basis.shape[0] > 1:
        n = basis.shape[0] // 2
        w = basis.shape[2]
        pairs = basis.reshape(n, 2, RANK, w)
        bt = jnp.concatenate(
            [place(pairs[:, 0], 0, 2 * w), place(pairs[:, 1], w, 2 * w)], axis=1
        )
        gs = jnp.concatenate(
            [g_ref[k * 2 * w : (k + 1) * 2 * w, k * 2 * w : (k + 1) * 2 * w][None] for k in range(n)],
            axis=0,
        )
        h = bdot_t(bdot(bt, gs), bt)
        basis = bdot(merge_coeffs(h), bt)
    return basis[0]


def finish_body(n_tm, g_ref, w_ref, out_ref, part_ref, buf, send, recv, own):
    s = lax.axis_index("space")
    t = lax.axis_index("tm")
    basis_t = tree_levels(g_ref)
    hi = basis_t.astype(jnp.bfloat16)
    rest = basis_t - hi.astype(jnp.float32)
    mid = rest.astype(jnp.bfloat16)
    lo = (rest - mid.astype(jnp.float32)).astype(jnp.bfloat16)
    pieces = jnp.concatenate([hi, mid, lo], axis=0)
    for x in range(w_ref.shape[0]):
        terms = jnp.dot(pieces, w_ref[x], preferred_element_type=jnp.float32)
        part_ref[:, x, :] = (terms[:RANK] + terms[RANK : 2 * RANK]) + terms[2 * RANK :]
    share = part_ref.shape[0] // n_tm
    width = w_ref.shape[2]
    src_at = lambda a: part_ref.at[pl.ds(a * share, share)]
    dst_at = lambda j: buf.at[:, :, lanes(j, width)]
    copies = []
    for k in range(1, n_tm):
        a = lax.rem(t + k, n_tm)
        c = pltpu.make_async_remote_copy(
            src_ref=src_at(a), dst_ref=dst_at(t), send_sem=send.at[k], recv_sem=recv.at[t],
            device_id=(s, a), device_id_type=MESH,
        )
        c.start()
        copies.append(c)
    mine = pltpu.make_async_copy(src_at(t), dst_at(t), own.at[0])
    mine.start()
    mine.wait()
    for k in range(1, n_tm):
        j = lax.rem(t + k, n_tm)
        pltpu.make_async_remote_copy(
            src_ref=src_at(j), dst_ref=dst_at(j), send_sem=send.at[k], recv_sem=recv.at[j],
            device_id=(s, j), device_id_type=MESH,
        ).wait_recv()
    for c in copies:
        c.wait_send()
    out_ref[...] = buf[...]


def local(velocity):
    rows = velocity.shape[2]
    span_v = velocity[:, 1].astype(jnp.float32)
    u = velocity[:, 0]
    cols = u.shape[2]
    wrapped = jnp.concatenate([u[:, :, cols - 2 :], u, u[:, :, :2]], axis=2)
    f32 = lambda lo: wrapped[:, :, lo : lo + cols].astype(jnp.float32)
    du_dz = (8.0 * (f32(3) - f32(1)) - (f32(4) - f32(0))) / 12.0
    dv_dx = (
        8.0 * (span_v[:, 3 : rows - 1] - span_v[:, 1 : rows - 3])
        - (span_v[:, 4:rows] - span_v[:, : rows - 4])
    ) / 12.0
    interior = (dv_dx - du_dz[:, 2 : rows - 2]).astype(jnp.bfloat16)
    v = velocity[:, 1]
    vloc = jnp.swapaxes(jnp.concatenate([v[:, :4], v[:, rows - 4 :]], axis=1), 0, 1)
    dudz = jnp.swapaxes(jnp.concatenate([du_dz[:, :2], du_dz[:, rows - 2 :]], axis=1), 0, 1)
    modes, fixed = front(jnp.swapaxes(interior, 0, 1), vloc, dudz)
    fixed = jnp.swapaxes(fixed, 0, 1)
    vorticity = jnp.concatenate([fixed[:, :2], interior, fixed[:, 2:]], axis=1)
    return (vorticity, modes)


def solution(mesh):
    in_specs = (P("tm", None, "space", None),)
    out_specs = (P("tm", "space", None), P("tm", "space", None))
    return jax.shard_map(local, mesh=mesh, in_specs=in_specs, out_specs=out_specs, check_vma=False)
```

```python
import functools

import jax
import jax.numpy as jnp
from jax import lax
from jax.experimental import pallas as pl
from jax.experimental.pallas import tpu as pltpu
from jax.sharding import PartitionSpec as P

RANK = 32
HIGH = lax.Precision.HIGHEST


def halo_rows(block, width):
    count = lax.axis_size("space")
    forward = [(i, (i + 1) % count) for i in range(count)]
    backward = [(target, source) for source, target in forward]
    rows = block.shape[1]
    low = lax.ppermute(block[:, rows - width :], "space", forward)
    high = lax.ppermute(block[:, :width], "space", backward)
    return jnp.concatenate([low, block, high], axis=1)


def spanwise(field):
    ahead = jnp.roll(field, -1, 2)
    behind = jnp.roll(field, 1, 2)
    ahead_two = jnp.roll(field, -2, 2)
    behind_two = jnp.roll(field, 2, 2)
    return (8.0 * (ahead - behind) - (ahead_two - behind_two)) / 12.0


MESH = pl.DeviceIdType.MESH


def greet_all(n_space, n_tm):
    s = lax.axis_index("space")
    t = lax.axis_index("tm")
    barrier = pltpu.get_barrier_semaphore()

    def greet_space(k, carry):
        b = lax.rem(s + k, n_space)
        pl.semaphore_signal(barrier, inc=1, device_id=(b, t), device_id_type=MESH)
        return carry

    def greet_tm(k, carry):
        a = lax.rem(t + k, n_tm)
        pl.semaphore_signal(barrier, inc=1, device_id=(s, a), device_id_type=MESH)
        return carry

    lax.fori_loop(1, n_space, greet_space, 0)
    lax.fori_loop(1, n_tm, greet_tm, 0)
    pl.semaphore_wait(barrier, (n_space - 1) + (n_tm - 1))


def allreduce_body(n_space, n_tm, g_ref, out_ref, buf1, buf2, buf3, send1, recv1, send2, recv2, send3, recv3):
    s = lax.axis_index("space")
    t = lax.axis_index("tm")

    def space_copy(src, dst_buf, send, recv, k):
        b = lax.rem(s + k, n_space)
        return pltpu.make_async_remote_copy(
            src_ref=src(b), dst_ref=dst_buf.at[s], send_sem=send.at[k], recv_sem=recv.at[s],
            device_id=(b, t), device_id_type=MESH,
        )

    def space_wait(dst_buf, send, recv, k):
        j = lax.rem(s + k, n_space)
        pltpu.make_async_remote_copy(
            src_ref=dst_buf.at[j], dst_ref=dst_buf.at[j], send_sem=send.at[k], recv_sem=recv.at[j],
            device_id=(j, t), device_id_type=MESH,
        ).wait_recv()

    def send_p1(k, carry):
        space_copy(lambda b: g_ref.at[b], buf1, send1, recv1, k).start()
        return carry

    lax.fori_loop(1, n_space, send_p1, 0)
    buf1[s] = g_ref[s]

    def wait_p1(k, carry):
        space_wait(buf1, send1, recv1, k)
        return carry

    lax.fori_loop(1, n_space, wait_p1, 0)
    acc = buf1[0]
    for j in range(1, n_space):
        acc = acc + buf1[j]
    buf2[t] = acc

    copies = []
    for k in range(1, n_tm):
        a = lax.rem(t + k, n_tm)
        c = pltpu.make_async_remote_copy(
            src_ref=buf2.at[t], dst_ref=buf2.at[t], send_sem=send2.at[k], recv_sem=recv2.at[t],
            device_id=(s, a), device_id_type=MESH,
        )
        c.start()
        copies.append(c)
    for k in range(1, n_tm):
        j = lax.rem(t + k, n_tm)
        pltpu.make_async_remote_copy(
            src_ref=buf2.at[j], dst_ref=buf2.at[j], send_sem=send2.at[k], recv_sem=recv2.at[j],
            device_id=(s, j), device_id_type=MESH,
        ).wait_recv()
    for c in copies:
        c.wait_send()
    acc = buf2[0]
    for j in range(1, n_tm):
        acc = acc + buf2[j]
    buf3[s] = acc

    def send_p3(k, carry):
        space_copy(lambda b: buf3.at[s], buf3, send3, recv3, k).start()
        return carry

    lax.fori_loop(1, n_space, send_p3, 0)

    def wait_p3(k, carry):
        space_wait(buf3, send3, recv3, k)
        return carry

    lax.fori_loop(1, n_space, wait_p3, 0)

    def drain(k, carry):
        space_copy(lambda b: g_ref.at[b], buf1, send1, recv1, k).wait_send()
        space_copy(lambda b: buf3.at[s], buf3, send3, recv3, k).wait_send()
        return carry

    lax.fori_loop(1, n_space, drain, 0)
    out_ref[...] = buf3[...]


def a2a_body(n_tm, src_at, dst_at, x_ref, buf, send, recv, own):
    s = lax.axis_index("space")
    t = lax.axis_index("tm")
    copies = []
    for k in range(1, n_tm):
        a = lax.rem(t + k, n_tm)
        c = pltpu.make_async_remote_copy(
            src_ref=src_at(x_ref, a), dst_ref=dst_at(buf, t), send_sem=send.at[k], recv_sem=recv.at[t],
            device_id=(s, a), device_id_type=MESH,
        )
        c.start()
        copies.append(c)
    mine = pltpu.make_async_copy(src_at(x_ref, t), dst_at(buf, t), own.at[0])
    mine.start()
    mine.wait()
    for k in range(1, n_tm):
        j = lax.rem(t + k, n_tm)
        pltpu.make_async_remote_copy(
            src_ref=src_at(x_ref, j), dst_ref=dst_at(buf, j), send_sem=send.at[k], recv_sem=recv.at[j],
            device_id=(s, j), device_id_type=MESH,
        ).wait_recv()
    for c in copies:
        c.wait_send()


def fix_edges(vloc_ref, dudz_ref, halo, fix):
    f = lambda ref, i: ref[i].astype(jnp.float32)
    d = lambda ahead, behind, ahead_two, behind_two: (8.0 * (ahead - behind) - (ahead_two - behind_two)) / 12.0
    v = [f(vloc_ref, i) for i in range(8)]
    lo = [f(halo, 0), f(halo, 1)]
    hi = [f(halo, 2), f(halo, 3)]
    rows_dv = [
        d(v[1], lo[1], v[2], lo[0]),
        d(v[2], v[0], v[3], lo[1]),
        d(v[7], v[5], hi[0], v[4]),
        d(hi[0], v[6], hi[1], v[5]),
    ]
    for i in range(4):
        fix[i] = (rows_dv[i] - dudz_ref[i]).astype(fix.dtype)


def front_kernel(
    n_space, n_tm, x_ref, vloc_ref, dudz_ref, modes_ref, fixed_ref,
    cells, gpart, buf1, buf2, buf3, gfull, part, gathered, halo, fix, *sems,
):
    send, recv, own, esend, hsend, hrecv = sems[:6]
    s = lax.axis_index("space")
    t = lax.axis_index("tm")
    greet_all(n_space, n_tm)
    inner, _, cols = x_ref.shape
    rows = inner + 4
    width = cols // n_tm
    left = lax.rem(s + n_space - 1, n_space)
    right = lax.rem(s + 1, n_space)

    def remote(src_ref, dst_ref, ss, rs, dev):
        return pltpu.make_async_remote_copy(
            src_ref=src_ref, dst_ref=dst_ref, send_sem=ss, recv_sem=rs, device_id=dev, device_id_type=MESH
        )

    halo_out = [
        remote(vloc_ref.at[pl.ds(6, 2)], halo.at[pl.ds(0, 2)], hsend.at[0], hrecv.at[0], (right, t)),
        remote(vloc_ref.at[pl.ds(0, 2)], halo.at[pl.ds(2, 2)], hsend.at[1], hrecv.at[1], (left, t)),
    ]
    for c in halo_out:
        c.start()
    src = lambda ref, a, r0, nr: ref.at[pl.ds(r0, nr), :, lanes(a, width)]
    dst = lambda j, r0, nr: cells.at[pl.ds(r0, nr), pl.ds(j * RANK, RANK), :]
    copies = []
    for k in range(1, n_tm):
        a = lax.rem(t + k, n_tm)
        c = remote(src(x_ref, a, 0, inner), dst(t, 2, inner), send.at[k], recv.at[t], (s, a))
        c.start()
        copies.append(c)
    mine = pltpu.make_async_copy(src(x_ref, t, 0, inner), dst(t, 2, inner), own.at[0])
    mine.start()
    remote(vloc_ref.at[pl.ds(6, 2)], halo.at[pl.ds(0, 2)], hsend.at[0], hrecv.at[0], (left, t)).wait_recv()
    remote(vloc_ref.at[pl.ds(0, 2)], halo.at[pl.ds(2, 2)], hsend.at[1], hrecv.at[1], (right, t)).wait_recv()
    fix_edges(vloc_ref, dudz_ref, halo, fix)
    fixed_ref[...] = fix[...]
    for k in range(1, n_tm):
        a = lax.rem(t + k, n_tm)
        for e, (r0, d0) in enumerate(((0, 0), (2, rows - 2))):
            c = remote(src(fix, a, r0, 2), dst(t, d0, 2), esend.at[k, e], recv.at[t], (s, a))
            c.start()
            copies.append(c)
    mine.wait()
    for r0, d0 in ((0, 0), (2, rows - 2)):
        mine = pltpu.make_async_copy(src(fix, t, r0, 2), dst(t, d0, 2), own.at[0])
        mine.start()
        mine.wait()
    for k in range(1, n_tm):
        j = lax.rem(t + k, n_tm)
        remote(dst(j, 0, rows), dst(j, 0, rows), send.at[k], recv.at[j], (s, j)).wait_recv()
    for c in copies + halo_out:
        c.wait_send()
    size = cells.shape[1]
    gram = jnp.zeros((size, size), jnp.float32)
    for x in range(rows):
        w = cells[x]
        gram = gram + lax.dot_general(
            w, w, (((1,), (1,)), ((), ())), preferred_element_type=jnp.float32
        )
    gpart[...] = gram.reshape(gpart.shape)
    allreduce_body(n_space, n_tm, gpart, buf1, buf1, buf2, buf3, *sems[6:12])
    gfull[...] = buf3[...].reshape(gfull.shape)
    finish_body(n_tm, gfull, cells, modes_ref, part, gathered, *sems[12:])


def front(vort_x, vloc, dudz):
    n_space = lax.axis_size("space")
    n_tm = lax.axis_size("tm")
    inner, _, cols = vort_x.shape
    rows = inner + 4
    size = n_tm * RANK
    width = cols // n_tm
    cells_shape = (rows, size, width)
    chunks = (n_space, size // n_space, size)
    out_shape = (RANK // n_tm, rows, cols)
    edge_shape = (4, RANK, cols)
    return pl.pallas_call(
        functools.partial(front_kernel, n_space, n_tm),
        out_shape=(
            jax.ShapeDtypeStruct(out_shape, jnp.float32),
            jax.ShapeDtypeStruct(edge_shape, vort_x.dtype),
        ),
        in_specs=[pl.BlockSpec(memory_space=pltpu.VMEM)] * 3,
        out_specs=(pl.BlockSpec(memory_space=pltpu.VMEM), pl.BlockSpec(memory_space=pltpu.VMEM)),
        scratch_shapes=[
            pltpu.VMEM(cells_shape, vort_x.dtype),
            pltpu.VMEM(chunks, jnp.float32),
            pltpu.VMEM(chunks, jnp.float32),
            pltpu.VMEM((n_tm,) + chunks[1:], jnp.float32),
            pltpu.VMEM(chunks, jnp.float32),
            pltpu.VMEM((size, size), jnp.float32),
            pltpu.VMEM((RANK, rows, width), jnp.float32),
            pltpu.VMEM(out_shape, jnp.float32),
            pltpu.VMEM(edge_shape, vort_x.dtype),
            pltpu.VMEM(edge_shape, vort_x.dtype),
            pltpu.SemaphoreType.DMA((n_tm,)),
            pltpu.SemaphoreType.DMA((n_tm,)),
            pltpu.SemaphoreType.DMA((1,)),
            pltpu.SemaphoreType.DMA((n_tm, 2)),
            pltpu.SemaphoreType.DMA((2,)),
            pltpu.SemaphoreType.DMA((2,)),
            pltpu.SemaphoreType.DMA((n_space,)),
            pltpu.SemaphoreType.DMA((n_space,)),
            pltpu.SemaphoreType.DMA((n_tm,)),
            pltpu.SemaphoreType.DMA((n_tm,)),
            pltpu.SemaphoreType.DMA((n_space,)),
            pltpu.SemaphoreType.DMA((n_space,)),
            pltpu.SemaphoreType.DMA((n_tm,)),
            pltpu.SemaphoreType.DMA((n_tm,)),
            pltpu.SemaphoreType.DMA((1,)),
        ],
        compiler_params=pltpu.CompilerParams(collective_id=0, has_side_effects=True),
    )(vort_x, vloc, dudz)


def lanes(a, width):
    return pl.ds(pl.multiple_of(a * width, width), width)


def bdot(x, y):
    return jnp.einsum("nab,nbc->nac", x, y, precision=HIGH, preferred_element_type=jnp.float32)


def bdot_t(x, y):
    return jnp.einsum("nac,nbc->nab", x, y, precision=HIGH, preferred_element_type=jnp.float32)


def iotas(shape):
    return lax.broadcasted_iota(jnp.int32, shape, 1), lax.broadcasted_iota(jnp.int32, shape, 2)


def merge_coeffs(h):
    n = h.shape[0]
    kt = h[:, :RANK, :] + h[:, RANK:, :]
    row, col = iotas(h.shape)
    dcol = jnp.sum(jnp.where(row == col, h, 0.0), axis=2, keepdims=True)
    scales = jnp.sqrt(dcol[:, :RANK] + dcol[:, RANK:])
    inner = bdot_t(bdot(kt, h), kt)
    row, col = iotas(inner.shape)

    a = inner
    r = kt
    below = row[:, :, :1]
    for j in range(RANK):
        a_row = a[:, j : j + 1, :]
        r_row = r[:, j : j + 1, :]
        factor = jnp.where(below > j, a[:, :, j : j + 1] / a_row[:, :, j : j + 1], 0.0)
        a = a - factor * a_row
        r = r - factor * r_row
    diag_u = jnp.sum(jnp.where(row == col, a, 0.0), axis=2, keepdims=True)
    return r * (scales / jnp.sqrt(diag_u))


def split3(x):
    hi = x.astype(jnp.bfloat16)
    rest = x - hi.astype(jnp.float32)
    mid = rest.astype(jnp.bfloat16)
    lo = (rest - mid.astype(jnp.float32)).astype(jnp.bfloat16)
    return hi, mid, lo


def place(x, offset, width):
    n, r, w = x.shape
    row, col = iotas((n, w, width))
    pick = jnp.where(col == row + offset, 1.0, 0.0).astype(jnp.bfloat16)
    terms = jnp.einsum(
        "nab,nbc->nac", jnp.concatenate(split3(x), axis=1), pick, preferred_element_type=jnp.float32
    )
    return (terms[:, :r] + terms[:, r : 2 * r]) + terms[:, 2 * r :]


def tree_levels(g_ref):
    size = 2 * RANK
    leaves = g_ref.shape[0] // RANK
    picks = []
    for k in range(leaves // 2):
        lane0 = (k * size) // 128 * 128
        block = g_ref[k * size : (k + 1) * size, lane0 : lane0 + 128][None]
        picks.append(place(block, -(k * size - lane0), size))
    basis = merge_coeffs(jnp.concatenate(picks, axis=0))
    while basis.shape[0] > 1:
        n = basis.shape[0] // 2
        w = basis.shape[2]
        pairs = basis.reshape(n, 2, RANK, w)
        bt = jnp.concatenate(
            [place(pairs[:, 0], 0, 2 * w), place(pairs[:, 1], w, 2 * w)], axis=1
        )
        gs = jnp.concatenate(
            [g_ref[k * 2 * w : (k + 1) * 2 * w, k * 2 * w : (k + 1) * 2 * w][None] for k in range(n)],
            axis=0,
        )
        h = bdot_t(bdot(bt, gs), bt)
        basis = bdot(merge_coeffs(h), bt)
    return basis[0]


def finish_body(n_tm, g_ref, w_ref, out_ref, part_ref, buf, send, recv, own):
    s = lax.axis_index("space")
    t = lax.axis_index("tm")
    basis_t = tree_levels(g_ref)
    hi = basis_t.astype(jnp.bfloat16)
    rest = basis_t - hi.astype(jnp.float32)
    mid = rest.astype(jnp.bfloat16)
    lo = (rest - mid.astype(jnp.float32)).astype(jnp.bfloat16)
    pieces = jnp.concatenate([hi, mid, lo], axis=0)
    for x in range(w_ref.shape[0]):
        terms = jnp.dot(pieces, w_ref[x], preferred_element_type=jnp.float32)
        part_ref[:, x, :] = (terms[:RANK] + terms[RANK : 2 * RANK]) + terms[2 * RANK :]
    share = part_ref.shape[0] // n_tm
    width = w_ref.shape[2]
    src_at = lambda a: part_ref.at[pl.ds(a * share, share)]
    dst_at = lambda j: buf.at[:, :, lanes(j, width)]
    copies = []
    for k in range(1, n_tm):
        a = lax.rem(t + k, n_tm)
        c = pltpu.make_async_remote_copy(
            src_ref=src_at(a), dst_ref=dst_at(t), send_sem=send.at[k], recv_sem=recv.at[t],
            device_id=(s, a), device_id_type=MESH,
        )
        c.start()
        copies.append(c)
    mine = pltpu.make_async_copy(src_at(t), dst_at(t), own.at[0])
    mine.start()
    mine.wait()
    for k in range(1, n_tm):
        j = lax.rem(t + k, n_tm)
        pltpu.make_async_remote_copy(
            src_ref=src_at(j), dst_ref=dst_at(j), send_sem=send.at[k], recv_sem=recv.at[j],
            device_id=(s, j), device_id_type=MESH,
        ).wait_recv()
    for c in copies:
        c.wait_send()
    out_ref[...] = buf[...]


def local(velocity):
    rows = velocity.shape[2]
    span_v = velocity[:, 1].astype(jnp.float32)
    u = velocity[:, 0]
    cols = u.shape[2]
    wrapped = jnp.concatenate([u[:, :, cols - 2 :], u, u[:, :, :2]], axis=2)
    f32 = lambda lo: wrapped[:, :, lo : lo + cols].astype(jnp.float32)
    du_dz = (8.0 * (f32(3) - f32(1)) - (f32(4) - f32(0))) / 12.0
    dv_dx = (
        8.0 * (span_v[:, 3 : rows - 1] - span_v[:, 1 : rows - 3])
        - (span_v[:, 4:rows] - span_v[:, : rows - 4])
    ) / 12.0
    interior = (dv_dx - du_dz[:, 2 : rows - 2]).astype(jnp.bfloat16)
    v = velocity[:, 1]
    vloc = jnp.swapaxes(jnp.concatenate([v[:, :4], v[:, rows - 4 :]], axis=1), 0, 1)
    dudz = jnp.swapaxes(jnp.concatenate([du_dz[:, :2], du_dz[:, rows - 2 :]], axis=1), 0, 1)
    modes, fixed = front(jnp.swapaxes(interior, 0, 1), vloc, dudz)
    fixed = jnp.swapaxes(fixed, 0, 1)
    vorticity = jnp.concatenate([fixed[:, :2], interior, fixed[:, 2:]], axis=1)
    return (vorticity, modes)


def solution(mesh):
    in_specs = (P("tm", None, "space", None),)
    out_specs = (P("tm", "space", None), P("tm", "space", None))
    return jax.shard_map(local, mesh=mesh, in_specs=in_specs, out_specs=out_specs, check_vma=False)
```

```python
import functools

import jax
import jax.numpy as jnp
from jax import lax
from jax.experimental import pallas as pl
from jax.experimental.pallas import tpu as pltpu
from jax.sharding import PartitionSpec as P

RANK = 32
HIGH = lax.Precision.HIGHEST


def halo_rows(block, width):
    count = lax.axis_size("space")
    forward = [(i, (i + 1) % count) for i in range(count)]
    backward = [(target, source) for source, target in forward]
    rows = block.shape[1]
    low = lax.ppermute(block[:, rows - width :], "space", forward)
    high = lax.ppermute(block[:, :width], "space", backward)
    return jnp.concatenate([low, block, high], axis=1)


def spanwise(field):
    ahead = jnp.roll(field, -1, 2)
    behind = jnp.roll(field, 1, 2)
    ahead_two = jnp.roll(field, -2, 2)
    behind_two = jnp.roll(field, 2, 2)
    return (8.0 * (ahead - behind) - (ahead_two - behind_two)) / 12.0


MESH = pl.DeviceIdType.MESH


def greet_all(n_space, n_tm):
    s = lax.axis_index("space")
    t = lax.axis_index("tm")
    barrier = pltpu.get_barrier_semaphore()

    def greet_space(k, carry):
        b = lax.rem(s + k, n_space)
        pl.semaphore_signal(barrier, inc=1, device_id=(b, t), device_id_type=MESH)
        return carry

    def greet_tm(k, carry):
        a = lax.rem(t + k, n_tm)
        pl.semaphore_signal(barrier, inc=1, device_id=(s, a), device_id_type=MESH)
        return carry

    lax.fori_loop(1, n_space, greet_space, 0)
    lax.fori_loop(1, n_tm, greet_tm, 0)
    pl.semaphore_wait(barrier, (n_space - 1) + (n_tm - 1))


def allreduce_body(n_space, n_tm, g_ref, out_ref, buf1, buf2, buf3, send1, recv1, send2, recv2, send3, recv3):
    s = lax.axis_index("space")
    t = lax.axis_index("tm")

    def space_copy(src, dst_buf, send, recv, k):
        b = lax.rem(s + k, n_space)
        return pltpu.make_async_remote_copy(
            src_ref=src(b), dst_ref=dst_buf.at[s], send_sem=send.at[k], recv_sem=recv.at[s],
            device_id=(b, t), device_id_type=MESH,
        )

    def space_wait(dst_buf, send, recv, k):
        j = lax.rem(s + k, n_space)
        pltpu.make_async_remote_copy(
            src_ref=dst_buf.at[j], dst_ref=dst_buf.at[j], send_sem=send.at[k], recv_sem=recv.at[j],
            device_id=(j, t), device_id_type=MESH,
        ).wait_recv()

    def send_p1(k, carry):
        space_copy(lambda b: g_ref.at[b], buf1, send1, recv1, k).start()
        return carry

    lax.fori_loop(1, n_space, send_p1, 0)
    buf1[s] = g_ref[s]

    def wait_p1(k, carry):
        space_wait(buf1, send1, recv1, k)
        return carry

    lax.fori_loop(1, n_space, wait_p1, 0)
    acc = buf1[0]
    for j in range(1, n_space):
        acc = acc + buf1[j]
    buf2[t] = acc

    copies = []
    for k in range(1, n_tm):
        a = lax.rem(t + k, n_tm)
        c = pltpu.make_async_remote_copy(
            src_ref=buf2.at[t], dst_ref=buf2.at[t], send_sem=send2.at[k], recv_sem=recv2.at[t],
            device_id=(s, a), device_id_type=MESH,
        )
        c.start()
        copies.append(c)
    for k in range(1, n_tm):
        j = lax.rem(t + k, n_tm)
        pltpu.make_async_remote_copy(
            src_ref=buf2.at[j], dst_ref=buf2.at[j], send_sem=send2.at[k], recv_sem=recv2.at[j],
            device_id=(s, j), device_id_type=MESH,
        ).wait_recv()
    for c in copies:
        c.wait_send()
    acc = buf2[0]
    for j in range(1, n_tm):
        acc = acc + buf2[j]
    buf3[s] = acc

    def send_p3(k, carry):
        space_copy(lambda b: buf3.at[s], buf3, send3, recv3, k).start()
        return carry

    lax.fori_loop(1, n_space, send_p3, 0)

    def wait_p3(k, carry):
        space_wait(buf3, send3, recv3, k)
        return carry

    lax.fori_loop(1, n_space, wait_p3, 0)

    def drain(k, carry):
        space_copy(lambda b: g_ref.at[b], buf1, send1, recv1, k).wait_send()
        space_copy(lambda b: buf3.at[s], buf3, send3, recv3, k).wait_send()
        return carry

    lax.fori_loop(1, n_space, drain, 0)
    out_ref[...] = buf3[...]


def a2a_body(n_tm, src_at, dst_at, x_ref, buf, send, recv, own):
    s = lax.axis_index("space")
    t = lax.axis_index("tm")
    copies = []
    for k in range(1, n_tm):
        a = lax.rem(t + k, n_tm)
        c = pltpu.make_async_remote_copy(
            src_ref=src_at(x_ref, a), dst_ref=dst_at(buf, t), send_sem=send.at[k], recv_sem=recv.at[t],
            device_id=(s, a), device_id_type=MESH,
        )
        c.start()
        copies.append(c)
    mine = pltpu.make_async_copy(src_at(x_ref, t), dst_at(buf, t), own.at[0])
    mine.start()
    mine.wait()
    for k in range(1, n_tm):
        j = lax.rem(t + k, n_tm)
        pltpu.make_async_remote_copy(
            src_ref=src_at(x_ref, j), dst_ref=dst_at(buf, j), send_sem=send.at[k], recv_sem=recv.at[j],
            device_id=(s, j), device_id_type=MESH,
        ).wait_recv()
    for c in copies:
        c.wait_send()


def fix_edges(vloc_ref, dudz_ref, halo, fix):
    f = lambda ref, i: ref[i].astype(jnp.float32)
    d = lambda ahead, behind, ahead_two, behind_two: (8.0 * (ahead - behind) - (ahead_two - behind_two)) / 12.0
    v = [f(vloc_ref, i) for i in range(8)]
    lo = [f(halo, 0), f(halo, 1)]
    hi = [f(halo, 2), f(halo, 3)]
    rows_dv = [
        d(v[1], lo[1], v[2], lo[0]),
        d(v[2], v[0], v[3], lo[1]),
        d(v[7], v[5], hi[0], v[4]),
        d(hi[0], v[6], hi[1], v[5]),
    ]
    for i in range(4):
        fix[i] = (rows_dv[i] - dudz_ref[i]).astype(fix.dtype)


def front_kernel(
    n_space, n_tm, x_ref, vloc_ref, dudz_ref, modes_ref, fixed_ref,
    cells, gpart, buf1, buf2, buf3, gfull, part, gathered, halo, fix, *sems,
):
    send, recv, own, esend, hsend, hrecv = sems[:6]
    s = lax.axis_index("space")
    t = lax.axis_index("tm")
    greet_all(n_space, n_tm)
    inner, _, cols = x_ref.shape
    rows = inner + 4
    width = cols // n_tm
    left = lax.rem(s + n_space - 1, n_space)
    right = lax.rem(s + 1, n_space)

    def remote(src_ref, dst_ref, ss, rs, dev):
        return pltpu.make_async_remote_copy(
            src_ref=src_ref, dst_ref=dst_ref, send_sem=ss, recv_sem=rs, device_id=dev, device_id_type=MESH
        )

    halo_out = [
        remote(vloc_ref.at[pl.ds(6, 2)], halo.at[pl.ds(0, 2)], hsend.at[0], hrecv.at[0], (right, t)),
        remote(vloc_ref.at[pl.ds(0, 2)], halo.at[pl.ds(2, 2)], hsend.at[1], hrecv.at[1], (left, t)),
    ]
    for c in halo_out:
        c.start()
    src = lambda ref, a, r0, nr: ref.at[pl.ds(r0, nr), :, lanes(a, width)]
    dst = lambda j, r0, nr: cells.at[pl.ds(r0, nr), pl.ds(j * RANK, RANK), :]
    copies = []
    for k in range(1, n_tm):
        a = lax.rem(t + k, n_tm)
        c = remote(src(x_ref, a, 0, inner), dst(t, 2, inner), send.at[k], recv.at[t], (s, a))
        c.start()
        copies.append(c)
    mine = pltpu.make_async_copy(src(x_ref, t, 0, inner), dst(t, 2, inner), own.at[0])
    mine.start()
    remote(vloc_ref.at[pl.ds(6, 2)], halo.at[pl.ds(0, 2)], hsend.at[0], hrecv.at[0], (left, t)).wait_recv()
    remote(vloc_ref.at[pl.ds(0, 2)], halo.at[pl.ds(2, 2)], hsend.at[1], hrecv.at[1], (right, t)).wait_recv()
    fix_edges(vloc_ref, dudz_ref, halo, fix)
    fixed_ref[...] = fix[...]
    for k in range(1, n_tm):
        a = lax.rem(t + k, n_tm)
        for e, (r0, d0) in enumerate(((0, 0), (2, rows - 2))):
            c = remote(src(fix, a, r0, 2), dst(t, d0, 2), esend.at[k, e], recv.at[t], (s, a))
            c.start()
            copies.append(c)
    mine.wait()
    for r0, d0 in ((0, 0), (2, rows - 2)):
        mine = pltpu.make_async_copy(src(fix, t, r0, 2), dst(t, d0, 2), own.at[0])
        mine.start()
        mine.wait()
    for k in range(1, n_tm):
        j = lax.rem(t + k, n_tm)
        remote(dst(j, 0, rows), dst(j, 0, rows), send.at[k], recv.at[j], (s, j)).wait_recv()
    for c in copies + halo_out:
        c.wait_send()
    size = cells.shape[1]
    gram = jnp.zeros((size, size), jnp.float32)
    for x in range(rows):
        w = cells[x]
        gram = gram + lax.dot_general(
            w, w, (((1,), (1,)), ((), ())), preferred_element_type=jnp.float32
        )
    gpart[...] = gram.reshape(gpart.shape)
    allreduce_body(n_space, n_tm, gpart, buf1, buf1, buf2, buf3, *sems[6:12])
    gfull[...] = buf3[...].reshape(gfull.shape)
    finish_body(n_tm, gfull, cells, modes_ref, part, gathered, *sems[12:])


def front(vort_x, vloc, dudz):
    n_space = lax.axis_size("space")
    n_tm = lax.axis_size("tm")
    inner, _, cols = vort_x.shape
    rows = inner + 4
    size = n_tm * RANK
    width = cols // n_tm
    cells_shape = (rows, size, width)
    chunks = (n_space, size // n_space, size)
    out_shape = (RANK // n_tm, rows, cols)
    edge_shape = (4, RANK, cols)
    return pl.pallas_call(
        functools.partial(front_kernel, n_space, n_tm),
        out_shape=(
            jax.ShapeDtypeStruct(out_shape, jnp.float32),
            jax.ShapeDtypeStruct(edge_shape, vort_x.dtype),
        ),
        in_specs=[pl.BlockSpec(memory_space=pltpu.VMEM)] * 3,
        out_specs=(pl.BlockSpec(memory_space=pltpu.VMEM), pl.BlockSpec(memory_space=pltpu.VMEM)),
        scratch_shapes=[
            pltpu.VMEM(cells_shape, vort_x.dtype),
            pltpu.VMEM(chunks, jnp.float32),
            pltpu.VMEM(chunks, jnp.float32),
            pltpu.VMEM((n_tm,) + chunks[1:], jnp.float32),
            pltpu.VMEM(chunks, jnp.float32),
            pltpu.VMEM((size, size), jnp.float32),
            pltpu.VMEM((RANK, rows, width), jnp.float32),
            pltpu.VMEM(out_shape, jnp.float32),
            pltpu.VMEM(edge_shape, vort_x.dtype),
            pltpu.VMEM(edge_shape, vort_x.dtype),
            pltpu.SemaphoreType.DMA((n_tm,)),
            pltpu.SemaphoreType.DMA((n_tm,)),
            pltpu.SemaphoreType.DMA((1,)),
            pltpu.SemaphoreType.DMA((n_tm, 2)),
            pltpu.SemaphoreType.DMA((2,)),
            pltpu.SemaphoreType.DMA((2,)),
            pltpu.SemaphoreType.DMA((n_space,)),
            pltpu.SemaphoreType.DMA((n_space,)),
            pltpu.SemaphoreType.DMA((n_tm,)),
            pltpu.SemaphoreType.DMA((n_tm,)),
            pltpu.SemaphoreType.DMA((n_space,)),
            pltpu.SemaphoreType.DMA((n_space,)),
            pltpu.SemaphoreType.DMA((n_tm,)),
            pltpu.SemaphoreType.DMA((n_tm,)),
            pltpu.SemaphoreType.DMA((1,)),
        ],
        compiler_params=pltpu.CompilerParams(collective_id=0, has_side_effects=True),
    )(vort_x, vloc, dudz)


def lanes(a, width):
    return pl.ds(pl.multiple_of(a * width, width), width)


def bdot(x, y):
    return jnp.einsum("nab,nbc->nac", x, y, precision=HIGH, preferred_element_type=jnp.float32)


def bdot_t(x, y):
    return jnp.einsum("nac,nbc->nab", x, y, precision=HIGH, preferred_element_type=jnp.float32)


def iotas(shape):
    return lax.broadcasted_iota(jnp.int32, shape, 1), lax.broadcasted_iota(jnp.int32, shape, 2)


def merge_coeffs(h):
    n = h.shape[0]
    kt = h[:, :RANK, :] + h[:, RANK:, :]
    row, col = iotas(h.shape)
    dcol = jnp.sum(jnp.where(row == col, h, 0.0), axis=2, keepdims=True)
    scales = jnp.sqrt(dcol[:, :RANK] + dcol[:, RANK:])
    inner = bdot_t(bdot(kt, h), kt)
    row, col = iotas(inner.shape)

    a = inner
    r = kt
    below = row[:, :, :1]
    for j in range(RANK):
        a_row = a[:, j : j + 1, :]
        r_row = r[:, j : j + 1, :]
        factor = jnp.where(below > j, a[:, :, j : j + 1] / a_row[:, :, j : j + 1], 0.0)
        a = a - factor * a_row
        r = r - factor * r_row
    diag_u = jnp.sum(jnp.where(row == col, a, 0.0), axis=2, keepdims=True)
    return r * (scales / jnp.sqrt(diag_u))


def split3(x):
    hi = x.astype(jnp.bfloat16)
    rest = x - hi.astype(jnp.float32)
    mid = rest.astype(jnp.bfloat16)
    lo = (rest - mid.astype(jnp.float32)).astype(jnp.bfloat16)
    return hi, mid, lo


def place(x, offset, width):
    n, r, w = x.shape
    row, col = iotas((n, w, width))
    pick = jnp.where(col == row + offset, 1.0, 0.0).astype(jnp.bfloat16)
    terms = jnp.einsum(
        "nab,nbc->nac", jnp.concatenate(split3(x), axis=1), pick, preferred_element_type=jnp.float32
    )
    return (terms[:, :r] + terms[:, r : 2 * r]) + terms[:, 2 * r :]


def tree_levels(g_ref):
    size = 2 * RANK
    leaves = g_ref.shape[0] // RANK
    picks = []
    for k in range(leaves // 2):
        lane0 = (k * size) // 128 * 128
        block = g_ref[k * size : (k + 1) * size, lane0 : lane0 + 128][None]
        picks.append(place(block, -(k * size - lane0), size))
    basis = merge_coeffs(jnp.concatenate(picks, axis=0))
    while basis.shape[0] > 1:
        n = basis.shape[0] // 2
        w = basis.shape[2]
        pairs = basis.reshape(n, 2, RANK, w)
        bt = jnp.concatenate(
            [place(pairs[:, 0], 0, 2 * w), place(pairs[:, 1], w, 2 * w)], axis=1
        )
        gs = jnp.concatenate(
            [g_ref[k * 2 * w : (k + 1) * 2 * w, k * 2 * w : (k + 1) * 2 * w][None] for k in range(n)],
            axis=0,
        )
        h = bdot_t(bdot(bt, gs), bt)
        basis = bdot(merge_coeffs(h), bt)
    return basis[0]


def finish_body(n_tm, g_ref, w_ref, out_ref, part_ref, buf, send, recv, own):
    s = lax.axis_index("space")
    t = lax.axis_index("tm")
    basis_t = tree_levels(g_ref)
    hi = basis_t.astype(jnp.bfloat16)
    rest = basis_t - hi.astype(jnp.float32)
    mid = rest.astype(jnp.bfloat16)
    lo = (rest - mid.astype(jnp.float32)).astype(jnp.bfloat16)
    pieces = jnp.concatenate([hi, mid, lo], axis=0)
    for x in range(w_ref.shape[0]):
        terms = jnp.dot(pieces, w_ref[x], preferred_element_type=jnp.float32)
        part_ref[:, x, :] = (terms[:RANK] + terms[RANK : 2 * RANK]) + terms[2 * RANK :]
    share = part_ref.shape[0] // n_tm
    width = w_ref.shape[2]
    src_at = lambda a: part_ref.at[pl.ds(a * share, share)]
    dst_at = lambda j: buf.at[:, :, lanes(j, width)]
    copies = []
    for k in range(1, n_tm):
        a = lax.rem(t + k, n_tm)
        c = pltpu.make_async_remote_copy(
            src_ref=src_at(a), dst_ref=dst_at(t), send_sem=send.at[k], recv_sem=recv.at[t],
            device_id=(s, a), device_id_type=MESH,
        )
        c.start()
        copies.append(c)
    mine = pltpu.make_async_copy(src_at(t), dst_at(t), own.at[0])
    mine.start()
    for k in range(1, n_tm):
        j = lax.rem(t + k, n_tm)
        pltpu.make_async_remote_copy(
            src_ref=src_at(j), dst_ref=dst_at(j), send_sem=send.at[k], recv_sem=recv.at[j],
            device_id=(s, j), device_id_type=MESH,
        ).wait_recv()
    mine.wait()
    for c in copies:
        c.wait_send()
    out_ref[...] = buf[...]


def local(velocity):
    rows = velocity.shape[2]
    span_v = velocity[:, 1].astype(jnp.float32)
    u = velocity[:, 0]
    cols = u.shape[2]
    wrapped = jnp.concatenate([u[:, :, cols - 2 :], u, u[:, :, :2]], axis=2)
    f32 = lambda lo: wrapped[:, :, lo : lo + cols].astype(jnp.float32)
    du_dz = (8.0 * (f32(3) - f32(1)) - (f32(4) - f32(0))) / 12.0
    dv_dx = (
        8.0 * (span_v[:, 3 : rows - 1] - span_v[:, 1 : rows - 3])
        - (span_v[:, 4:rows] - span_v[:, : rows - 4])
    ) / 12.0
    interior = (dv_dx - du_dz[:, 2 : rows - 2]).astype(jnp.bfloat16)
    v = velocity[:, 1]
    vloc = jnp.swapaxes(jnp.concatenate([v[:, :4], v[:, rows - 4 :]], axis=1), 0, 1)
    dudz = jnp.swapaxes(jnp.concatenate([du_dz[:, :2], du_dz[:, rows - 2 :]], axis=1), 0, 1)
    modes, fixed = front(jnp.swapaxes(interior, 0, 1), vloc, dudz)
    fixed = jnp.swapaxes(fixed, 0, 1)
    vorticity = jnp.concatenate([fixed[:, :2], interior, fixed[:, 2:]], axis=1)
    return (vorticity, modes)


def solution(mesh):
    in_specs = (P("tm", None, "space", None),)
    out_specs = (P("tm", "space", None), P("tm", "space", None))
    return jax.shard_map(local, mesh=mesh, in_specs=in_specs, out_specs=out_specs, check_vma=False)
```
